256 devices in a mesh: gx: 8 (over z), gy: 4 (over x), gz: 8 (over y, core).
Axes of the slice: x: 4, y: 4, z: 8, core: 2. Of those that a mesh axis runs over, the one named last changes fastest.
Arguments:
- positions: float32 [3, 32, 16, 2048], P(None, 'gx', 'gy', 'gz'), may hold values from -0.5 to 0.5
- charges: float32 [32, 16, 2048], P('gx', 'gy', 'gz'), may hold values from -0.06 to 0.06
- counts: int32 [32, 16, 32], P('gx', 'gy', 'gz'), may hold values from 1 to 64, 1280 in all within a row
- near_flags: int32 [26, 32, 16, 32], P(None, 'gx', 'gy', 'gz'), may hold values 0 or 1
- far_flags: int32 [343, 32, 16, 32], P(None, 'gx', 'gy', 'gz'), may hold values from 0 to 1, as said below
- up_operator: float32 [152, 152], replicated, may hold values from -0.00032461911 to 0.00045446676
- down_operator: float32 [152, 152], replicated, may hold values from -0.00032461911 to 0.00045446676
Outputs:
- potential: float32 [32, 16, 2048], P('gx', 'gy', 'gz')
The draws below stay inside these ranges and needn't reach their ends.
Inputs may be any that keep to these rules, and one draw needn't show every extreme that they name: far_flags[c, t] is 1 only where d_c is in the octree interaction list of leaf t: some component of d_c has magnitude 2 or more and, along every dimension with leaf index i, the component lies in -2 - (i mod 2) .. 3 - (i mod 2); some entries of that list are left out.
All inputs are finite; a program needn't handle non-finite values. No bound on the sum of `counts` or of `near_flags` on one device may be relied on, other than what follows from the above.
Results may differ from the reference program's by a relative error of at most 0.0003.
Values may be sent and summed in bfloat16 or wider, within the bound.
No kernel may reach another device: no remote copies, remote signals or barrier semaphores. Data moves between devices by JAX's collectives and lax.ppermute only.
A program may use at most 128 MiB of HBM per device.

```python
import math
import jax
import jax.numpy as jnp
import numpy as np
from jax import lax

ORDER = 6
SURF = 152
REACH = 3
CLASSES = 343
NEAR = 26
SLOTS = 64
BX = 4
BY = 4
BZ = 4
NXL = 32
NYL = 16
NZL = 32
N_GX = 8
N_GY = 4
N_GZ = 8


def draw_far_flags(key, part):
    class_side = 2 * REACH + 1
    number = jnp.arange(class_side ** 3, dtype=jnp.int32)
    along_x = (number // (class_side * class_side) - REACH)[:, None, None, None]
    along_y = (number // class_side % class_side - REACH)[:, None, None, None]
    along_z = (number % class_side - REACH)[:, None, None, None]
    parity_x = (jnp.arange(NXL, dtype=jnp.int32) % 2)[None, :, None, None]
    parity_y = (jnp.arange(NYL, dtype=jnp.int32) % 2)[None, None, :, None]
    parity_z = (jnp.arange(NZL, dtype=jnp.int32) % 2)[None, None, None, :]
    inside_x = (along_x >= -2 - parity_x) & (along_x <= 3 - parity_x)
    inside_y = (along_y >= -2 - parity_y) & (along_y <= 3 - parity_y)
    inside_z = (along_z >= -2 - parity_z) & (along_z <= 3 - parity_z)
    largest = jnp.maximum(jnp.maximum(jnp.abs(along_x), jnp.abs(along_y)), jnp.abs(along_z))
    listed = inside_x & inside_y & inside_z & (largest >= 2)
    keep_draw = jax.random.randint(jax.random.fold_in(key, 3), (class_side ** 3, NXL, NYL, NZL), 0, 4, dtype=jnp.int32)
    return jnp.where(listed & (keep_draw != 0), 1, 0).astype(jnp.int32)


def operator_law(key, fold_value):
    noise_draw = jax.random.normal(jax.random.fold_in(key, fold_value), (SURF, SURF), jnp.float32)
    noise_draw = jnp.clip(noise_draw, -6.0, 6.0)
    return ((1.5 + 1.5 * noise_draw) / (SURF * SURF)).astype(jnp.float32)


def draw_up_operator(key, part):
    return operator_law(key, 1)


def draw_down_operator(key, part):
    return operator_law(key, 2)


def plant(values, rng, least, high):
    spot = [jax.random.randint(jax.random.fold_in(rng, axis), (), 0, length) for axis, length in enumerate(values.shape)]
    longest = values.shape.index(max(values.shape))
    next_to = spot[:longest] + [(spot[longest] + 1) % values.shape[longest]] + spot[longest + 1:]
    return values.at[tuple(spot)].set(least).at[tuple(next_to)].set(high)


def block_scale(key, extent, split, least, high):
    level = 1.0
    for dim, parts in split:
        steps = jax.random.uniform(jax.random.fold_in(jax.random.fold_in(key, 6), dim), (parts,), jnp.float32, least / len(split), high / len(split))
        level = level * jnp.repeat(jnp.exp(steps), extent[dim] // parts).reshape((-1,) + (1,) * (len(extent) - 1 - dim))
    return level


def length_profile(count, total, most, skew):
    weights = [(1 << 20) // math.isqrt(rank ** skew) + 1 for rank in range(2, count + 1)]
    surplus, given = total - most - (count - 1), [1] * (count - 1)
    while surplus > 0:
        candidates = [i for i in range(count - 1) if given[i] < most]
        pool, remaining = sum([weights[i] for i in candidates]), surplus
        for i in candidates:
            more = min(most - given[i], max(1, remaining * weights[i] // pool), surplus)
            given[i] = given[i] + more
            surplus = surplus - more
    return np.array([most] + given)


def uneven_parts(key, count, total, most, lean):
    if count == 2:
        one = jax.random.randint(key, (), max(1, total - most), min(most, total - 1) + 1)
        return jnp.stack([one, total - one])
    sizes = jnp.asarray(length_profile(count, total, most, lean), jnp.int32)
    pairs = (count - 1) // 2
    source_of, sink = sizes[1:1 + 2 * pairs:2], sizes[2:2 + 2 * pairs:2]
    room = jnp.minimum(source_of - 1, most - sink)
    passed = jax.random.randint(jax.random.fold_in(key, 1), (pairs,), 0, 1 << 20) % (room + 1)
    sizes = sizes.at[1:1 + 2 * pairs:2].set(source_of - passed).at[2:2 + 2 * pairs:2].set(sink + passed)
    return sizes[jax.random.permutation(jax.random.fold_in(key, 2), count)]


def centred(stream_key, dims, scale, bound, split=(), kind=jnp.bfloat16):
    values = jax.random.normal(stream_key, dims, jnp.float32) * scale
    if len(split) > 0:
        values = block_scale(stream_key, dims, split, -0.22, 0.18) * values
    return jnp.clip(values, min=-bound, max=bound).astype(kind)


def setup_inputs(seed: int = 0) -> dict:
    keys = jax.random.split(jax.random.key(seed), 8)
    return {
        "positions": jnp.clip(jax.random.uniform(keys[0], (3, NXL, NYL, NZL * SLOTS), jnp.float32, -0.5, 0.5) * block_scale(keys[0], (3, NXL, NYL, NZL * SLOTS), ((1, 8), (2, 4), (3, 8)), -0.4, 0.0), -0.5, 0.5),
        "charges": centred(keys[1], (NXL, NYL, NZL * SLOTS), 0.01, 0.06, ((0, 8), (1, 4), (2, 8)), jnp.float32),
        "counts": jax.vmap(lambda own: uneven_parts(own, NZL, NZL * SLOTS * 5 // 8, SLOTS, 2))(jax.random.split(keys[2], NXL * NYL)).reshape((NXL, NYL, NZL)).astype(jnp.int32),
        "near_flags": plant((jax.random.randint(keys[3], (NEAR, NXL, NYL, NZL), 0, 4) < 3).astype(jnp.int32), jax.random.fold_in(keys[3], 1), 0, 1),
        "far_flags": draw_far_flags(jax.random.fold_in(keys[7], 71), 0),
        "up_operator": draw_up_operator(jax.random.fold_in(keys[7], 71), 0),
        "down_operator": draw_down_operator(jax.random.fold_in(keys[7], 71), 0),
    }


INNER = 1.05
OUTER = 2.95
SOFTEN = 0.01
HIGHEST = lax.Precision.HIGHEST

def unit_surface():
    spacing = np.linspace(-1.0, 1.0, ORDER)
    collected = []
    for along_x in range(ORDER):
        for along_y in range(ORDER):
            for along_z in range(ORDER):
                lowest = min(along_x, along_y, along_z)
                highest = max(along_x, along_y, along_z)
                if lowest == 0 or highest == ORDER - 1:
                    collected.append([spacing[along_x], spacing[along_y], spacing[along_z]])
    return np.array(collected, dtype=np.float32)

def near_offsets():
    table = []
    for along_x in (-1, 0, 1):
        for along_y in (-1, 0, 1):
            for along_z in (-1, 0, 1):
                if (along_x, along_y, along_z) != (0, 0, 0):
                    table.append((along_x, along_y, along_z))
    return table

def leaf_centres(block_x, block_y, block_z):
    centre_x = np.arange(block_x, dtype=np.float32) + np.float32(0.5 - block_x * 0.5)
    centre_y = np.arange(block_y, dtype=np.float32) + np.float32(0.5 - block_y * 0.5)
    centre_z = np.arange(block_z, dtype=np.float32) + np.float32(0.5 - block_z * 0.5)
    grids = np.meshgrid(centre_x, centre_y, centre_z, indexing='ij')
    return tuple((np.asarray(part, dtype=np.float32) for part in grids))

def kernel(along_x, along_y, along_z):
    return 1.0 / jnp.sqrt(along_x * along_x + along_y * along_y + along_z * along_z + SOFTEN)

def check_upward(points, weights, surface):
    radius = OUTER * 0.5
    kernel_terms = kernel(radius * surface[:, 0, None] - points[0][..., None, :], radius * surface[:, 1, None] - points[1][..., None, :], radius * surface[:, 2, None] - points[2][..., None, :])
    return lax.optimization_barrier(jnp.sum(kernel_terms * weights[..., None, :], axis=-1))

def evaluate_local(points, local, surface):
    radius = OUTER * 0.5
    kernel_terms = kernel(points[0][..., :, None] - radius * surface[:, 0], points[1][..., :, None] - radius * surface[:, 1], points[2][..., :, None] - radius * surface[:, 2])
    return lax.optimization_barrier(jnp.sum(kernel_terms * local[..., None, :], axis=-1))

def pair_sum(targets, sources, weights, displace, exclude):
    kernel_terms = kernel(targets[0][..., :, None] - (displace[0] + sources[0][..., None, :]), targets[1][..., :, None] - (displace[1] + sources[1][..., None, :]), targets[2][..., :, None] - (displace[2] + sources[2][..., None, :]))
    if exclude:
        slot_count = targets.shape[-1]
        kernel_terms = kernel_terms * (1.0 - jnp.eye(slot_count, dtype=jnp.float32))
    return lax.optimization_barrier(jnp.sum(kernel_terms * weights[..., None, :], axis=-1))

def block_upward_kernel(surface, centres, halves):
    components = []
    for axis_id in range(3):
        target = OUTER * halves[axis_id] * surface[:, axis_id]
        source = centres[axis_id][..., None] + INNER * 0.5 * surface[:, axis_id]
        components.append(target.reshape((-1,) + (1,) * source.ndim) - source[None])
    return kernel(components[0], components[1], components[2])

def block_downward_kernel(surface, centres, halves):
    components = []
    for axis_id in range(3):
        target = centres[axis_id][..., None] + INNER * 0.5 * surface[:, axis_id]
        source = OUTER * halves[axis_id] * surface[:, axis_id]
        components.append(target[..., None] - source)
    return kernel(components[0], components[1], components[2])

def block_pair_kernel(surface, halves, displace):
    components = []
    for axis_id in range(3):
        target = INNER * halves[axis_id] * surface[:, axis_id]
        source = displace[axis_id] + INNER * halves[axis_id] * surface[:, axis_id]
        components.append(target[:, None] - source[None, :])
    return kernel(components[0], components[1], components[2])

def reference(positions, charges, counts, near_flags, far_flags, up_operator, down_operator):
    surface = jnp.asarray(unit_surface())
    halves = (BX * 0.5, BY * 0.5, BZ * 0.5)
    breadth = (BX + BY + BZ) / 3.0
    block_count = N_GX * N_GY * N_GZ
    slot_pos = positions.reshape(3, NXL, NYL, NZL, SLOTS)
    occupied = (jnp.arange(SLOTS, dtype=jnp.int32)[None, None, None, :] < counts[..., None]).astype(jnp.float32)
    strengths = charges.reshape(NXL, NYL, NZL, SLOTS) * occupied
    slab_pos = jnp.moveaxis(slot_pos, 1, 0)

    def upward_slab(element):
        points, weights = element
        check_pot = check_upward(points, weights, surface)
        return jnp.einsum('yzs,es->yze', check_pot, up_operator, precision=HIGHEST)
    up_eq = lax.map(upward_slab, (slab_pos, strengths))
    centres = leaf_centres(BX, BY, BZ)
    up_terms = block_upward_kernel(surface, centres, halves)
    grouped = up_eq.reshape(N_GX, BX, N_GY, BY, N_GZ, BZ, SURF).transpose(0, 2, 4, 1, 3, 5, 6)
    grouped = grouped.reshape(block_count, BX, BY, BZ, SURF)
    block_check = jnp.einsum('sxyze,dxyze->ds', up_terms, grouped, precision=HIGHEST)
    block_eq = breadth * jnp.einsum('ds,es->de', block_check, up_operator, precision=HIGHEST)
    eq_grid = block_eq.reshape(N_GX, N_GY, N_GZ, SURF)

    def coarse_term(running, number):
        index_x = number // (N_GY * N_GZ)
        index_y = number // N_GZ % N_GY
        index_z = number % N_GZ
        delta_x = (index_x + N_GX // 2) % N_GX - N_GX // 2
        delta_y = (index_y + N_GY // 2) % N_GY - N_GY // 2
        delta_z = (index_z + N_GZ // 2) % N_GZ - N_GZ // 2
        largest = jnp.maximum(jnp.maximum(jnp.abs(delta_x), jnp.abs(delta_y)), jnp.abs(delta_z))
        weight = (largest >= 1).astype(jnp.float32)
        displace = (delta_x.astype(jnp.float32) * BX, delta_y.astype(jnp.float32) * BY, delta_z.astype(jnp.float32) * BZ)
        translation = block_pair_kernel(surface, halves, displace)
        shifted = jnp.roll(eq_grid, (-delta_x, -delta_y, -delta_z), (0, 1, 2))
        return (running + weight * jnp.einsum('abce,se->abcs', shifted, translation, precision=HIGHEST), None)
    block_down, _ = lax.scan(coarse_term, jnp.zeros((N_GX, N_GY, N_GZ, SURF), jnp.float32), jnp.arange(block_count, dtype=jnp.int32))
    block_down = block_down.reshape(block_count, SURF)
    block_local = breadth * jnp.einsum('ds,es->de', block_down, down_operator, precision=HIGHEST)
    down_terms = block_downward_kernel(surface, centres, halves)
    coarse_check = jnp.einsum('xyzse,de->dxyzs', down_terms, block_local, precision=HIGHEST)
    coarse_check = coarse_check.reshape(N_GX, N_GY, N_GZ, BX, BY, BZ, SURF).transpose(0, 3, 1, 4, 2, 5, 6)
    coarse_check = coarse_check.reshape(NXL, NYL, NZL, SURF)
    eq_low = up_eq.astype(jnp.bfloat16)
    class_side = 2 * REACH + 1

    def far_term(running, number):
        along_x = number // (class_side * class_side) - REACH
        along_y = number // class_side % class_side - REACH
        along_z = number % class_side - REACH
        displace = (along_x.astype(jnp.float32), along_y.astype(jnp.float32), along_z.astype(jnp.float32))
        translation = block_pair_kernel(surface, (0.5, 0.5, 0.5), displace).astype(jnp.bfloat16)
        shifted = jnp.roll(eq_low, (-along_x, -along_y, -along_z), (0, 1, 2))
        chosen = jnp.where(far_flags[number][..., None] == 1, shifted, jnp.zeros_like(shifted))
        added = jnp.einsum('xyze,se->xyzs', chosen.astype(jnp.float32), translation.astype(jnp.float32), precision=HIGHEST)
        return (running + added, None)
    leaf_check, _ = lax.scan(far_term, coarse_check, jnp.arange(CLASSES, dtype=jnp.int32))
    leaf_local = jnp.einsum('xyzs,es->xyze', leaf_check, down_operator, precision=HIGHEST)

    def local_slab(element):
        points, local = element
        return evaluate_local(points, local, surface)
    far_part = lax.map(local_slab, (slab_pos, leaf_local))
    neighbours = near_offsets()

    def near_slab(slab_index):
        targets = lax.dynamic_index_in_dim(slot_pos, slab_index, 1, keepdims=False)
        weights = lax.dynamic_index_in_dim(strengths, slab_index, 0, keepdims=False)
        near_mask = lax.dynamic_index_in_dim(near_flags, slab_index, 1, keepdims=False).astype(jnp.float32)
        running = pair_sum(targets, targets, weights, (0.0, 0.0, 0.0), True)
        for number, offset in enumerate(neighbours):
            source_x = (slab_index + offset[0]) % NXL
            source_pos = jnp.roll(lax.dynamic_index_in_dim(slot_pos, source_x, 1, keepdims=False), (-offset[1], -offset[2]), (1, 2))
            source_q = jnp.roll(lax.dynamic_index_in_dim(strengths, source_x, 0, keepdims=False), (-offset[1], -offset[2]), (0, 1))
            running = running + near_mask[number][..., None] * pair_sum(targets, source_pos, source_q, offset, False)
        return running
    near_part = lax.map(near_slab, jnp.arange(NXL, dtype=jnp.int32))
    potential = (far_part + near_part) * occupied
    return potential.reshape(NXL, NYL, NZL * SLOTS)
```

```python
import functools

import jax
import jax.numpy as jnp
import ml_dtypes
import numpy as np
from jax import lax
from jax.experimental import pallas as pl
from jax.experimental.pallas import tpu as pltpu
from jax.sharding import PartitionSpec as P

ORDER = 6
SURF = 152
SPAD = 160
WIDE = 256
LEAVES = 4
SLOTS = 64
CLASSES = 343
INNER = 1.05
OUTER = 2.95
SOFTEN = 0.01
HALF = 2.0
BREADTH = 4.0
HIGHEST = lax.Precision.HIGHEST
F32 = jnp.float32
BF16 = jnp.bfloat16
NT = (((1,), (1,)), ((), ()))
STEPS = (("gx", 4), ("gx", 2), ("gx", 1), ("gy", 2), ("gz", 4), ("gz", 2), ("gy", 1), ("gz", 1))


def surface_points():
    points = []
    for i in range(ORDER):
        for j in range(ORDER):
            for k in range(ORDER):
                if min(i, j, k) == 0 or max(i, j, k) == ORDER - 1:
                    points.append((i, j, k))
    return points


def tables():
    points = surface_points()
    spacing = np.linspace(-1.0, 1.0, ORDER)
    g = np.array([[spacing[i] for i in p] for p in points], dtype=np.float32)
    column = np.zeros((3, SPAD, WIDE), np.float32)
    column[:, :SURF, :] = g.T[:, :, None]
    row = np.zeros((8, WIDE), np.float32)
    row[:3, :SURF] = g.T
    where = {p: n for n, p in enumerate(points)}
    mirror = np.full((8, WIDE), -1, np.int32)
    for h in range(8):
        sign = (h >> 2 & 1, h >> 1 & 1, h & 1)
        for n, p in enumerate(points):
            mirror[h, n] = where[tuple(ORDER - 1 - c if f else c for c, f in zip(p, sign))]
    pick = np.zeros((64 * 8, 384), np.float32)
    for a in range(4):
        for b in range(4):
            for c in range(4):
                if max(a, b, c) < 2:
                    continue
                for h in range(8):
                    d = [-v if f else v for v, f in zip((a, b, c), (h >> 2 & 1, h >> 1 & 1, h & 1))]
                    number = (d[0] + 3) * 49 + (d[1] + 3) * 7 + d[2] + 3
                    pick[(a * 16 + b * 4 + c) * 8 + h, number] = 1.0
    return column, row, mirror, pick.astype(ml_dtypes.bfloat16)


def gathered_order():
    offsets = [(0, 0, 0)]
    for axis, distance in STEPS:
        n = ("gx", "gy", "gz").index(axis)
        offsets = offsets + [tuple(v + (distance if i == n else 0) for i, v in enumerate(o)) for o in offsets]
    table = np.zeros((256,), np.int32)
    for m, (x, y, z) in enumerate(offsets):
        table[(x * 4 + y) * 8 + z] = m
    return table


def iota(shape, dim):
    return lax.broadcasted_iota(jnp.int32, shape, dim)


def split2(v):
    hi = v.astype(BF16)
    return hi, (v - hi.astype(F32)).astype(BF16)


def inverse_distance(x, y, z):
    return lax.rsqrt(x * x + y * y + z * z + SOFTEN)


def occupied_row(counts, x, y):
    lane = iota((1, WIDE), 1)
    zone = lane >> 6
    n = jnp.where(
        zone < 2,
        jnp.where(zone == 0, counts[x, y, 0], counts[x, y, 1]),
        jnp.where(zone == 2, counts[x, y, 2], counts[x, y, 3]),
    )
    return ((lane & 63) < n).astype(F32)


def padded_operator(ref, out):
    out[...] = jnp.zeros_like(out)
    out[0:SURF, 0:SURF] = ref[...]


def leaf_squares(column, row, squares):
    for axis in range(3):
        outer = (OUTER * HALF) * column[axis]
        inner = (INNER * 0.5) * row[axis : axis + 1, :]
        for t in range(LEAVES):
            d = outer - ((t - 1.5) + inner)
            squares[axis * LEAVES + t] = d * d + (SOFTEN if axis == 2 else 0.0)


def upward_kernel(
    pos, chg, counts, up, column, row,
    eq_out, own_out, down_out, above_out, block_out,
    terms, operator, squares, acc,
):
    padded_operator(up, operator)
    leaf_squares(column, row, squares)

    for x in range(4):
        for y in range(4):
            r = x * 4 + y
            q = chg[x, y : y + 1, :] * occupied_row(counts, x, y)
            px, py, pz = (pos[c, x, y : y + 1, :] for c in range(3))
            k = (
                inverse_distance(
                    (OUTER * 0.5) * column[0] - px,
                    (OUTER * 0.5) * column[1] - py,
                    (OUTER * 0.5) * column[2] - pz,
                )
                * q
            )
            hi, lo = split2(k)
            terms[0:SPAD, r * WIDE : (r + 1) * WIDE] = hi
            terms[SPAD : 2 * SPAD, r * WIDE : (r + 1) * WIDE] = lo
            own_out[r, 0:1, :] = px
            own_out[r, 1:2, :] = py
            own_out[r, 2:3, :] = pz
            own_out[r, 3:4, :] = q
            for out, at in ((down_out, 0), (above_out, 128)):
                out[r, 2:3, 0:128] = px[:, at : at + 128]
                out[r, 2:3, 128:256] = py[:, at : at + 128]
                out[r, 3:4, 0:128] = pz[:, at : at + 128]
                out[r, 3:4, 128:256] = q[:, at : at + 128]
    gather = ((iota((16 * WIDE, 128), 0) >> 6) == iota((16 * WIDE, 128), 1)).astype(F32).astype(BF16)
    both = jnp.dot(terms[...], gather, preferred_element_type=F32)
    check = both[0:SPAD] + both[SPAD : 2 * SPAD]
    check = jnp.concatenate([check, jnp.zeros((WIDE - SPAD, 128), F32)], axis=0).T[0:64, :]
    up_eq = lax.dot_general(check, operator[...], NT, precision=HIGHEST, preferred_element_type=F32)
    low = up_eq.astype(BF16).astype(F32)
    for r in range(16):
        eq_out[r] = low[r * 4 : r * 4 + 4]
        down_out[r, 0:2, :] = low[r * 4 : r * 4 + 2]
        above_out[r, 0:2, :] = low[r * 4 + 2 : r * 4 + 4]
    acc[...] = jnp.zeros_like(acc)
    for part in range(4):
        rows = slice(part * 40, part * 40 + 40)
        total = jnp.zeros((40, WIDE), F32)
        for x in range(4):
            for y in range(4):
                xy = squares[x, rows, :] + squares[4 + y, rows, :]
                for z in range(4):
                    t = x * 16 + y * 4 + z
                    total = total + lax.rsqrt(xy + squares[8 + z, rows, :]) * up_eq[t : t + 1, :]
        acc[rows, :] = total
    ones = jnp.ones((8, WIDE), F32)
    summed = lax.dot_general(ones, acc[...], NT, precision=HIGHEST, preferred_element_type=F32)
    block = lax.dot_general(summed, operator[...], NT, precision=HIGHEST, preferred_element_type=F32)
    block_out[...] = (BREADTH * block)[0:1, :]


def merge_kernel(eq, own, right, left, eq_out, own_out, down_out, above_out):
    for r in range(16):
        x, y = r // 4, r % 4
        eq_out[r, 0:2, :] = left[r, 0:2, :]
        eq_out[r, 2:6, :] = eq[r]
        eq_out[r, 6:8, :] = right[r, 0:2, :]
        own_out[r, 0:4, :] = own[r]
        first = iota((1, 128), 1) < 64
        for c in range(4):
            at = slice((c % 2) * 128, (c % 2) * 128 + 128)
            line = 2 + c // 2
            own_out[r, 4 + c : 5 + c, 0:128] = jnp.where(first, right[r, line : line + 1, at], left[r, line : line + 1, at])
            own_out[r, 4 + c : 5 + c, 128:256] = jnp.zeros((1, 128), F32)
    for x in range(4):
        for n in range(2):
            down_out[x * 3 + n] = eq_out[x * 4 + n]
            above_out[x * 3 + n] = eq_out[x * 4 + 2 + n]
        down_out[x * 3 + 2] = own_out[x * 4]
        above_out[x * 3 + 2] = own_out[x * 4 + 3]


def eq_tile(refs, x, y):
    eq, _, ylo, yhi, xlo, xhi = refs
    if x < 2:
        return xlo[x * 8 + y]
    if x > 5:
        return xhi[(x - 6) * 8 + y]
    if y < 2:
        return ylo[(x - 2) * 3 + y]
    if y > 5:
        return yhi[(x - 2) * 3 + y - 6]
    return eq[(x - 2) * 4 + y - 2]


def own_tile(refs, x, y):
    _, own, ylo, yhi, xlo, xhi = refs
    if x < 0:
        return xlo[16 + y + 1]
    if x > 3:
        return xhi[16 + y + 1]
    if y < 0:
        return ylo[x * 3 + 2]
    if y > 3:
        return yhi[x * 3 + 2]
    return own[x * 4 + y]


def edge_kernel(eq, own, ylo, yhi, down_out, above_out):
    refs = (eq, own, ylo, yhi, None, None)
    for n in range(2):
        for y in range(8):
            down_out[n * 8 + y] = eq_tile(refs, 2 + n, y)
            above_out[n * 8 + y] = eq_tile(refs, 4 + n, y)
    for y in range(-1, 5):
        down_out[16 + y + 1] = own_tile(refs, 0, y)
        above_out[16 + y + 1] = own_tile(refs, 3, y)


def far_groups():
    groups = {}
    for a in range(4):
        for b in range(4):
            for c in range(4):
                if max(a, b, c) >= 2:
                    key = tuple(v in (1, 2) for v in (a, b, c))
                    groups.setdefault(key, []).append((a, b, c))
    return groups


def far_kernel(
    eq, own, ylo, yhi, xlo, xhi, flags, pick, mirror, column, row,
    out, low, turned, framed, chosen, squares, stacked, matrices, total,
):
    refs = (eq, own, ylo, yhi, xlo, xhi)
    for x in range(8):
        for y in range(0, 8, 2):
            pair = jnp.concatenate([eq_tile(refs, x, y), eq_tile(refs, x, y + 1)], axis=0)
            low[(x * 8 + y) * 8 : (x * 8 + y) * 8 + 16, :] = pair.astype(BF16)
    turn = ((iota((WIDE, WIDE), 0) ^ 7) == iota((WIDE, WIDE), 1)).astype(F32).astype(BF16)
    for n in range(2):
        part = slice(n * WIDE, n * WIDE + WIDE)
        turned[part, :] = jnp.dot(turn, low[part, :], preferred_element_type=F32).astype(BF16)

    def permutation(h):
        return (iota((WIDE, WIDE), 0) == mirror[h : h + 1, :]).astype(F32).astype(BF16)

    for h in range(8):
        source = turned if h & 1 else low
        frame = jnp.dot(source[...], permutation(h), preferred_element_type=F32)
        for x in range(8):
            for y in range(8):
                xf, yf = (7 - x if h & 4 else x), (7 - y if h & 2 else y)
                at = (x * 8 + y) * 8
                for n in range(2):
                    framed.at[n][pl.ds((xf * 8 + yf) * 64 + h, 8, stride=8), :] = frame[
                        at : at + 8, n * 128 : n * 128 + 128
                    ]
    picked = jnp.dot(pick[...], flags[...], preferred_element_type=F32)
    which = iota((512, 128), 0) & 7
    for h in range(8):
        mask = (48 if h & 4 else 0) + (12 if h & 2 else 0) + (3 if h & 1 else 0)
        turn = ((iota((128, 128), 0) ^ mask) == iota((128, 128), 1)).astype(F32).astype(BF16)
        part = jnp.dot(jnp.where(which == h, picked, 0.0).astype(BF16), turn, preferred_element_type=F32)
        chosen[...] = part if h == 0 else chosen[...] + part
    for axis in range(3):
        for d in range(4):
            v = (INNER * 0.5) * row[axis : axis + 1, :] - d - (INNER * 0.5) * column[axis]
            squares[axis * 4 + d] = v * v + (SOFTEN if axis == 2 else 0.0)
    matrices[...] = jnp.zeros_like(matrices)
    total[...] = jnp.zeros_like(total)
    for key, members in far_groups().items():
        ranges = [range(4) if every else (0, 2) for every in key]
        leaves = [(x, y, z) for x in ranges[0] for y in ranges[1] for z in ranges[2]]
        for n, (a, b, c) in enumerate(members):
            m = lax.rsqrt(squares[a] + squares[4 + b] + squares[8 + c])
            matrices[n * WIDE : n * WIDE + SPAD, :] = m.astype(BF16)
            flag = chosen[(a * 16 + b * 4 + c) * 8 : (a * 16 + b * 4 + c) * 8 + 8, :]
            for i in range(0, len(leaves), 2):
                tiles = []
                for x, y, z in leaves[i : i + 2]:
                    at = (((x + 2 + a) * 8 + y + 2 + b) * 8 + z + 2 + c) * 8
                    leaf = x * 16 + y * 4 + z
                    keep = jnp.broadcast_to(flag[:, leaf : leaf + 1], (8, 128))
                    tiles.append([framed[half, at : at + 8, :] * keep for half in range(2)])
                for half in range(2):
                    lanes = slice(n * WIDE + half * 128, n * WIDE + half * 128 + 128)
                    stacked[i * 8 : i * 8 + 16, lanes] = jnp.concatenate([t[half] for t in tiles], axis=0).astype(BF16)
        rows, depth = len(leaves) * 8, len(members) * WIDE
        product = jnp.dot(stacked[0:rows, 0:depth], matrices[0:depth, :], preferred_element_type=F32)
        for i, (x, y, z) in enumerate(leaves):
            leaf = x * 16 + y * 4 + z
            for half in range(2):
                total[half, leaf * 8 : leaf * 8 + 8, :] += product[i * 8 : i * 8 + 8, half * 128 : half * 128 + 128]
    result = jnp.zeros((64, WIDE), F32)
    for h in range(8):
        parts = [total.at[half][pl.ds(h, 64, stride=8), :] for half in range(2)]
        hi, lo = split2(jnp.concatenate(parts, axis=1))
        both = jnp.dot(jnp.concatenate([hi, lo], axis=0), permutation(h), preferred_element_type=F32).astype(BF16)
        mask = (48 if h & 4 else 0) + (12 if h & 2 else 0) + (3 if h & 1 else 0)
        turn = ((iota((64, 128), 0) ^ mask) == (iota((64, 128), 1) & 63)).astype(F32).astype(BF16)
        result = result + jnp.dot(turn, both, preferred_element_type=F32)
    out[...] = result


def near_kernel(own, ylo, yhi, xlo, xhi, flags, out, sources, points, listed, sums):
    refs = (None, own, ylo, yhi, xlo, xhi)
    for x in range(6):
        for y in range(6):
            tile = own_tile(refs, x - 1, y - 1)
            line = jnp.concatenate([tile[0:4, :], tile[4:8, 0:128]], axis=1)
            line = jnp.concatenate([line, line], axis=0)
            third = (iota((8, WIDE), 0) & 3) == 2
            for e, shift in ((0, 64), (1, 0), (2, 320)):
                moved = pltpu.roll(line, shift, 1) if shift else line
                sources[(x * 6 + y) * 3 + e] = moved[:, 0:256] + jnp.where(third, float(e - 1), 0.0)
    same = (iota((64, WIDE), 1) & 63) == iota((64, WIDE), 0)
    block = ((iota((WIDE, WIDE), 0) >> 6) == (iota((WIDE, WIDE), 1) >> 6)).astype(F32).astype(BF16)
    zone = iota((32, WIDE), 1) >> 6

    def one_row(r, carry):
        x, y = r >> 2, r & 3
        pieces = []
        for c in range(3):
            v = own[r, c : c + 1, :]
            for _ in range(3):
                b = v.astype(BF16).astype(F32)
                pieces.append(jnp.where(same, b, 0.0).astype(BF16))
                v = v - b
        spread = jnp.dot(jnp.concatenate(pieces, axis=0), block, preferred_element_type=F32)
        for c in range(3):
            at = c * 192
            points[c] = spread[at : at + 64] + spread[at + 64 : at + 128] + spread[at + 128 : at + 192]
        f = flags[x, y]
        lists = jnp.zeros((32, WIDE), F32)
        for z in range(4):
            lists = jnp.where(zone == z, f[:, z : z + 1], lists)
        listed[...] = lists

        def one_part(p, carry):
            at = pl.multiple_of(p * 16, 16)
            tx, ty, tz = (points[c, pl.ds(at, 16), :] for c in range(3))
            acc = jnp.zeros((16, WIDE), F32)
            n = 0
            for ex in range(3):
                for ey in range(3):
                    for ez in range(3):
                        s = ((x + ex) * 6 + y + ey) * 3 + ez
                        line = sources[s]
                        sx = line[0:1] + float(ex - 1)
                        sy = line[1:2] + float(ey - 1)
                        k = inverse_distance(tx - sx, ty - sy, tz - line[2:3])
                        if (ex, ey, ez) == (1, 1, 1):
                            me = (iota((16, WIDE), 1) & 63) == iota((16, WIDE), 0) + at
                            acc = acc + jnp.where(me, 0.0, k) * line[3:4]
                        else:
                            acc = acc + k * (line[3:4] * listed[n : n + 1, :])
                            n += 1
            sums[pl.ds(at, 16), :] = acc
            return carry

        lax.fori_loop(0, 4, one_part, 0)
        hi, lo = split2(sums[...])
        both = jnp.dot(jnp.concatenate([hi, lo], axis=0), block, preferred_element_type=F32)
        picked = jnp.where(same, both[0:64] + both[64:128], 0.0)
        out[pl.ds(r, 1), :] = jnp.sum(picked, axis=0, keepdims=True)
        return carry

    lax.fori_loop(0, 16, one_row, 0)


def last_kernel(
    order, counts, gathered, far, near, pos, down, column, row,
    out, operator, squares, offsets, acc, checks,
):
    padded_operator(down, operator)
    at = 0
    for axis, n in enumerate((8, 4, 8)):
        base = (INNER * HALF) * column[axis] - (INNER * HALF) * row[axis : axis + 1, :]
        for i in range(n):
            delta = (i + n // 2) % n - n // 2
            v = base - float(delta * 4)
            offsets[at + i] = v * v + (SOFTEN if axis == 2 else 0.0)
        at += n
    acc[...] = jnp.zeros_like(acc)

    def pair(i, carry):
        x, y = i >> 2, i & 3
        lines = []
        for z in range(8):
            m = order[i * 8 + z]
            lines.append(gathered[pl.ds(m, 1), :] * jnp.where(m == 0, 0.0, 1.0))
        for part in range(4):
            rows = slice(part * 40, part * 40 + 40)
            xy = offsets[x, rows, :] + offsets[8 + y, rows, :]
            total = acc[rows, :]
            for z in range(8):
                total = total + lax.rsqrt(xy + offsets[12 + z, rows, :]) * lines[z]
            acc[rows, :] = total
        return carry

    lax.fori_loop(0, 32, pair, 0)
    ones = jnp.ones((WIDE, WIDE), F32)
    summed = jnp.dot(acc[...], ones, precision=HIGHEST, preferred_element_type=F32)
    local = BREADTH * jnp.dot(operator[...], summed, precision=HIGHEST, preferred_element_type=F32)
    leaf_squares(column, row, squares)
    checks[...] = jnp.zeros_like(checks)
    for x in range(4):
        for y in range(4):
            lines = [jnp.zeros((8, WIDE), F32)] * 4
            for part in range(4):
                rows = slice(part * 40, part * 40 + 40)
                xy = squares[x, rows, :] + squares[4 + y, rows, :]
                weight = local[rows]
                for z in range(4):
                    v = lax.rsqrt(xy + squares[8 + z, rows, :]) * weight
                    for s in range(5):
                        lines[z] = lines[z] + v[s * 8 : s * 8 + 8]
            for z in range(4):
                t = x * 16 + y * 4 + z
                checks[t : t + 1, :] = jnp.sum(lines[z], axis=0, keepdims=True)
    checks[0:64, :] += far[...]
    local = jnp.dot(operator[...], checks[...].T, precision=HIGHEST, preferred_element_type=F32)
    hi, lo = split2(local[0:SPAD])
    both = jnp.concatenate([hi, lo], axis=0)
    for x in range(4):
        for y in range(4):
            r = x * 4 + y
            spread = (iota((128, WIDE), 0) == r * 4 + (iota((128, WIDE), 1) >> 6)).astype(F32).astype(BF16)
            wide = jnp.dot(both, spread, preferred_element_type=F32)
            px, py, pz = (pos[c, x, y : y + 1, :] for c in range(3))
            k = inverse_distance(
                (OUTER * 0.5) * column[0] - px,
                (OUTER * 0.5) * column[1] - py,
                (OUTER * 0.5) * column[2] - pz,
            )
            line = jnp.sum(k * (wide[0:SPAD] + wide[SPAD : 2 * SPAD]), axis=0, keepdims=True)
            out[x, y : y + 1, :] = occupied_row(counts, x, y) * (line + near[r : r + 1, :])


def call(body, outs, scratch, memory, name, *args):
    spaces = {"v": pltpu.VMEM, "s": pltpu.SMEM}
    return pl.pallas_call(
        body,
        out_shape=[jax.ShapeDtypeStruct(s, F32) for s in outs],
        in_specs=[pl.BlockSpec(memory_space=spaces[m]) for m in memory],
        out_specs=[pl.BlockSpec(memory_space=pltpu.VMEM) for _ in outs],
        scratch_shapes=[pltpu.VMEM(s, d) for s, d in scratch],
        compiler_params=pltpu.CompilerParams(vmem_limit_bytes=58 << 20),
        name=name,
    )(*args)


def exchanged(axis, down, above):
    n = lax.axis_size(axis)
    from_above = lax.ppermute(down, axis, [((i + 1) % n, i) for i in range(n)])
    from_below = lax.ppermute(above, axis, [(i, (i + 1) % n) for i in range(n)])
    return from_above, from_below


def body(positions, charges, counts, near_flags, far_flags, up_operator, down_operator):
    column, row, mirror, pick = (jnp.asarray(t) for t in tables())
    order = jnp.asarray(gathered_order())
    eq, own, down, above, block = call(
        upward_kernel,
        [(16, 4, WIDE), (16, 4, WIDE), (16, 4, WIDE), (16, 4, WIDE), (1, WIDE)],
        [((2 * SPAD, 16 * WIDE), BF16), ((WIDE, WIDE), F32), ((12, SPAD, WIDE), F32), ((WIDE, WIDE), F32)],
        "vvsvvv", "upward", positions, charges, counts, up_operator, column, row,
    )
    right, left = exchanged("gz", down, above)
    eq, own, down, above = call(
        merge_kernel, [(16, 8, WIDE), (16, 8, WIDE), (12, 8, WIDE), (12, 8, WIDE)], [], "vvvv", "merge", eq, own, right, left
    )
    yhi, ylo = exchanged("gy", down, above)
    down, above = call(edge_kernel, [(22, 8, WIDE), (22, 8, WIDE)], [], "vvvv", "edge", eq, own, ylo, yhi)
    xhi, xlo = exchanged("gx", down, above)
    gathered = block
    for axis, distance in STEPS:
        n = lax.axis_size(axis)
        other = lax.ppermute(gathered, axis, [((i + distance) % n, i) for i in range(n)])
        gathered = jnp.concatenate([gathered, other], axis=0)
    flags = jnp.pad(far_flags.reshape(CLASSES, 64).astype(BF16), ((0, 384 - CLASSES), (0, 64)))
    (far,) = call(
        far_kernel,
        [(64, WIDE)],
        [
            ((512, WIDE), BF16), ((512, WIDE), BF16), ((2, 4096, 128), F32), ((512, 128), F32),
            ((12, SPAD, WIDE), F32), ((512, 8 * WIDE), BF16), ((8 * WIDE, WIDE), BF16), ((2, 512, 128), F32),
        ],
        "vvvvvvvvvvv", "far", eq, own, ylo, yhi, xlo, xhi, flags, pick, mirror, column, row,
    )
    listed = jnp.pad(near_flags.transpose(1, 2, 0, 3).astype(F32), ((0, 0), (0, 0), (0, 6), (0, 0)))
    (near,) = call(
        near_kernel,
        [(16, WIDE)],
        [((108, 8, WIDE), F32), ((3, 64, WIDE), F32), ((32, WIDE), F32), ((64, WIDE), F32)],
        "vvvvvv", "near", own, ylo, yhi, xlo, xhi, listed,
    )
    (potential,) = call(
        last_kernel,
        [(4, 4, WIDE)],
        [((WIDE, WIDE), F32), ((12, SPAD, WIDE), F32), ((20, SPAD, WIDE), F32), ((WIDE, WIDE), F32), ((128, WIDE), F32)],
        "ssvvvvvvv", "last", order, counts, gathered, far, near, positions, down_operator, column, row,
    )
    return potential


def solution(mesh):
    return jax.shard_map(
        body,
        mesh=mesh,
        in_specs=(
            P(None, "gx", "gy", "gz"),
            P("gx", "gy", "gz"),
            P("gx", "gy", "gz"),
            P(None, "gx", "gy", "gz"),
            P(None, "gx", "gy", "gz"),
            P(),
            P(),
        ),
        out_specs=P("gx", "gy", "gz"),
        check_vma=False,
    )
```

```python
import functools

import jax
import jax.numpy as jnp
import ml_dtypes
import numpy as np
from jax import lax
from jax.experimental import pallas as pl
from jax.experimental.pallas import tpu as pltpu
from jax.sharding import PartitionSpec as P

ORDER = 6
SURF = 152
SPAD = 160
WIDE = 256
LEAVES = 4
SLOTS = 64
CLASSES = 343
INNER = 1.05
OUTER = 2.95
SOFTEN = 0.01
HALF = 2.0
BREADTH = 4.0
HIGHEST = lax.Precision.HIGHEST
F32 = jnp.float32
BF16 = jnp.bfloat16
NT = (((1,), (1,)), ((), ()))
RING8 = (-1, 0, 1, 2, 3, -4, -3, -2)
RING4 = (-1, 0, 1, -2)
SELF = (1 * 4 + 1) * 8 + 1


def surface_points():
    points = []
    for i in range(ORDER):
        for j in range(ORDER):
            for k in range(ORDER):
                if min(i, j, k) == 0 or max(i, j, k) == ORDER - 1:
                    points.append((i, j, k))
    return points


def tables():
    points = surface_points()
    spacing = np.linspace(-1.0, 1.0, ORDER)
    g = np.array([[spacing[i] for i in p] for p in points], dtype=np.float32)
    column = np.zeros((3, SPAD, WIDE), np.float32)
    column[:, :SURF, :] = g.T[:, :, None]
    row = np.zeros((8, WIDE), np.float32)
    row[:3, :SURF] = g.T
    tail = np.tile(row[:, 128:160], (1, 4))
    where = {p: n for n, p in enumerate(points)}
    mirror = np.full((8, WIDE), -1, np.int32)
    for h in range(8):
        sign = (h >> 2 & 1, h >> 1 & 1, h & 1)
        for n, p in enumerate(points):
            mirror[h, n] = where[tuple(ORDER - 1 - c if f else c for c, f in zip(p, sign))]
    pick = np.zeros((64 * 8, 384), np.float32)
    for a in range(4):
        for b in range(4):
            for c in range(4):
                if max(a, b, c) < 2:
                    continue
                for h in range(8):
                    d = [-v if f else v for v, f in zip((a, b, c), (h >> 2 & 1, h >> 1 & 1, h & 1))]
                    number = (d[0] + 3) * 49 + (d[1] + 3) * 7 + d[2] + 3
                    pick[(a * 16 + b * 4 + c) * 8 + h, number] = 1.0
    return column, row, tail, mirror, pick.astype(ml_dtypes.bfloat16)


def iota(shape, dim):
    return lax.broadcasted_iota(jnp.int32, shape, dim)


def split2(v):
    hi = v.astype(BF16)
    return hi, (v - hi.astype(F32)).astype(BF16)


def inverse_distance(x, y, z):
    return lax.rsqrt(x * x + y * y + z * z + SOFTEN)


def occupied_row(counts, x, y):
    lane = iota((1, WIDE), 1)
    zone = lane >> 6
    n = jnp.where(
        zone < 2,
        jnp.where(zone == 0, counts[x, y, 0], counts[x, y, 1]),
        jnp.where(zone == 2, counts[x, y, 2], counts[x, y, 3]),
    )
    return ((lane & 63) < n).astype(F32)


def padded_operator(ref, out):
    out[...] = jnp.zeros_like(out)
    out[0:SURF, 0:SURF] = ref[...]


def leaf_squares(column, row, tail, squares):
    segment = (iota((1, 128), 1) >> 5).astype(F32)
    for axis in range(3):
        outer = (OUTER * HALF) * column[axis, :, 0:128]
        inner = (INNER * 0.5) * row[axis : axis + 1, 0:128]
        last = (INNER * 0.5) * tail[axis : axis + 1, :]
        soft = SOFTEN if axis == 2 else 0.0
        for t in range(LEAVES):
            d = outer - ((t - 1.5) + inner)
            squares[axis * LEAVES + t, :, 0:128] = d * d + soft
            if axis < 2:
                d = outer - ((t - 1.5) + last)
                squares[axis * LEAVES + t, :, 128:256] = d * d
            elif t == 0:
                d = outer - ((segment - 1.5) + last)
                squares[axis * LEAVES, :, 128:256] = d * d + soft


def upward_kernel(
    pos, chg, counts, up, column, row, tail,
    below, above,
    terms, operator, squares, acc, leaves,
):
    padded_operator(up, operator)
    leaf_squares(column, row, tail, squares)
    for x in range(4):
        for y in range(4):
            r = x * 4 + y
            q = chg[x, y : y + 1, :] * occupied_row(counts, x, y)
            px, py, pz = (pos[c, x, y : y + 1, :] for c in range(3))
            k = (
                inverse_distance(
                    (OUTER * 0.5) * column[0] - px,
                    (OUTER * 0.5) * column[1] - py,
                    (OUTER * 0.5) * column[2] - pz,
                )
                * q
            )
            hi, lo = split2(k)
            terms[0:SPAD, r * WIDE : (r + 1) * WIDE] = hi
            terms[SPAD : 2 * SPAD, r * WIDE : (r + 1) * WIDE] = lo
            for c, v in enumerate((px, py, pz, q)):
                below[16 + r, c : c + 1, :] = v[:, 0:128]
                above[16 + r, c : c + 1, :] = v[:, 128:256]
    gather = ((iota((16 * WIDE, 128), 0) >> 6) == iota((16 * WIDE, 128), 1)).astype(F32).astype(BF16)
    both = jnp.dot(terms[...], gather, preferred_element_type=F32)
    check = both[0:SPAD] + both[SPAD : 2 * SPAD]
    check = jnp.concatenate([check, jnp.zeros((WIDE - SPAD, 128), F32)], axis=0).T[0:64, :]
    up_eq = lax.dot_general(check, operator[...], NT, precision=HIGHEST, preferred_element_type=F32)
    low = up_eq.astype(BF16).astype(F32)
    for r in range(16):
        for out, at in ((below, 0), (above, 2)):
            pair = low[r * 4 + at : r * 4 + at + 2]
            out[r, 0:2, :] = pair[:, 0:128]
            out[r, 2:4, :] = pair[:, 128:256]
    leaves[0] = up_eq[:, 128:256]
    lines = leaves.at[0][pl.ds(0, 16, stride=4), :]
    for z in range(1, 4):
        lines = lines + pltpu.roll(leaves.at[0][pl.ds(z, 16, stride=4), :], 32 * z, 1)
    acc[...] = jnp.zeros_like(acc)
    for part in range(4):
        rows = slice(part * 40, part * 40 + 40)
        first, last = jnp.zeros((40, 128), F32), jnp.zeros((40, 128), F32)
        for x in range(4):
            for y in range(4):
                xy = squares[x, rows, 0:128] + squares[4 + y, rows, 0:128]
                for z in range(4):
                    t = x * 16 + y * 4 + z
                    first = first + lax.rsqrt(xy + squares[8 + z, rows, 0:128]) * up_eq[t : t + 1, 0:128]
                xy = squares[x, rows, 128:256] + squares[4 + y, rows, 128:256]
                r = x * 4 + y
                last = last + lax.rsqrt(xy + squares[8, rows, 128:256]) * lines[r : r + 1, :]
        acc[rows, 0:128] = first
        acc[rows, 128:256] = last
    ones = jnp.ones((8, WIDE), F32)
    summed = lax.dot_general(ones, acc[...], NT, precision=HIGHEST, preferred_element_type=F32)
    block = BREADTH * lax.dot_general(summed, operator[...], NT, precision=HIGHEST, preferred_element_type=F32)
    for out in (below, above):
        out[32, 0:1, :] = block[0:1, 0:128]
        out[32, 1:2, :] = block[0:1, 128:256]
        out[32, 2:4, :] = jnp.zeros((2, 128), F32)


def eq_record(refs, x, y, s):
    own, ylo, yhi, xlo, xhi = refs
    if x < 2:
        return xlo[(s * 2 + x) * 8 + y]
    if x > 5:
        return xhi[(s * 2 + x - 6) * 8 + y]
    if y < 2:
        return ylo[s * 8 + (x - 2) * 2 + y]
    if y > 5:
        return yhi[s * 8 + (x - 2) * 2 + y - 6]
    return own[s][(x - 2) * 4 + y - 2]


def particle_record(refs, x, y, s):
    own, ylo, yhi, xlo, xhi = refs
    if x < 0:
        return xlo[64 + s * 6 + y + 1]
    if x > 3:
        return xhi[64 + s * 6 + y + 1]
    if y < 0:
        return ylo[32 + s * 4 + x]
    if y > 3:
        return yhi[32 + s * 4 + x]
    return own[s][16 + x * 4 + y]


def far_groups():
    groups = {}
    for a in range(4):
        for b in range(4):
            for c in range(4):
                if max(a, b, c) >= 2:
                    key = tuple(v in (1, 2) for v in (a, b, c))
                    groups.setdefault(key, []).append((a, b, c))
    return groups


def far_kernel(
    z0, z1, z2, z3, ylo, yhi, xlo, xhi, flags, pick, mirror, column, row,
    out, halo, low, turned, framed, chosen, squares, stacked, matrices, total,
):
    refs = ((z0, z1, z2, z3), ylo, yhi, xlo, xhi)
    for x in range(8):
        for y in range(8):
            for pair in range(4):
                record = eq_record(refs, x, y, pair)
                at = (x * 8 + y) * 8 + pair * 2
                halo[0, at : at + 2, :] = record[0:2]
                halo[1, at : at + 2, :] = record[2:4]
    for half in range(2):
        low[:, half * 128 : half * 128 + 128] = halo[half].astype(BF16)
    turn = ((iota((WIDE, WIDE), 0) ^ 7) == iota((WIDE, WIDE), 1)).astype(F32).astype(BF16)
    for n in range(2):
        part = slice(n * WIDE, n * WIDE + WIDE)
        turned[part, :] = jnp.dot(turn, low[part, :], preferred_element_type=F32).astype(BF16)

    def permutation(h):
        return (iota((WIDE, WIDE), 0) == mirror[h : h + 1, :]).astype(F32).astype(BF16)

    for h in range(8):
        source = turned if h & 1 else low
        frame = jnp.dot(source[...], permutation(h), preferred_element_type=F32)
        for x in range(8):
            for y in range(8):
                xf, yf = (7 - x if h & 4 else x), (7 - y if h & 2 else y)
                at = (x * 8 + y) * 8
                for n in range(2):
                    framed.at[n][pl.ds((xf * 8 + yf) * 64 + h, 8, stride=8), :] = frame[
                        at : at + 8, n * 128 : n * 128 + 128
                    ]
    picked = jnp.dot(pick[...], flags[...], preferred_element_type=F32)
    which = iota((512, 128), 0) & 7
    for h in range(8):
        mask = (48 if h & 4 else 0) + (12 if h & 2 else 0) + (3 if h & 1 else 0)
        turn = ((iota((128, 128), 0) ^ mask) == iota((128, 128), 1)).astype(F32).astype(BF16)
        part = jnp.dot(jnp.where(which == h, picked, 0.0).astype(BF16), turn, preferred_element_type=F32)
        chosen[...] = part if h == 0 else chosen[...] + part
    for axis in range(3):
        for d in range(4):
            v = (INNER * 0.5) * row[axis : axis + 1, :] - d - (INNER * 0.5) * column[axis]
            squares[axis * 4 + d] = v * v + (SOFTEN if axis == 2 else 0.0)
    matrices[...] = jnp.zeros_like(matrices)
    total[...] = jnp.zeros_like(total)
    for key, members in far_groups().items():
        ranges = [range(4) if every else (0, 2) for every in key]
        leaves = [(x, y, z) for x in ranges[0] for y in ranges[1] for z in ranges[2]]
        for n, (a, b, c) in enumerate(members):
            m = lax.rsqrt(squares[a] + squares[4 + b] + squares[8 + c])
            matrices[n * WIDE : n * WIDE + SPAD, :] = m.astype(BF16)
            flag = chosen[(a * 16 + b * 4 + c) * 8 : (a * 16 + b * 4 + c) * 8 + 8, :]
            for i in range(0, len(leaves), 2):
                tiles = []
                for x, y, z in leaves[i : i + 2]:
                    at = (((x + 2 + a) * 8 + y + 2 + b) * 8 + z + 2 + c) * 8
                    leaf = x * 16 + y * 4 + z
                    keep = jnp.broadcast_to(flag[:, leaf : leaf + 1], (8, 128))
                    tiles.append([framed[half, at : at + 8, :] * keep for half in range(2)])
                for half in range(2):
                    lanes = slice(n * WIDE + half * 128, n * WIDE + half * 128 + 128)
                    stacked[i * 8 : i * 8 + 16, lanes] = jnp.concatenate([t[half] for t in tiles], axis=0).astype(BF16)
        rows, depth = len(leaves) * 8, len(members) * WIDE
        product = jnp.dot(stacked[0:rows, 0:depth], matrices[0:depth, :], preferred_element_type=F32)
        for i, (x, y, z) in enumerate(leaves):
            leaf = x * 16 + y * 4 + z
            for half in range(2):
                total[half, leaf * 8 : leaf * 8 + 8, :] += product[i * 8 : i * 8 + 8, half * 128 : half * 128 + 128]
    result = jnp.zeros((64, WIDE), F32)
    for h in range(8):
        parts = [total.at[half][pl.ds(h, 64, stride=8), :] for half in range(2)]
        hi, lo = split2(jnp.concatenate(parts, axis=1))
        both = jnp.dot(jnp.concatenate([hi, lo], axis=0), permutation(h), preferred_element_type=F32).astype(BF16)
        mask = (48 if h & 4 else 0) + (12 if h & 2 else 0) + (3 if h & 1 else 0)
        turn = ((iota((64, 128), 0) ^ mask) == (iota((64, 128), 1) & 63)).astype(F32).astype(BF16)
        result = result + jnp.dot(turn, both, preferred_element_type=F32)
    out[...] = result


def near_kernel(
    first_row, rows_here, z0, z1, z2, z3, ylo, yhi, xlo, xhi, flags,
    out, lines, sources, points, listed, shifted, sums,
):
    refs = ((z0, z1, z2, z3), ylo, yhi, xlo, xhi)
    for x in range(6):
        for y in range(6):
            for pair in range(4):
                record = particle_record(refs, x - 1, y - 1, pair)
                for c in range(4):
                    lines[c, x * 6 + y : x * 6 + y + 1, pair * 128 : pair * 128 + 128] = record[c : c + 1]
    for c in range(4):
        whole = lines[c]
        half_turn = pltpu.roll(whole, 64, 1)
        for e, (line, at) in enumerate(((half_turn, 128), (whole, 128), (half_turn, 256))):
            if c == 2:
                line = line + float(e - 1)
            for half in range(2):
                sources.at[c, half][pl.ds(e, 40, stride=3), :] = line[:, at + half * 128 : at + half * 128 + 128]
    same = (iota((64, WIDE), 1) & 63) == iota((64, WIDE), 0)
    block = ((iota((WIDE, WIDE), 0) >> 6) == (iota((WIDE, WIDE), 1) >> 6)).astype(F32).astype(BF16)
    zone = iota((32, WIDE), 1) >> 6
    step_y = (iota((9, WIDE), 0) // 3 - 1).astype(F32)

    def one_row(i, carry):
        r = i + first_row
        x, y = r >> 2, r & 3
        pieces = []
        for c in range(3):
            v = jnp.concatenate([z1[16 + r, c : c + 1, :], z2[16 + r, c : c + 1, :]], axis=1)
            for _ in range(3):
                b = v.astype(BF16).astype(F32)
                pieces.append(jnp.where(same, b, 0.0).astype(BF16))
                v = v - b
        spread = jnp.dot(jnp.concatenate(pieces, axis=0), block, preferred_element_type=F32)
        square = jnp.full((64, WIDE), SOFTEN, F32)
        for c in range(3):
            at = c * 192
            v = spread[at : at + 64] + spread[at + 64 : at + 128] + spread[at + 128 : at + 192]
            square = square + v * v
            points[c] = -2.0 * v
        points[3] = square
        f = flags[x, y]
        lists = jnp.zeros((32, WIDE), F32)
        for z in range(4):
            lists = jnp.where(zone == z, f[:, z : z + 1], lists)
        listed[...] = lists
        for ex in range(3):
            at = ((x + ex) * 6 + y) * 3
            sx, sy, sz, q = (
                jnp.concatenate([sources.at[c, half][pl.ds(at, 9), :] for half in range(2)], axis=1) for c in range(4)
            )
            sx = sx + float(ex - 1)
            sy = sy + step_y
            shifted[0, ex * 9 : ex * 9 + 9, :] = sx
            shifted[1, ex * 9 : ex * 9 + 9, :] = sy
            shifted[2, ex * 9 : ex * 9 + 9, :] = sz
            shifted[3, ex * 9 : ex * 9 + 9, :] = sx * sx + sy * sy + sz * sz
            shifted[4, ex * 9 : ex * 9 + 9, :] = q * listed[ex * 9 : ex * 9 + 9, :]
        for part in range(2):
            for half in range(2):
                lanes = slice(half * 128, half * 128 + 128)
                rows = slice(part * 32, part * 32 + 32)
                tx, ty, tz, tt = (points[c, rows, lanes] for c in range(4))
                acc = jnp.zeros((32, 128), F32)
                for n in range(27):
                    sx, sy, sz, ss, q = (shifted[c, n : n + 1, lanes] for c in range(5))
                    k = lax.rsqrt((tt + ss) + tx * sx + ty * sy + tz * sz)
                    if n == 13:
                        k = jnp.where(same[rows, lanes], 0.0, k)
                    acc = acc + k * q
                sums[rows, lanes] = acc
        hi, lo = split2(sums[...])
        both = jnp.dot(jnp.concatenate([hi, lo], axis=0), block, preferred_element_type=F32)
        picked = jnp.where(same, both[0:64] + both[64:128], 0.0)
        out[pl.ds(i, 1), :] = jnp.sum(picked, axis=0, keepdims=True)
        return carry

    lax.fori_loop(0, rows_here, one_row, 0)


def last_kernel(
    counts, gathered, far, near0, near1, pos, down, column, row, tail,
    out, operator, squares, offsets, tails, acc, checks, ends,
):
    padded_operator(down, operator)
    segment = iota((1, 128), 1) >> 5
    at = 0
    for axis, ring in enumerate((RING8, RING4, RING8)):
        outer = (INNER * HALF) * column[axis, :, 0:128]
        base = outer - (INNER * HALF) * row[axis : axis + 1, 0:128]
        end = outer - (INNER * HALF) * tail[axis : axis + 1, :]
        soft = SOFTEN if axis == 2 else 0.0
        for i, delta in enumerate(ring):
            v = base - float(delta * 4)
            offsets[at + i] = v * v + soft
            if axis < 2:
                v = end - float(delta * 4)
                tails[at + i] = v * v
            elif i % 4 == 0:
                d = ring[i : i + 4]
                shift = jnp.where(
                    segment < 2, jnp.where(segment == 0, d[0], d[1]), jnp.where(segment == 2, d[2], d[3])
                ).astype(F32)
                v = end - 4.0 * shift
                tails[at + i // 4] = v * v + soft
        at += len(ring)
    acc[...] = jnp.zeros_like(acc)

    def pair(i, carry):
        x, y = i >> 2, i & 3
        lines, ends = [], [jnp.zeros((1, 128), F32)] * 2
        for z in range(8):
            m = i * 8 + z
            both = gathered[m] * jnp.where(m == SELF, 0.0, 1.0)
            lines.append(both[0:1])
            end = both[1:2]
            ends[z // 4] = ends[z // 4] + (pltpu.roll(end, 32 * (z % 4), 1) if z % 4 else end)
        for part in range(4):
            rows = slice(part * 40, part * 40 + 40)
            xy = offsets[x, rows, :] + offsets[8 + y, rows, :]
            total = acc[rows, 0:128]
            for z in range(8):
                total = total + lax.rsqrt(xy + offsets[12 + z, rows, :]) * lines[z]
            acc[rows, 0:128] = total
            xy = tails[x, rows, :] + tails[8 + y, rows, :]
            total = acc[rows, 128:256]
            for z in range(2):
                total = total + lax.rsqrt(xy + tails[12 + z, rows, :]) * ends[z]
            acc[rows, 128:256] = total
        return carry

    lax.fori_loop(0, 32, pair, 0)
    ones = jnp.ones((WIDE, WIDE), F32)
    summed = jnp.dot(acc[...], ones, precision=HIGHEST, preferred_element_type=F32)
    local = BREADTH * jnp.dot(operator[...], summed, precision=HIGHEST, preferred_element_type=F32)
    leaf_squares(column, row, tail, squares)
    checks[...] = jnp.zeros_like(checks)
    for x in range(4):
        for y in range(4):
            lines = [jnp.zeros((8, 128), F32)] * 5
            for part in range(4):
                rows = slice(part * 40, part * 40 + 40)
                weight = local[rows, 0:128]
                for z in range(5):
                    lanes = slice(0, 128) if z < 4 else slice(128, 256)
                    xy = squares[x, rows, lanes] + squares[4 + y, rows, lanes]
                    v = lax.rsqrt(xy + squares[8 + z % 4, rows, lanes]) * weight
                    for s in range(5):
                        lines[z] = lines[z] + v[s * 8 : s * 8 + 8]
            for z in range(4):
                t = x * 16 + y * 4 + z
                checks[0, t : t + 1, :] = jnp.sum(lines[z], axis=0, keepdims=True)
            r = x * 4 + y
            ends[r : r + 1, :] = jnp.sum(lines[4], axis=0, keepdims=True)
    used = iota((16, 128), 1) < SURF - 128
    for z in range(4):
        part = pltpu.roll(ends[...], 128 - 32 * z, 1) if z else ends[...]
        checks.at[1][pl.ds(z, 16, stride=4), :] = jnp.where(used, part, 0.0)
    both = jnp.concatenate([checks[0], checks[1]], axis=1)
    both = both + jnp.concatenate([far[...], jnp.zeros((64, WIDE), F32)], axis=0)
    local = jnp.dot(operator[...], both.T, precision=HIGHEST, preferred_element_type=F32)
    hi, lo = split2(local[0:SPAD])
    both = jnp.concatenate([hi, lo], axis=0)
    for x in range(4):
        for y in range(4):
            r = x * 4 + y
            spread = (iota((128, WIDE), 0) == r * 4 + (iota((128, WIDE), 1) >> 6)).astype(F32).astype(BF16)
            wide = jnp.dot(both, spread, preferred_element_type=F32)
            px, py, pz = (pos[c, x, y : y + 1, :] for c in range(3))
            k = inverse_distance(
                (OUTER * 0.5) * column[0] - px,
                (OUTER * 0.5) * column[1] - py,
                (OUTER * 0.5) * column[2] - pz,
            )
            line = jnp.sum(k * (wide[0:SPAD] + wide[SPAD : 2 * SPAD]), axis=0, keepdims=True)
            near = near0 if r < 8 else near1
            out[x, y : y + 1, :] = occupied_row(counts, x, y) * (line + near[r % 8 : r % 8 + 1, :])


def call(body, outs, scratch, memory, name, work, *args):
    spaces = {"v": pltpu.VMEM, "s": pltpu.SMEM}
    return pl.pallas_call(
        body,
        out_shape=[jax.ShapeDtypeStruct(s, F32) for s in outs],
        in_specs=[pl.BlockSpec(memory_space=spaces[m]) for m in memory],
        out_specs=[pl.BlockSpec(memory_space=pltpu.VMEM) for _ in outs],
        scratch_shapes=[pltpu.VMEM(s, d) for s, d in scratch],
        compiler_params=pltpu.CompilerParams(vmem_limit_bytes=40 << 20),
        cost_estimate=pl.CostEstimate(flops=work * 1000000, transcendentals=0, bytes_accessed=1 << 20),
        name=name,
    )(*args)


def shifted(array, axis, distance):
    n = lax.axis_size(axis)
    return lax.ppermute(array, axis, [((i + distance) % n, i) for i in range(n)])


def body(positions, charges, counts, near_flags, far_flags, up_operator, down_operator):
    column, row, tail, mirror, pick = (jnp.asarray(t) for t in tables())
    below, above = call(
        upward_kernel,
        [(33, 4, 128), (33, 4, 128)],
        [
            ((2 * SPAD, 16 * WIDE), BF16), ((WIDE, WIDE), F32), ((12, SPAD, WIDE), F32),
            ((WIDE, WIDE), F32), ((1, 64, 128), F32),
        ],
        "vvsvvvv", "upward", 6000, positions, charges, counts, up_operator, column, row, tail,
    )
    own = (shifted(above, "gz", -1), below, above, shifted(below, "gz", 1))

    grid = [[v[k * 16 : k * 16 + 16].reshape(4, 4, 4, 128) for v in own] for k in range(2)]
    blocks = [own[n][32:33] for n in (0, 1, 3)]

    def to_y(low, one):
        parts = [v[:, low : low + 2].reshape(8, 4, 128) for v in grid[0]]
        parts += [v[:, one].reshape(4, 4, 128) for v in grid[1]]
        return jnp.concatenate(parts + blocks, axis=0)

    ylo = shifted(to_y(2, 3), "gy", -1)
    yhi = shifted(to_y(0, 0), "gy", 1)
    blocks = jnp.concatenate([ylo[48:51]] + blocks + [yhi[48:51]], axis=0)

    def to_x(low, one):
        parts = []
        for s in range(4):
            sides = [v[s * 8 : s * 8 + 8].reshape(4, 2, 4, 128)[low : low + 2] for v in (ylo, yhi)]
            parts.append(jnp.concatenate([sides[0], grid[0][s][low : low + 2], sides[1]], axis=1).reshape(16, 4, 128))
        for s in range(4):
            at = 32 + s * 4 + one
            parts += [ylo[at : at + 1], grid[1][s][one], yhi[at : at + 1]]
        return jnp.concatenate(parts + [blocks], axis=0)

    xlo = shifted(to_x(2, 3), "gx", -1)
    xhi = shifted(to_x(0, 0), "gx", 1)
    halo = (*own, ylo, yhi, xlo, xhi)

    held = jnp.concatenate([xlo[88:97], blocks, xhi[88:97]], axis=0)[:, 0:2]
    held = jnp.concatenate([held, shifted(held, "gx", 3), shifted(held[9:27], "gx", -3)], axis=0)
    held = held.reshape(8, 3, 3, 2, 128)
    held = jnp.concatenate([held, shifted(held[:, 1], "gy", 2)[:, None]], axis=1)
    forward, back = shifted(held, "gz", 3), shifted(held[:, :, 1:3], "gz", -3)
    gathered = jnp.concatenate([held, forward, back], axis=2).reshape(256, 2, 128)

    flags = jnp.pad(far_flags.reshape(CLASSES, 64).astype(BF16), ((0, 384 - CLASSES), (0, 64)))
    (far,) = call(
        far_kernel,
        [(64, WIDE)],
        [
            ((2, 512, 128), F32),
            ((512, WIDE), BF16), ((512, WIDE), BF16), ((2, 4096, 128), F32), ((512, 128), F32),
            ((12, SPAD, WIDE), F32), ((512, 8 * WIDE), BF16), ((8 * WIDE, WIDE), BF16), ((2, 512, 128), F32),
        ],
        "v" * 13, "far", 7000, *halo, flags, pick, mirror, column, row,
    )
    near_flags = near_flags.astype(F32)
    centre = jnp.ones((1, *near_flags.shape[1:]), F32)
    listed = jnp.concatenate([near_flags[0:13], centre, near_flags[13:26], jnp.zeros((5, *near_flags.shape[1:]), F32)], axis=0)
    listed = listed.transpose(1, 2, 0, 3)
    near = []
    for n in range(2):
        near += call(
            functools.partial(near_kernel, 8 * n, 8),
            [(8, WIDE)],
            [
                ((4, 40, 512), F32), ((4, 2, 120, 128), F32), ((4, 64, WIDE), F32), ((32, WIDE), F32),
                ((5, 32, WIDE), F32), ((64, WIDE), F32),
            ],
            "v" * 9, "near", 6000, *halo, listed,
        )
    (potential,) = call(
        last_kernel,
        [(4, 4, WIDE)],
        [
            ((WIDE, WIDE), F32), ((12, SPAD, WIDE), F32), ((20, SPAD, 128), F32), ((14, SPAD, 128), F32),
            ((WIDE, WIDE), F32), ((2, 128, 128), F32), ((16, 128), F32),
        ],
        "svvvvvvvvv", "last", 9000, counts, gathered, far, near[0], near[1], positions, down_operator, column, row, tail,
    )
    return potential


def solution(mesh):
    return jax.shard_map(
        body,
        mesh=mesh,
        in_specs=(
            P(None, "gx", "gy", "gz"),
            P("gx", "gy", "gz"),
            P("gx", "gy", "gz"),
            P(None, "gx", "gy", "gz"),
            P(None, "gx", "gy", "gz"),
            P(),
            P(),
        ),
        out_specs=P("gx", "gy", "gz"),
        check_vma=False,
    )
```

```python
import functools

import jax
import jax.numpy as jnp
import ml_dtypes
import numpy as np
from jax import lax
from jax.experimental import pallas as pl
from jax.experimental.pallas import tpu as pltpu
from jax.sharding import PartitionSpec as P

ORDER = 6
SURF = 152
SPAD = 160
WIDE = 256
LEAVES = 4
SLOTS = 64
CLASSES = 343
INNER = 1.05
OUTER = 2.95
SOFTEN = 0.01
HALF = 2.0
BREADTH = 4.0
HIGHEST = lax.Precision.HIGHEST
F32 = jnp.float32
BF16 = jnp.bfloat16
NT = (((1,), (1,)), ((), ()))
RING8 = (-1, 0, 1, 2, 3, -4, -3, -2)
RING4 = (-1, 0, 1, -2)
SELF = (1 * 4 + 1) * 8 + 1


def surface_points():
    points = []
    for i in range(ORDER):
        for j in range(ORDER):
            for k in range(ORDER):
                if min(i, j, k) == 0 or max(i, j, k) == ORDER - 1:
                    points.append((i, j, k))
    return points


def tables():
    points = surface_points()
    spacing = np.linspace(-1.0, 1.0, ORDER)
    g = np.array([[spacing[i] for i in p] for p in points], dtype=np.float32)
    column = np.zeros((3, SPAD, WIDE), np.float32)
    column[:, :SURF, :] = g.T[:, :, None]
    row = np.zeros((8, WIDE), np.float32)
    row[:3, :SURF] = g.T
    tail = np.tile(row[:, 128:160], (1, 4))
    where = {p: n for n, p in enumerate(points)}
    mirror = np.full((8, WIDE), -1, np.int32)
    for h in range(8):
        sign = (h >> 2 & 1, h >> 1 & 1, h & 1)
        for n, p in enumerate(points):
            mirror[h, n] = where[tuple(ORDER - 1 - c if f else c for c, f in zip(p, sign))]
    pick = np.zeros((64 * 8, 384), np.float32)
    for a in range(4):
        for b in range(4):
            for c in range(4):
                if max(a, b, c) < 2:
                    continue
                for h in range(8):
                    d = [-v if f else v for v, f in zip((a, b, c), (h >> 2 & 1, h >> 1 & 1, h & 1))]
                    number = (d[0] + 3) * 49 + (d[1] + 3) * 7 + d[2] + 3
                    pick[(a * 16 + b * 4 + c) * 8 + h, number] = 1.0
    return column, row, tail, mirror, pick.astype(ml_dtypes.bfloat16)


def iota(shape, dim):
    return lax.broadcasted_iota(jnp.int32, shape, dim)


def split2(v):
    hi = v.astype(BF16)
    return hi, (v - hi.astype(F32)).astype(BF16)


def inverse_distance(x, y, z):
    return lax.rsqrt(x * x + y * y + z * z + SOFTEN)


def occupied_row(counts, x, y):
    lane = iota((1, WIDE), 1)
    zone = lane >> 6
    n = jnp.where(
        zone < 2,
        jnp.where(zone == 0, counts[x, y, 0], counts[x, y, 1]),
        jnp.where(zone == 2, counts[x, y, 2], counts[x, y, 3]),
    )
    return ((lane & 63) < n).astype(F32)


def padded_operator(ref, out):
    out[...] = jnp.zeros_like(out)
    out[0:SURF, 0:SURF] = ref[...]


def leaf_squares(column, row, tail, squares):
    segment = (iota((1, 128), 1) >> 5).astype(F32)
    for axis in range(3):
        outer = (OUTER * HALF) * column[axis, :, 0:128]
        inner = (INNER * 0.5) * row[axis : axis + 1, 0:128]
        last = (INNER * 0.5) * tail[axis : axis + 1, :]
        soft = SOFTEN if axis == 2 else 0.0
        for t in range(LEAVES):
            d = outer - ((t - 1.5) + inner)
            squares[axis * LEAVES + t, :, 0:128] = d * d + soft
            if axis < 2:
                d = outer - ((t - 1.5) + last)
                squares[axis * LEAVES + t, :, 128:256] = d * d
            elif t == 0:
                d = outer - ((segment - 1.5) + last)
                squares[axis * LEAVES, :, 128:256] = d * d + soft


def upward_kernel(
    pos, chg, counts, up, column, row, tail,
    below, above,
    terms, operator, squares, acc, leaves,
):
    padded_operator(up, operator)
    leaf_squares(column, row, tail, squares)
    for x in range(4):
        for y in range(4):
            r = x * 4 + y
            q = chg[x, y : y + 1, :] * occupied_row(counts, x, y)
            px, py, pz = (pos[c, x, y : y + 1, :] for c in range(3))
            k = (
                inverse_distance(
                    (OUTER * 0.5) * column[0] - px,
                    (OUTER * 0.5) * column[1] - py,
                    (OUTER * 0.5) * column[2] - pz,
                )
                * q
            )
            hi, lo = split2(k)
            terms[0:SPAD, r * WIDE : (r + 1) * WIDE] = hi
            terms[SPAD : 2 * SPAD, r * WIDE : (r + 1) * WIDE] = lo
            for c, v in enumerate((px, py, pz, q)):
                below[16 + r, c : c + 1, :] = v[:, 0:128]
                above[16 + r, c : c + 1, :] = v[:, 128:256]
    gather = ((iota((16 * WIDE, 128), 0) >> 6) == iota((16 * WIDE, 128), 1)).astype(F32).astype(BF16)
    both = jnp.dot(terms[...], gather, preferred_element_type=F32)
    check = both[0:SPAD] + both[SPAD : 2 * SPAD]
    check = jnp.concatenate([check, jnp.zeros((WIDE - SPAD, 128), F32)], axis=0).T[0:64, :]
    up_eq = lax.dot_general(check, operator[...], NT, precision=HIGHEST, preferred_element_type=F32)
    low = up_eq.astype(BF16).astype(F32)
    for r in range(16):
        for out, at in ((below, 0), (above, 2)):
            pair = low[r * 4 + at : r * 4 + at + 2]
            out[r, 0:2, :] = pair[:, 0:128]
            out[r, 2:4, :] = pair[:, 128:256]
    leaves[0] = up_eq[:, 128:256]
    lines = leaves.at[0][pl.ds(0, 16, stride=4), :]
    for z in range(1, 4):
        lines = lines + pltpu.roll(leaves.at[0][pl.ds(z, 16, stride=4), :], 32 * z, 1)
    acc[...] = jnp.zeros_like(acc)
    for part in range(4):
        rows = slice(part * 40, part * 40 + 40)
        first, last = jnp.zeros((40, 128), F32), jnp.zeros((40, 128), F32)
        for x in range(4):
            for y in range(4):
                xy = squares[x, rows, 0:128] + squares[4 + y, rows, 0:128]
                for z in range(4):
                    t = x * 16 + y * 4 + z
                    first = first + lax.rsqrt(xy + squares[8 + z, rows, 0:128]) * up_eq[t : t + 1, 0:128]
                xy = squares[x, rows, 128:256] + squares[4 + y, rows, 128:256]
                r = x * 4 + y
                last = last + lax.rsqrt(xy + squares[8, rows, 128:256]) * lines[r : r + 1, :]
        acc[rows, 0:128] = first
        acc[rows, 128:256] = last
    ones = jnp.ones((8, WIDE), F32)
    summed = lax.dot_general(ones, acc[...], NT, precision=HIGHEST, preferred_element_type=F32)
    block = BREADTH * lax.dot_general(summed, operator[...], NT, precision=HIGHEST, preferred_element_type=F32)
    for out in (below, above):
        out[32, 0:1, :] = block[0:1, 0:128]
        out[32, 1:2, :] = block[0:1, 128:256]
        out[32, 2:4, :] = jnp.zeros((2, 128), F32)


def eq_record(refs, x, y, s):
    own, ylo, yhi, xlo, xhi = refs
    if x < 2:
        return xlo[(s * 2 + x) * 8 + y]
    if x > 5:
        return xhi[(s * 2 + x - 6) * 8 + y]
    if y < 2:
        return ylo[s * 8 + (x - 2) * 2 + y]
    if y > 5:
        return yhi[s * 8 + (x - 2) * 2 + y - 6]
    return own[s][(x - 2) * 4 + y - 2]


def particle_record(refs, x, y, s):
    own, ylo, yhi, xlo, xhi = refs
    if x < 0:
        return xlo[64 + s * 6 + y + 1]
    if x > 3:
        return xhi[64 + s * 6 + y + 1]
    if y < 0:
        return ylo[32 + s * 4 + x]
    if y > 3:
        return yhi[32 + s * 4 + x]
    return own[s][16 + x * 4 + y]


def far_groups():
    groups = {}
    for a in range(4):
        for b in range(4):
            for c in range(4):
                if max(a, b, c) >= 2:
                    key = tuple(v in (1, 2) for v in (a, b, c))
                    groups.setdefault(key, []).append((a, b, c))
    return groups


def far_kernel(
    z0, z1, z2, z3, ylo, yhi, xlo, xhi, flags, pick, mirror, column, row,
    out, halo, low, turned, framed, chosen, squares, stacked, matrices, total,
):
    refs = ((z0, z1, z2, z3), ylo, yhi, xlo, xhi)
    for x in range(8):
        for y in range(8):
            for pair in range(4):
                record = eq_record(refs, x, y, pair)
                at = (x * 8 + y) * 8 + pair * 2
                halo[0, at : at + 2, :] = record[0:2]
                halo[1, at : at + 2, :] = record[2:4]
    for half in range(2):
        low[:, half * 128 : half * 128 + 128] = halo[half].astype(BF16)
    turn = ((iota((WIDE, WIDE), 0) ^ 7) == iota((WIDE, WIDE), 1)).astype(F32).astype(BF16)
    for n in range(2):
        part = slice(n * WIDE, n * WIDE + WIDE)
        turned[part, :] = jnp.dot(turn, low[part, :], preferred_element_type=F32).astype(BF16)

    def permutation(h):
        return (iota((WIDE, WIDE), 0) == mirror[h : h + 1, :]).astype(F32).astype(BF16)

    for h in range(8):
        source = turned if h & 1 else low
        frame = jnp.dot(source[...], permutation(h), preferred_element_type=F32)
        for x in range(8):
            for y in range(8):
                xf, yf = (7 - x if h & 4 else x), (7 - y if h & 2 else y)
                at = (x * 8 + y) * 8
                for n in range(2):
                    framed.at[n][pl.ds((xf * 8 + yf) * 64 + h, 8, stride=8), :] = frame[
                        at : at + 8, n * 128 : n * 128 + 128
                    ]
    picked = jnp.dot(pick[...], flags[...], preferred_element_type=F32)
    which = iota((512, 128), 0) & 7
    for h in range(8):
        mask = (48 if h & 4 else 0) + (12 if h & 2 else 0) + (3 if h & 1 else 0)
        turn = ((iota((128, 128), 0) ^ mask) == iota((128, 128), 1)).astype(F32).astype(BF16)
        part = jnp.dot(jnp.where(which == h, picked, 0.0).astype(BF16), turn, preferred_element_type=F32)
        chosen[...] = part if h == 0 else chosen[...] + part
    for axis in range(3):
        for d in range(4):
            v = (INNER * 0.5) * row[axis : axis + 1, :] - d - (INNER * 0.5) * column[axis]
            squares[axis * 4 + d] = v * v + (SOFTEN if axis == 2 else 0.0)
    matrices[...] = jnp.zeros_like(matrices)
    total[...] = jnp.zeros_like(total)
    for key, members in far_groups().items():
        ranges = [range(4) if every else (0, 2) for every in key]
        leaves = [(x, y, z) for x in ranges[0] for y in ranges[1] for z in ranges[2]]
        for n, (a, b, c) in enumerate(members):
            m = lax.rsqrt(squares[a] + squares[4 + b] + squares[8 + c])
            matrices[n * WIDE : n * WIDE + SPAD, :] = m.astype(BF16)
            flag = chosen[(a * 16 + b * 4 + c) * 8 : (a * 16 + b * 4 + c) * 8 + 8, :]
            for i in range(0, len(leaves), 2):
                tiles = []
                for x, y, z in leaves[i : i + 2]:
                    at = (((x + 2 + a) * 8 + y + 2 + b) * 8 + z + 2 + c) * 8
                    leaf = x * 16 + y * 4 + z
                    keep = jnp.broadcast_to(flag[:, leaf : leaf + 1], (8, 128))
                    tiles.append([framed[half, at : at + 8, :] * keep for half in range(2)])
                for half in range(2):
                    lanes = slice(n * WIDE + half * 128, n * WIDE + half * 128 + 128)
                    stacked[i * 8 : i * 8 + 16, lanes] = jnp.concatenate([t[half] for t in tiles], axis=0).astype(BF16)
        rows, depth = len(leaves) * 8, len(members) * WIDE
        product = jnp.dot(stacked[0:rows, 0:depth], matrices[0:depth, :], preferred_element_type=F32)
        for i, (x, y, z) in enumerate(leaves):
            leaf = x * 16 + y * 4 + z
            for half in range(2):
                total[half, leaf * 8 : leaf * 8 + 8, :] += product[i * 8 : i * 8 + 8, half * 128 : half * 128 + 128]
    result = jnp.zeros((64, WIDE), F32)
    for h in range(8):
        parts = [total.at[half][pl.ds(h, 64, stride=8), :] for half in range(2)]
        hi, lo = split2(jnp.concatenate(parts, axis=1))
        both = jnp.dot(jnp.concatenate([hi, lo], axis=0), permutation(h), preferred_element_type=F32).astype(BF16)
        mask = (48 if h & 4 else 0) + (12 if h & 2 else 0) + (3 if h & 1 else 0)
        turn = ((iota((64, 128), 0) ^ mask) == (iota((64, 128), 1) & 63)).astype(F32).astype(BF16)
        result = result + jnp.dot(turn, both, preferred_element_type=F32)
    out[...] = result


def near_kernel(first, planes, *refs):
    *halo, flags, out, lines, sources, points, shifted, sums = refs
    refs = (halo[0:4], *halo[4:])
    if len(halo) == 6:
        refs = (*refs, None, None)
    z1, z2 = halo[1], halo[2]
    count = (planes + 2) * 6
    for x in range(planes + 2):
        for y in range(6):
            for pair in range(4):
                record = particle_record(refs, x + first - 1, y - 1, pair)
                for c in range(4):
                    lines[c, x * 6 + y : x * 6 + y + 1, pair * 128 : pair * 128 + 128] = record[c : c + 1]
    for c in range(4):
        whole = lines[c]
        half_turn = pltpu.roll(whole, 64, 1)
        for e, (line, at) in enumerate(((half_turn, 128), (whole, 128), (half_turn, 256))):
            if c == 2:
                line = line + float(e - 1)
            for half in range(2):
                lanes = slice(at + half * 128, at + half * 128 + 128)
                sources.at[c, half][pl.ds(e, count, stride=3), :] = line[0:count, lanes]
    same = (iota((64, WIDE), 1) & 63) == iota((64, WIDE), 0)
    block = ((iota((WIDE, WIDE), 0) >> 6) == (iota((WIDE, WIDE), 1) >> 6)).astype(F32).astype(BF16)
    zone = iota((32, WIDE), 1) >> 6
    step_y = (iota((9, WIDE), 0) // 3 - 1).astype(F32)
    for i in range(planes * 4):
        r = first * 4 + i
        x, y = i // 4, i % 4
        pieces = []
        for c in range(3):
            v = jnp.concatenate([z1[16 + r, c : c + 1, :], z2[16 + r, c : c + 1, :]], axis=1)
            for _ in range(3):
                b = v.astype(BF16).astype(F32)
                pieces.append(jnp.where(same, b, 0.0).astype(BF16))
                v = v - b
        spread = jnp.dot(jnp.concatenate(pieces, axis=0), block, preferred_element_type=F32)
        square = jnp.full((64, WIDE), SOFTEN, F32)
        for c in range(3):
            at = c * 192
            v = spread[at : at + 64] + spread[at + 64 : at + 128] + spread[at + 128 : at + 192]
            square = square + v * v
            points[i, c] = -2.0 * v
        points[i, 3] = square
        f = flags[x + first, y]
        lists = jnp.zeros((32, WIDE), F32)
        for z in range(4):
            lists = jnp.where(zone == z, f[:, z : z + 1], lists)
        for ex in range(3):
            at = ((x + ex) * 6 + y) * 3
            here = slice(ex * 9, ex * 9 + 9)
            sx, sy, sz, q = (
                jnp.concatenate([sources[c, half, at : at + 9, :] for half in range(2)], axis=1) for c in range(4)
            )
            sx = sx + float(ex - 1)
            sy = sy + step_y
            shifted[i, 0, here, :] = sx
            shifted[i, 1, here, :] = sy
            shifted[i, 2, here, :] = sz
            shifted[i, 3, here, :] = sx * sx + sy * sy + sz * sz
            shifted[i, 4, here, :] = q * lists[here]

    def one_row(i, carry):
        for half in range(2):
            lanes = slice(half * 128, half * 128 + 128)
            tx, ty, tz, tt = (points[i, c, :, lanes] for c in range(4))
            acc = jnp.zeros((64, 128), F32)
            for n in range(27):
                sx, sy, sz, ss, q = (shifted[i, c, n : n + 1, lanes] for c in range(5))
                k = lax.rsqrt((tt + ss) + tx * sx + ty * sy + tz * sz)
                if n == 13:
                    k = jnp.where(same[:, lanes], 0.0, k)
                acc = acc + k * q
            sums[i, :, lanes] = acc
        return carry

    lax.fori_loop(0, planes * 4, one_row, 0)
    for i in range(planes * 4):
        hi, lo = split2(sums[i])
        both = jnp.dot(jnp.concatenate([hi, lo], axis=0), block, preferred_element_type=F32)
        picked = jnp.where(same, both[0:64] + both[64:128], 0.0)
        out[i : i + 1, :] = jnp.sum(picked, axis=0, keepdims=True)


def last_kernel(
    counts, gathered, far, near0, near12, near3, pos, down, column, row, tail,
    out, operator, squares, offsets, tails, acc, checks, ends,
):
    padded_operator(down, operator)
    segment = iota((1, 128), 1) >> 5
    at = 0
    for axis, ring in enumerate((RING8, RING4, RING8)):
        outer = (INNER * HALF) * column[axis, :, 0:128]
        base = outer - (INNER * HALF) * row[axis : axis + 1, 0:128]
        end = outer - (INNER * HALF) * tail[axis : axis + 1, :]
        soft = SOFTEN if axis == 2 else 0.0
        for i, delta in enumerate(ring):
            v = base - float(delta * 4)
            offsets[at + i] = v * v + soft
            if axis < 2:
                v = end - float(delta * 4)
                tails[at + i] = v * v
            elif i % 4 == 0:
                d = ring[i : i + 4]
                shift = jnp.where(
                    segment < 2, jnp.where(segment == 0, d[0], d[1]), jnp.where(segment == 2, d[2], d[3])
                ).astype(F32)
                v = end - 4.0 * shift
                tails[at + i // 4] = v * v + soft
        at += len(ring)
    acc[...] = jnp.zeros_like(acc)

    def pair(i, carry):
        x, y = i >> 2, i & 3
        lines, ends = [], [jnp.zeros((1, 128), F32)] * 2
        for z in range(8):
            m = i * 8 + z
            both = gathered[m] * jnp.where(m == SELF, 0.0, 1.0)
            lines.append(both[0:1])
            end = both[1:2]
            ends[z // 4] = ends[z // 4] + (pltpu.roll(end, 32 * (z % 4), 1) if z % 4 else end)
        for part in range(4):
            rows = slice(part * 40, part * 40 + 40)
            xy = offsets[x, rows, :] + offsets[8 + y, rows, :]
            total = acc[rows, 0:128]
            for z in range(8):
                total = total + lax.rsqrt(xy + offsets[12 + z, rows, :]) * lines[z]
            acc[rows, 0:128] = total
            xy = tails[x, rows, :] + tails[8 + y, rows, :]
            total = acc[rows, 128:256]
            for z in range(2):
                total = total + lax.rsqrt(xy + tails[12 + z, rows, :]) * ends[z]
            acc[rows, 128:256] = total
        return carry

    lax.fori_loop(0, 32, pair, 0)
    ones = jnp.ones((WIDE, WIDE), F32)
    summed = jnp.dot(acc[...], ones, precision=HIGHEST, preferred_element_type=F32)
    local = BREADTH * jnp.dot(operator[...], summed, precision=HIGHEST, preferred_element_type=F32)
    leaf_squares(column, row, tail, squares)
    checks[...] = jnp.zeros_like(checks)
    for x in range(4):
        for y in range(4):
            lines = [jnp.zeros((8, 128), F32)] * 5
            for part in range(4):
                rows = slice(part * 40, part * 40 + 40)
                weight = local[rows, 0:128]
                for z in range(5):
                    lanes = slice(0, 128) if z < 4 else slice(128, 256)
                    xy = squares[x, rows, lanes] + squares[4 + y, rows, lanes]
                    v = lax.rsqrt(xy + squares[8 + z % 4, rows, lanes]) * weight
                    for s in range(5):
                        lines[z] = lines[z] + v[s * 8 : s * 8 + 8]
            for z in range(4):
                t = x * 16 + y * 4 + z
                checks[0, t : t + 1, :] = jnp.sum(lines[z], axis=0, keepdims=True)
            r = x * 4 + y
            ends[r : r + 1, :] = jnp.sum(lines[4], axis=0, keepdims=True)
    used = iota((16, 128), 1) < SURF - 128
    for z in range(4):
        part = pltpu.roll(ends[...], 128 - 32 * z, 1) if z else ends[...]
        checks.at[1][pl.ds(z, 16, stride=4), :] = jnp.where(used, part, 0.0)
    both = jnp.concatenate([checks[0], checks[1]], axis=1)
    both = both + jnp.concatenate([far[...], jnp.zeros((64, WIDE), F32)], axis=0)
    local = jnp.dot(operator[...], both.T, precision=HIGHEST, preferred_element_type=F32)
    hi, lo = split2(local[0:SPAD])
    both = jnp.concatenate([hi, lo], axis=0)
    for x in range(4):
        for y in range(4):
            r = x * 4 + y
            spread = (iota((128, WIDE), 0) == r * 4 + (iota((128, WIDE), 1) >> 6)).astype(F32).astype(BF16)
            wide = jnp.dot(both, spread, preferred_element_type=F32)
            px, py, pz = (pos[c, x, y : y + 1, :] for c in range(3))
            k = inverse_distance(
                (OUTER * 0.5) * column[0] - px,
                (OUTER * 0.5) * column[1] - py,
                (OUTER * 0.5) * column[2] - pz,
            )
            line = jnp.sum(k * (wide[0:SPAD] + wide[SPAD : 2 * SPAD]), axis=0, keepdims=True)
            near, i = (near0, r) if x == 0 else (near3, r - 12) if x == 3 else (near12, r - 4)
            out[x, y : y + 1, :] = occupied_row(counts, x, y) * (line + near[i : i + 1, :])


def call(body, outs, scratch, memory, name, work, *args, vmem=40):
    spaces = {"v": pltpu.VMEM, "s": pltpu.SMEM}
    return pl.pallas_call(
        body,
        out_shape=[jax.ShapeDtypeStruct(s, F32) for s in outs],
        in_specs=[pl.BlockSpec(memory_space=spaces[m]) for m in memory],
        out_specs=[pl.BlockSpec(memory_space=pltpu.VMEM) for _ in outs],
        scratch_shapes=[pltpu.VMEM(s, d) for s, d in scratch],
        compiler_params=pltpu.CompilerParams(vmem_limit_bytes=vmem << 20),
        cost_estimate=pl.CostEstimate(flops=work * 1000000, transcendentals=0, bytes_accessed=1 << 20),
        name=name,
    )(*args)


def shifted(array, axis, distance):
    n = lax.axis_size(axis)
    return lax.ppermute(array, axis, [((i + distance) % n, i) for i in range(n)])


def body(positions, charges, counts, near_flags, far_flags, up_operator, down_operator):
    column, row, tail, mirror, pick = (jnp.asarray(t) for t in tables())
    below, above = call(
        upward_kernel,
        [(33, 4, 128), (33, 4, 128)],
        [
            ((2 * SPAD, 16 * WIDE), BF16), ((WIDE, WIDE), F32), ((12, SPAD, WIDE), F32),
            ((WIDE, WIDE), F32), ((1, 64, 128), F32),
        ],
        "vvsvvvv", "upward", 6000, positions, charges, counts, up_operator, column, row, tail, vmem=59,
    )
    own = (shifted(above, "gz", -1), below, above, shifted(below, "gz", 1))

    grid = [[v[k * 16 : k * 16 + 16].reshape(4, 4, 4, 128) for v in own] for k in range(2)]
    blocks = [own[n][32:33] for n in (0, 1, 3)]

    def to_y(low, one):
        parts = [v[:, low : low + 2].reshape(8, 4, 128) for v in grid[0]]
        parts += [v[:, one].reshape(4, 4, 128) for v in grid[1]]
        return jnp.concatenate(parts + blocks, axis=0)

    ylo = shifted(to_y(2, 3), "gy", -1)
    yhi = shifted(to_y(0, 0), "gy", 1)
    blocks = jnp.concatenate([ylo[48:51]] + blocks + [yhi[48:51]], axis=0)

    def to_x(low, one):
        parts = []
        for s in range(4):
            sides = [v[s * 8 : s * 8 + 8].reshape(4, 2, 4, 128)[low : low + 2] for v in (ylo, yhi)]
            parts.append(jnp.concatenate([sides[0], grid[0][s][low : low + 2], sides[1]], axis=1).reshape(16, 4, 128))
        for s in range(4):
            at = 32 + s * 4 + one
            parts += [ylo[at : at + 1], grid[1][s][one], yhi[at : at + 1]]
        return jnp.concatenate(parts + [blocks], axis=0)

    up, down = lax.optimization_barrier((to_x(2, 3), to_x(0, 0)))
    xlo = shifted(up, "gx", -1)
    xhi = shifted(down, "gx", 1)
    halo = (*own, ylo, yhi, xlo, xhi)

    held = jnp.concatenate([xlo[88:97], blocks, xhi[88:97]], axis=0)[:, 0:2]
    held = jnp.concatenate([held, shifted(held, "gx", 3), shifted(held[9:27], "gx", -3)], axis=0)
    held = held.reshape(8, 3, 3, 2, 128)
    held = jnp.concatenate([held, shifted(held[:, 1], "gy", 2)[:, None]], axis=1)
    forward, back = shifted(held, "gz", 3), shifted(held[:, :, 1:3], "gz", -3)
    gathered = jnp.concatenate([held, forward, back], axis=2).reshape(256, 2, 128)

    flags = jnp.pad(far_flags.reshape(CLASSES, 64).astype(BF16), ((0, 384 - CLASSES), (0, 64)))
    (far,) = call(
        far_kernel,
        [(64, WIDE)],
        [
            ((2, 512, 128), F32),
            ((512, WIDE), BF16), ((512, WIDE), BF16), ((2, 4096, 128), F32), ((512, 128), F32),
            ((12, SPAD, WIDE), F32), ((512, 8 * WIDE), BF16), ((8 * WIDE, WIDE), BF16), ((2, 512, 128), F32),
        ],
        "v" * 13, "far", 7000, *halo, flags, pick, mirror, column, row,
    )
    near_flags = near_flags.astype(F32)
    centre = jnp.ones((1, *near_flags.shape[1:]), F32)
    listed = jnp.concatenate([near_flags[0:13], centre, near_flags[13:26], jnp.zeros((5, *near_flags.shape[1:]), F32)], axis=0)
    listed = listed.transpose(1, 2, 0, 3)

    def near(first, planes, halo):
        count = (planes + 2) * 6
        (result,) = call(
            functools.partial(near_kernel, first, planes),
            [(planes * 4, WIDE)],
            [
                ((4, count + -count % 8, 512), F32), ((4, 2, count * 3, 128), F32), ((planes * 4, 4, 64, WIDE), F32),
                ((planes * 4, 5, 32, WIDE), F32), ((planes * 4, 64, WIDE), F32),
            ],
            "v" * (len(halo) + 1), "near", 3000 * planes, *halo, listed,
        )
        return result

    inner, low, high = near(1, 2, halo[0:6]), near(0, 1, halo), near(3, 1, halo)
    (potential,) = call(
        last_kernel,
        [(4, 4, WIDE)],
        [
            ((WIDE, WIDE), F32), ((12, SPAD, WIDE), F32), ((20, SPAD, 128), F32), ((14, SPAD, 128), F32),
            ((WIDE, WIDE), F32), ((2, 128, 128), F32), ((16, 128), F32),
        ],
        "svvvvvvvvvv", "last", 9000, counts, gathered, far, low, inner, high, positions, down_operator, column, row, tail,
    )
    return potential


def solution(mesh):
    return jax.shard_map(
        body,
        mesh=mesh,
        in_specs=(
            P(None, "gx", "gy", "gz"),
            P("gx", "gy", "gz"),
            P("gx", "gy", "gz"),
            P(None, "gx", "gy", "gz"),
            P(None, "gx", "gy", "gz"),
            P(),
            P(),
        ),
        out_specs=P("gx", "gy", "gz"),
        check_vma=False,
    )
```

```python
import functools

import jax
import jax.numpy as jnp
import ml_dtypes
import numpy as np
from jax import lax
from jax.experimental import pallas as pl
from jax.experimental.pallas import tpu as pltpu
from jax.sharding import PartitionSpec as P

ORDER = 6
SURF = 152
SPAD = 160
WIDE = 256
LEAVES = 4
SLOTS = 64
CLASSES = 343
INNER = 1.05
OUTER = 2.95
SOFTEN = 0.01
HALF = 2.0
BREADTH = 4.0
HIGHEST = lax.Precision.HIGHEST
F32 = jnp.float32
BF16 = jnp.bfloat16
RING8 = (-1, 0, 1, 2, 3, -4, -3, -2)
RING4 = (-1, 0, 1, -2)
SELF = (1 * 4 + 1) * 8 + 1


def surface_points():
    points = []
    for i in range(ORDER):
        for j in range(ORDER):
            for k in range(ORDER):
                if min(i, j, k) == 0 or max(i, j, k) == ORDER - 1:
                    points.append((i, j, k))
    return points


def tables():
    points = surface_points()
    spacing = np.linspace(-1.0, 1.0, ORDER)
    g = np.array([[spacing[i] for i in p] for p in points], dtype=np.float32)
    column = np.zeros((3, SPAD, 128), np.float32)
    column[:, :SURF, :] = g.T[:, :, None]
    row = np.zeros((8, WIDE), np.float32)
    row[:3, :SURF] = g.T
    tail = np.tile(row[:, 128:160], (1, 4))
    nodes = np.zeros((SPAD, 128), np.float32)
    for n, p in enumerate(points + [points[0]] * (SPAD - SURF)):
        for part in range(3):
            for axis in range(3):
                nodes[n, part * 24 + axis * 8 + p[axis]] = 1.0
    where = {p: n for n, p in enumerate(points)}
    mirror = np.full((8, WIDE), -1, np.int32)
    for h in range(8):
        sign = (h >> 2 & 1, h >> 1 & 1, h & 1)
        for n, p in enumerate(points):
            mirror[h, n] = where[tuple(ORDER - 1 - c if f else c for c, f in zip(p, sign))]
    pick = np.zeros((64 * 8, 384), np.float32)
    for a in range(4):
        for b in range(4):
            for c in range(4):
                if max(a, b, c) < 2:
                    continue
                for h in range(8):
                    d = [-v if f else v for v, f in zip((a, b, c), (h >> 2 & 1, h >> 1 & 1, h & 1))]
                    number = (d[0] + 3) * 49 + (d[1] + 3) * 7 + d[2] + 3
                    pick[(a * 16 + b * 4 + c) * 8 + h, number] = 1.0
    return column, row, tail, nodes.astype(ml_dtypes.bfloat16), mirror, pick.astype(ml_dtypes.bfloat16)


def iota(shape, dim):
    return lax.broadcasted_iota(jnp.int32, shape, dim)


def split2(v):
    hi = v.astype(BF16)
    return hi, (v - hi.astype(F32)).astype(BF16)


def surface_terms(px, py, pz, nodes):
    step = iota((8, WIDE), 0).astype(F32) * (OUTER / (ORDER - 1)) - OUTER * 0.5
    parts = []
    for n, p in enumerate((px, py, pz)):
        d = step - p
        parts.append(d * d + (SOFTEN if n == 2 else 0.0))
    rest = jnp.concatenate(parts, axis=0)
    parts = []
    for _ in range(3):
        b = rest.astype(BF16).astype(F32)
        parts.append(b)
        rest = rest - b
    parts.append(jnp.zeros((128 - 72, WIDE), F32))
    squares = jnp.concatenate(parts, axis=0).astype(BF16)
    return lax.rsqrt(jnp.dot(nodes, squares, preferred_element_type=F32))


def occupied_row(counts, x, y):
    lane = iota((1, WIDE), 1)
    zone = lane >> 6
    n = jnp.where(
        zone < 2,
        jnp.where(zone == 0, counts[x, y, 0], counts[x, y, 1]),
        jnp.where(zone == 2, counts[x, y, 2], counts[x, y, 3]),
    )
    return ((lane & 63) < n).astype(F32)


def padded_operator(ref, out):
    out[...] = jnp.zeros_like(out)
    out[0:SURF, 0:SURF] = ref[...]


def leaf_squares(column, row, tail, squares):
    segment = (iota((1, 128), 1) >> 5).astype(F32)
    for axis in range(3):
        outer = (OUTER * HALF) * column[axis]
        inner = (INNER * 0.5) * row[axis : axis + 1, 0:128]
        last = (INNER * 0.5) * tail[axis : axis + 1, :]
        soft = SOFTEN if axis == 2 else 0.0
        for t in range(LEAVES):
            d = outer - ((t - 1.5) + inner)
            squares[axis * LEAVES + t, :, 0:128] = d * d + soft
            if axis < 2:
                d = outer - ((t - 1.5) + last)
                squares[axis * LEAVES + t, :, 128:256] = d * d
            elif t == 0:
                d = outer - ((segment - 1.5) + last)
                squares[axis * LEAVES, :, 128:256] = d * d + soft


def upward_kernel(
    pos, chg, counts, up, column, row, tail, nodes,
    below, above,
    terms, operator, squares, leaves,
):
    padded_operator(up, operator)
    flipped = operator[...].T
    leaf_squares(column, row, tail, squares)
    for x in range(4):
        for y in range(4):
            r = x * 4 + y
            q = chg[x, y : y + 1, :] * occupied_row(counts, x, y)
            px, py, pz = (pos[c, x, y : y + 1, :] for c in range(3))
            k = surface_terms(px, py, pz, nodes[...]) * q
            hi, lo = split2(k)
            terms[0:SPAD, r * WIDE : (r + 1) * WIDE] = hi
            terms[SPAD : 2 * SPAD, r * WIDE : (r + 1) * WIDE] = lo
            for c, v in enumerate((px, py, pz, q)):
                below[16 + r, c : c + 1, :] = v[:, 0:128]
                above[16 + r, c : c + 1, :] = v[:, 128:256]
    gather = ((iota((16 * WIDE, 128), 0) >> 6) == iota((16 * WIDE, 128), 1)).astype(F32).astype(BF16)
    both = jnp.dot(terms[...], gather, preferred_element_type=F32)
    check = both[0:SPAD] + both[SPAD : 2 * SPAD]
    check = jnp.concatenate([check, jnp.zeros((WIDE - SPAD, 128), F32)], axis=0).T[0:64, :]
    up_eq = jnp.dot(check, flipped, precision=HIGHEST, preferred_element_type=F32)
    low = up_eq.astype(BF16).astype(F32)
    for r in range(16):
        for out, at in ((below, 0), (above, 2)):
            pair = low[r * 4 + at : r * 4 + at + 2]
            out[r, 0:2, :] = pair[:, 0:128]
            out[r, 2:4, :] = pair[:, 128:256]
    leaves[0] = up_eq[:, 128:256]
    lines = leaves.at[0][pl.ds(0, 16, stride=4), :]
    for z in range(1, 4):
        lines = lines + pltpu.roll(leaves.at[0][pl.ds(z, 16, stride=4), :], 32 * z, 1)
    block = jnp.zeros((8, WIDE), F32)
    for part in range(4):
        rows = slice(part * 40, part * 40 + 40)
        first, last = jnp.zeros((40, 128), F32), jnp.zeros((40, 128), F32)
        for x in range(4):
            for y in range(4):
                xy = squares[x, rows, 0:128] + squares[4 + y, rows, 0:128]
                for z in range(4):
                    t = x * 16 + y * 4 + z
                    first = first + lax.rsqrt(xy + squares[8 + z, rows, 0:128]) * up_eq[t : t + 1, 0:128]
                xy = squares[x, rows, 128:256] + squares[4 + y, rows, 128:256]
                r = x * 4 + y
                last = last + lax.rsqrt(xy + squares[8, rows, 128:256]) * lines[r : r + 1, :]
        weight = BREADTH * jnp.sum(first + last, axis=1, keepdims=True)
        for n in range(part * 40, part * 40 + 40, 8):
            block = block + flipped[n : n + 8] * weight[n - part * 40 : n - part * 40 + 8]
    block = jnp.sum(block, axis=0, keepdims=True)
    for out in (below, above):
        out[32, 0:1, :] = block[0:1, 0:128]
        out[32, 1:2, :] = block[0:1, 128:256]
        out[32, 2:4, :] = jnp.zeros((2, 128), F32)


def eq_record(refs, x, y, s):
    own, ylo, yhi, xlo, xhi = refs
    if x < 2:
        return xlo[(s * 2 + x) * 8 + y]
    if x > 5:
        return xhi[(s * 2 + x - 6) * 8 + y]
    if y < 2:
        return ylo[s * 8 + (x - 2) * 2 + y]
    if y > 5:
        return yhi[s * 8 + (x - 2) * 2 + y - 6]
    return own[s][(x - 2) * 4 + y - 2]


def particle_record(refs, x, y, s):
    own, ylo, yhi, xlo, xhi = refs
    if x < 0:
        return xlo[64 + s * 6 + y + 1]
    if x > 3:
        return xhi[64 + s * 6 + y + 1]
    if y < 0:
        return ylo[32 + s * 4 + x]
    if y > 3:
        return yhi[32 + s * 4 + x]
    return own[s][16 + x * 4 + y]


def far_groups():
    groups = {}
    for a in range(4):
        for b in range(4):
            for c in range(4):
                if max(a, b, c) >= 2:
                    key = tuple(v in (1, 2) for v in (a, b, c))
                    groups.setdefault(key, []).append((a, b, c))
    return groups


def far_kernel(
    z0, z1, z2, z3, ylo, yhi, xlo, xhi, flags, pick, mirror, column, row,
    out, halo, low, turned, framed, chosen, squares, stacked, matrices, total,
):
    refs = ((z0, z1, z2, z3), ylo, yhi, xlo, xhi)
    for x in range(8):
        for y in range(8):
            for pair in range(4):
                record = eq_record(refs, x, y, pair)
                at = (x * 8 + y) * 8 + pair * 2
                halo[0, at : at + 2, :] = record[0:2]
                halo[1, at : at + 2, :] = record[2:4]
    for half in range(2):
        low[:, half * 128 : half * 128 + 128] = halo[half].astype(BF16)
    turn = ((iota((WIDE, WIDE), 0) ^ 7) == iota((WIDE, WIDE), 1)).astype(F32).astype(BF16)
    for n in range(2):
        part = slice(n * WIDE, n * WIDE + WIDE)
        turned[part, :] = jnp.dot(turn, low[part, :], preferred_element_type=F32).astype(BF16)

    def permutation(h):
        return (iota((WIDE, WIDE), 0) == mirror[h : h + 1, :]).astype(F32).astype(BF16)

    for h in range(8):
        source = turned if h & 1 else low
        frame = jnp.dot(source[...], permutation(h), preferred_element_type=F32)
        for x in range(8):
            for y in range(8):
                xf, yf = (7 - x if h & 4 else x), (7 - y if h & 2 else y)
                at = (x * 8 + y) * 8
                for n in range(2):
                    framed.at[n][pl.ds((xf * 8 + yf) * 64 + h, 8, stride=8), :] = frame[
                        at : at + 8, n * 128 : n * 128 + 128
                    ]
    picked = jnp.dot(pick[...], flags[...], preferred_element_type=F32)
    which = iota((512, 128), 0) & 7
    for h in range(8):
        mask = (48 if h & 4 else 0) + (12 if h & 2 else 0) + (3 if h & 1 else 0)
        turn = ((iota((128, 128), 0) ^ mask) == iota((128, 128), 1)).astype(F32).astype(BF16)
        part = jnp.dot(jnp.where(which == h, picked, 0.0).astype(BF16), turn, preferred_element_type=F32)
        chosen[...] = part if h == 0 else chosen[...] + part
    for axis in range(3):
        for d in range(4):
            for half in range(2):
                lanes = slice(half * 128, half * 128 + 128)
                v = (INNER * 0.5) * row[axis : axis + 1, lanes] - d - (INNER * 0.5) * column[axis]
                squares[axis * 4 + d, :, lanes] = v * v + (SOFTEN if axis == 2 else 0.0)
    matrices[...] = jnp.zeros_like(matrices)
    total[...] = jnp.zeros_like(total)
    for key, members in far_groups().items():
        ranges = [range(4) if every else (0, 2) for every in key]
        leaves = [(x, y, z) for x in ranges[0] for y in ranges[1] for z in ranges[2]]
        for n, (a, b, c) in enumerate(members):
            m = lax.rsqrt(squares[a] + squares[4 + b] + squares[8 + c])
            matrices[n * WIDE : n * WIDE + SPAD, :] = m.astype(BF16)
            flag = chosen[(a * 16 + b * 4 + c) * 8 : (a * 16 + b * 4 + c) * 8 + 8, :]
            for i in range(0, len(leaves), 2):
                tiles = []
                for x, y, z in leaves[i : i + 2]:
                    at = (((x + 2 + a) * 8 + y + 2 + b) * 8 + z + 2 + c) * 8
                    leaf = x * 16 + y * 4 + z
                    keep = jnp.broadcast_to(flag[:, leaf : leaf + 1], (8, 128))
                    tiles.append([framed[half, at : at + 8, :] * keep for half in range(2)])
                for half in range(2):
                    lanes = slice(n * WIDE + half * 128, n * WIDE + half * 128 + 128)
                    stacked[i * 8 : i * 8 + 16, lanes] = jnp.concatenate([t[half] for t in tiles], axis=0).astype(BF16)
        rows, depth = len(leaves) * 8, len(members) * WIDE
        product = jnp.dot(stacked[0:rows, 0:depth], matrices[0:depth, :], preferred_element_type=F32)
        for i, (x, y, z) in enumerate(leaves):
            leaf = x * 16 + y * 4 + z
            for half in range(2):
                total[half, leaf * 8 : leaf * 8 + 8, :] += product[i * 8 : i * 8 + 8, half * 128 : half * 128 + 128]
    result = jnp.zeros((64, WIDE), F32)
    for h in range(8):
        parts = [total.at[half][pl.ds(h, 64, stride=8), :] for half in range(2)]
        hi, lo = split2(jnp.concatenate(parts, axis=1))
        both = jnp.dot(jnp.concatenate([hi, lo], axis=0), permutation(h), preferred_element_type=F32).astype(BF16)
        mask = (48 if h & 4 else 0) + (12 if h & 2 else 0) + (3 if h & 1 else 0)
        turn = ((iota((64, 128), 0) ^ mask) == (iota((64, 128), 1) & 63)).astype(F32).astype(BF16)
        result = result + jnp.dot(turn, both, preferred_element_type=F32)
    out[...] = result


def near_kernel(first, planes, *refs):
    *halo, flags, out, lines, sources, points, shifted, sums = refs
    refs = (halo[0:4], *halo[4:])
    if len(halo) == 6:
        refs = (*refs, None, None)
    z1, z2 = halo[1], halo[2]
    count = (planes + 2) * 6
    for x in range(planes + 2):
        for y in range(6):
            for pair in range(4):
                record = particle_record(refs, x + first - 1, y - 1, pair)
                for c in range(4):
                    lines[c, x * 6 + y : x * 6 + y + 1, pair * 128 : pair * 128 + 128] = record[c : c + 1]
    for c in range(4):
        whole = lines[c]
        half_turn = pltpu.roll(whole, 64, 1)
        for e, (line, at) in enumerate(((half_turn, 128), (whole, 128), (half_turn, 256))):
            if c == 2:
                line = line + float(e - 1)
            for half in range(2):
                lanes = slice(at + half * 128, at + half * 128 + 128)
                sources.at[c, half][pl.ds(e, count, stride=3), :] = line[0:count, lanes]
    same = (iota((64, WIDE), 1) & 63) == iota((64, WIDE), 0)
    block = ((iota((WIDE, WIDE), 0) >> 6) == (iota((WIDE, WIDE), 1) >> 6)).astype(F32).astype(BF16)
    zone = iota((32, WIDE), 1) >> 6
    step_y = (iota((9, WIDE), 0) // 3 - 1).astype(F32)
    for i in range(planes * 4):
        r = first * 4 + i
        x, y = i // 4, i % 4
        pieces = []
        for c in range(3):
            v = jnp.concatenate([z1[16 + r, c : c + 1, :], z2[16 + r, c : c + 1, :]], axis=1)
            for _ in range(3):
                b = v.astype(BF16).astype(F32)
                pieces.append(jnp.where(same, b, 0.0).astype(BF16))
                v = v - b
        spread = jnp.dot(jnp.concatenate(pieces, axis=0), block, preferred_element_type=F32)
        square = jnp.full((64, WIDE), SOFTEN, F32)
        for c in range(3):
            at = c * 192
            v = spread[at : at + 64] + spread[at + 64 : at + 128] + spread[at + 128 : at + 192]
            square = square + v * v
            points[i, c] = -2.0 * v
        points[i, 3] = square
        f = flags[x + first, y]
        lists = jnp.zeros((32, WIDE), F32)
        for z in range(4):
            lists = jnp.where(zone == z, f[:, z : z + 1], lists)
        for ex in range(3):
            at = ((x + ex) * 6 + y) * 3
            here = slice(ex * 9, ex * 9 + 9)
            sx, sy, sz, q = (
                jnp.concatenate([sources[c, half, at : at + 9, :] for half in range(2)], axis=1) for c in range(4)
            )
            sx = sx + float(ex - 1)
            sy = sy + step_y
            shifted[i, 0, here, :] = sx
            shifted[i, 1, here, :] = sy
            shifted[i, 2, here, :] = sz
            shifted[i, 3, here, :] = sx * sx + sy * sy + sz * sz
            shifted[i, 4, here, :] = q * lists[here]

    def one_row(i, carry):
        for half in range(2):
            lanes = slice(half * 128, half * 128 + 128)
            tx, ty, tz, tt = (points[i, c, :, lanes] for c in range(4))
            acc = jnp.zeros((64, 128), F32)
            for n in range(27):
                sx, sy, sz, ss, q = (shifted[i, c, n : n + 1, lanes] for c in range(5))
                k = lax.rsqrt((tt + ss) + tx * sx + ty * sy + tz * sz)
                if n == 13:
                    k = jnp.where(same[:, lanes], 0.0, k)
                acc = acc + k * q
            sums[i, :, lanes] = acc
        return carry

    lax.fori_loop(0, planes * 4, one_row, 0)
    for i in range(planes * 4):
        hi, lo = split2(sums[i])
        both = jnp.dot(jnp.concatenate([hi, lo], axis=0), block, preferred_element_type=F32)
        picked = jnp.where(same, both[0:64] + both[64:128], 0.0)
        out[i : i + 1, :] = jnp.sum(picked, axis=0, keepdims=True)


def last_kernel(
    counts, gathered, far, near0, near12, near3, pos, down, column, row, tail, nodes,
    out, operator, squares, offsets, tails, acc, checks, ends,
):
    padded_operator(down, operator)
    flipped = operator[...].T
    segment = iota((1, 128), 1) >> 5
    at = 0
    for axis, ring in enumerate((RING8, RING4, RING8)):
        outer = (INNER * HALF) * column[axis]
        base = outer - (INNER * HALF) * row[axis : axis + 1, 0:128]
        end = outer - (INNER * HALF) * tail[axis : axis + 1, :]
        soft = SOFTEN if axis == 2 else 0.0
        for i, delta in enumerate(ring):
            v = base - float(delta * 4)
            offsets[at + i] = v * v + soft
            if axis < 2:
                v = end - float(delta * 4)
                tails[at + i] = v * v
            elif i % 4 == 0:
                d = ring[i : i + 4]
                shift = jnp.where(
                    segment < 2, jnp.where(segment == 0, d[0], d[1]), jnp.where(segment == 2, d[2], d[3])
                ).astype(F32)
                v = end - 4.0 * shift
                tails[at + i // 4] = v * v + soft
        at += len(ring)
    acc[...] = jnp.zeros_like(acc)

    def pair(i, carry):
        x, y = i >> 2, i & 3
        lines, ends = [], [jnp.zeros((1, 128), F32)] * 2
        for z in range(8):
            m = i * 8 + z
            both = gathered[m] * jnp.where(m == SELF, 0.0, 1.0)
            lines.append(both[0:1])
            end = both[1:2]
            ends[z // 4] = ends[z // 4] + (pltpu.roll(end, 32 * (z % 4), 1) if z % 4 else end)
        for part in range(4):
            rows = slice(part * 40, part * 40 + 40)
            xy = offsets[x, rows, :] + offsets[8 + y, rows, :]
            total = acc[rows, 0:128]
            for z in range(8):
                total = total + lax.rsqrt(xy + offsets[12 + z, rows, :]) * lines[z]
            acc[rows, 0:128] = total
            xy = tails[x, rows, :] + tails[8 + y, rows, :]
            total = acc[rows, 128:256]
            for z in range(2):
                total = total + lax.rsqrt(xy + tails[12 + z, rows, :]) * ends[z]
            acc[rows, 128:256] = total
        return carry

    lax.fori_loop(0, 32, pair, 0)
    weight = BREADTH * jnp.sum(acc[0:SPAD, 0:128] + acc[0:SPAD, 128:256], axis=1, keepdims=True)
    line = jnp.sum(flipped[0:SPAD] * weight, axis=0, keepdims=True)
    local = jnp.broadcast_to(line, (128, WIDE)).T
    leaf_squares(column, row, tail, squares)
    checks[...] = jnp.zeros_like(checks)
    for x in range(4):
        for y in range(4):
            lines = [jnp.zeros((8, 128), F32)] * 5
            for part in range(4):
                rows = slice(part * 40, part * 40 + 40)
                weight = local[rows, 0:128]
                for z in range(5):
                    lanes = slice(0, 128) if z < 4 else slice(128, 256)
                    if z % 4 == 0:
                        xy = squares[x, rows, lanes] + squares[4 + y, rows, lanes]
                    v = lax.rsqrt(xy + squares[8 + z % 4, rows, lanes]) * weight
                    for s in range(5):
                        lines[z] = lines[z] + v[s * 8 : s * 8 + 8]
            for z in range(4):
                t = x * 16 + y * 4 + z
                checks[0, t : t + 1, :] = jnp.sum(lines[z], axis=0, keepdims=True)
            r = x * 4 + y
            ends[r : r + 1, :] = jnp.sum(lines[4], axis=0, keepdims=True)
    used = iota((16, 128), 1) < SURF - 128
    for z in range(4):
        part = pltpu.roll(ends[...], 128 - 32 * z, 1) if z else ends[...]
        checks.at[1][pl.ds(z, 16, stride=4), :] = jnp.where(used, part, 0.0)
    both = jnp.concatenate([checks[0], checks[1]], axis=1)
    local = jnp.dot(both[0:64] + far[...], flipped, precision=HIGHEST, preferred_element_type=F32)
    local = jnp.concatenate([local, jnp.zeros((64, WIDE), F32)], axis=0).T
    hi, lo = split2(local[0:SPAD])
    both = jnp.concatenate([hi, lo], axis=0)
    for x in range(4):
        for y in range(4):
            r = x * 4 + y
            spread = (iota((128, WIDE), 0) == r * 4 + (iota((128, WIDE), 1) >> 6)).astype(F32).astype(BF16)
            wide = jnp.dot(both, spread, preferred_element_type=F32)
            px, py, pz = (pos[c, x, y : y + 1, :] for c in range(3))
            k = surface_terms(px, py, pz, nodes[...])
            line = jnp.sum(k * (wide[0:SPAD] + wide[SPAD : 2 * SPAD]), axis=0, keepdims=True)
            near, i = (near0, r) if x == 0 else (near3, r - 12) if x == 3 else (near12, r - 4)
            out[x, y : y + 1, :] = occupied_row(counts, x, y) * (line + near[i : i + 1, :])


def call(body, outs, scratch, memory, name, work, *args, vmem=40):
    spaces = {"v": pltpu.VMEM, "s": pltpu.SMEM}
    return pl.pallas_call(
        body,
        out_shape=[jax.ShapeDtypeStruct(s, F32) for s in outs],
        in_specs=[pl.BlockSpec(memory_space=spaces[m]) for m in memory],
        out_specs=[pl.BlockSpec(memory_space=pltpu.VMEM) for _ in outs],
        scratch_shapes=[pltpu.VMEM(s, d) for s, d in scratch],
        compiler_params=pltpu.CompilerParams(vmem_limit_bytes=vmem << 20),
        cost_estimate=pl.CostEstimate(flops=work * 1000000, transcendentals=0, bytes_accessed=1 << 20),
        name=name,
    )(*args)


def shifted(array, axis, distance):
    n = lax.axis_size(axis)
    return lax.ppermute(array, axis, [((i + distance) % n, i) for i in range(n)])


def body(positions, charges, counts, near_flags, far_flags, up_operator, down_operator):
    column, row, tail, nodes, mirror, pick = (jnp.asarray(t) for t in tables())
    below, above = call(
        upward_kernel,
        [(33, 4, 128), (33, 4, 128)],
        [
            ((2 * SPAD, 16 * WIDE), BF16), ((WIDE, WIDE), F32), ((12, SPAD, WIDE), F32),
            ((1, 64, 128), F32),
        ],
        "vvsvvvvv", "upward", 6000, positions, charges, counts, up_operator, column, row, tail, nodes, vmem=59,
    )
    own = (shifted(above, "gz", -1), below, above, shifted(below, "gz", 1))

    grid = [[v[k * 16 : k * 16 + 16].reshape(4, 4, 4, 128) for v in own] for k in range(2)]
    blocks = [own[n][32:33] for n in (0, 1, 3)]

    def to_y(low, one):
        parts = [v[:, low : low + 2].reshape(8, 4, 128) for v in grid[0]]
        parts += [v[:, one].reshape(4, 4, 128) for v in grid[1]]
        return jnp.concatenate(parts + blocks, axis=0)

    up, down, far_flags, near_flags = lax.optimization_barrier((to_y(2, 3), to_y(0, 0), far_flags, near_flags))
    ylo = shifted(up, "gy", -1)
    yhi = shifted(down, "gy", 1)
    blocks = jnp.concatenate([ylo[48:51]] + blocks + [yhi[48:51]], axis=0)

    def to_x(low, one):
        parts = []
        for s in range(4):
            sides = [v[s * 8 : s * 8 + 8].reshape(4, 2, 4, 128)[low : low + 2] for v in (ylo, yhi)]
            parts.append(jnp.concatenate([sides[0], grid[0][s][low : low + 2], sides[1]], axis=1).reshape(16, 4, 128))
        for s in range(4):
            at = 32 + s * 4 + one
            parts += [ylo[at : at + 1], grid[1][s][one], yhi[at : at + 1]]
        return jnp.concatenate(parts + [blocks], axis=0)

    up, down = lax.optimization_barrier((to_x(2, 3), to_x(0, 0)))
    xlo = shifted(up, "gx", -1)
    xhi = shifted(down, "gx", 1)
    halo = (*own, ylo, yhi, xlo, xhi)

    held = jnp.concatenate([xlo[88:97], blocks, xhi[88:97]], axis=0)[:, 0:2]
    held = jnp.concatenate([held, shifted(held, "gx", 3), shifted(held[9:27], "gx", -3)], axis=0)
    held = held.reshape(8, 3, 3, 2, 128)
    held = jnp.concatenate([held, shifted(held[:, 1], "gy", 2)[:, None]], axis=1)
    forward, back = shifted(held, "gz", 3), shifted(held[:, :, 1:3], "gz", -3)
    gathered = jnp.concatenate([held, forward, back], axis=2).reshape(256, 2, 128)

    flags = jnp.pad(far_flags.reshape(CLASSES, 64).astype(BF16), ((0, 384 - CLASSES), (0, 64)))
    (far,) = call(
        far_kernel,
        [(64, WIDE)],
        [
            ((2, 512, 128), F32),
            ((512, WIDE), BF16), ((512, WIDE), BF16), ((2, 4096, 128), F32), ((512, 128), F32),
            ((12, SPAD, WIDE), F32), ((512, 8 * WIDE), BF16), ((8 * WIDE, WIDE), BF16), ((2, 512, 128), F32),
        ],
        "v" * 13, "far", 7000, *halo, flags, pick, mirror, column, row,
    )
    near_flags = near_flags.astype(F32)
    centre = jnp.ones((1, *near_flags.shape[1:]), F32)
    listed = jnp.concatenate([near_flags[0:13], centre, near_flags[13:26], jnp.zeros((5, *near_flags.shape[1:]), F32)], axis=0)
    listed = listed.transpose(1, 2, 0, 3)

    def near(first, planes, halo):
        count = (planes + 2) * 6
        (result,) = call(
            functools.partial(near_kernel, first, planes),
            [(planes * 4, WIDE)],
            [
                ((4, count + -count % 8, 512), F32), ((4, 2, count * 3, 128), F32), ((planes * 4, 4, 64, WIDE), F32),
                ((planes * 4, 5, 32, WIDE), F32), ((planes * 4, 64, WIDE), F32),
            ],
            "v" * (len(halo) + 1), "near", 3000 * planes, *halo, listed,
        )
        return result

    inner, low, high = near(1, 2, halo[0:6]), near(0, 1, halo), near(3, 1, halo)
    (potential,) = call(
        last_kernel,
        [(4, 4, WIDE)],
        [
            ((WIDE, WIDE), F32), ((12, SPAD, WIDE), F32), ((20, SPAD, 128), F32), ((14, SPAD, 128), F32),
            ((WIDE, WIDE), F32), ((2, 128, 128), F32), ((16, 128), F32),
        ],
        "svvvvvvvvvvv", "last", 9000, counts, gathered, far, low, inner, high, positions, down_operator, column, row, tail, nodes,
    )
    return potential


def solution(mesh):
    return jax.shard_map(
        body,
        mesh=mesh,
        in_specs=(
            P(None, "gx", "gy", "gz"),
            P("gx", "gy", "gz"),
            P("gx", "gy", "gz"),
            P(None, "gx", "gy", "gz"),
            P(None, "gx", "gy", "gz"),
            P(),
            P(),
        ),
        out_specs=P("gx", "gy", "gz"),
        check_vma=False,
    )
```

```python
import functools

import jax
import jax.numpy as jnp
import ml_dtypes
import numpy as np
from jax import lax
from jax.experimental import pallas as pl
from jax.experimental.pallas import tpu as pltpu
from jax.sharding import PartitionSpec as P

ORDER = 6
SURF = 152
SPAD = 160
WIDE = 256
LEAVES = 4
SLOTS = 64
CLASSES = 343
INNER = 1.05
OUTER = 2.95
SOFTEN = 0.01
HALF = 2.0
BREADTH = 4.0
HIGHEST = lax.Precision.HIGHEST
F32 = jnp.float32
BF16 = jnp.bfloat16
RING8 = (-1, 0, 1, 2, 3, -4, -3, -2)
RING4 = (-1, 0, 1, -2)
SELF = (1 * 4 + 1) * 8 + 1


def surface_points():
    points = []
    for i in range(ORDER):
        for j in range(ORDER):
            for k in range(ORDER):
                if min(i, j, k) == 0 or max(i, j, k) == ORDER - 1:
                    points.append((i, j, k))
    return points


def tables():
    points = surface_points()
    spacing = np.linspace(-1.0, 1.0, ORDER)
    g = np.array([[spacing[i] for i in p] for p in points], dtype=np.float32)
    column = np.zeros((3, SPAD, 128), np.float32)
    column[:, :SURF, :] = g.T[:, :, None]
    row = np.zeros((8, WIDE), np.float32)
    row[:3, :SURF] = g.T
    tail = np.tile(row[:, 128:160], (1, 4))
    nodes = np.zeros((SPAD, 128), np.float32)
    for n, p in enumerate(points + [points[0]] * (SPAD - SURF)):
        for part in range(3):
            for axis in range(3):
                nodes[n, part * 24 + axis * 8 + p[axis]] = 1.0
    where = {p: n for n, p in enumerate(points)}
    mirror = np.full((8, WIDE), -1, np.int32)
    for h in range(8):
        sign = (h >> 2 & 1, h >> 1 & 1, h & 1)
        for n, p in enumerate(points):
            mirror[h, n] = where[tuple(ORDER - 1 - c if f else c for c, f in zip(p, sign))]
    pick = np.zeros((64 * 8, 384), np.float32)
    for a in range(4):
        for b in range(4):
            for c in range(4):
                if max(a, b, c) < 2:
                    continue
                for h in range(8):
                    d = [-v if f else v for v, f in zip((a, b, c), (h >> 2 & 1, h >> 1 & 1, h & 1))]
                    number = (d[0] + 3) * 49 + (d[1] + 3) * 7 + d[2] + 3
                    pick[(a * 16 + b * 4 + c) * 8 + h, number] = 1.0
    return column, row, tail, nodes.astype(ml_dtypes.bfloat16), mirror, pick.astype(ml_dtypes.bfloat16)


def iota(shape, dim):
    return lax.broadcasted_iota(jnp.int32, shape, dim)


def split2(v):
    hi = v.astype(BF16)
    return hi, (v - hi.astype(F32)).astype(BF16)


def surface_terms(px, py, pz, nodes):
    step = iota((8, WIDE), 0).astype(F32) * (OUTER / (ORDER - 1)) - OUTER * 0.5
    parts = []
    for n, p in enumerate((px, py, pz)):
        d = step - p
        parts.append(d * d + (SOFTEN if n == 2 else 0.0))
    rest = jnp.concatenate(parts, axis=0)
    parts = []
    for _ in range(3):
        b = rest.astype(BF16).astype(F32)
        parts.append(b)
        rest = rest - b
    parts.append(jnp.zeros((128 - 72, WIDE), F32))
    squares = jnp.concatenate(parts, axis=0).astype(BF16)
    return lax.rsqrt(jnp.dot(nodes, squares, preferred_element_type=F32))


def occupied_row(counts, x, y):
    lane = iota((1, WIDE), 1)
    zone = lane >> 6
    n = jnp.where(
        zone < 2,
        jnp.where(zone == 0, counts[x, y, 0], counts[x, y, 1]),
        jnp.where(zone == 2, counts[x, y, 2], counts[x, y, 3]),
    )
    return ((lane & 63) < n).astype(F32)


def padded_operator(ref, out):
    out[...] = jnp.zeros_like(out)
    out[0:SURF, 0:SURF] = ref[...]


def leaf_squares(column, row, tail, squares):
    segment = (iota((1, 128), 1) >> 5).astype(F32)
    for axis in range(3):
        outer = (OUTER * HALF) * column[axis]
        inner = (INNER * 0.5) * row[axis : axis + 1, 0:128]
        last = (INNER * 0.5) * tail[axis : axis + 1, :]
        soft = SOFTEN if axis == 2 else 0.0
        for t in range(LEAVES):
            d = outer - ((t - 1.5) + inner)
            squares[axis * LEAVES + t, :, 0:128] = d * d + soft
            if axis < 2:
                d = outer - ((t - 1.5) + last)
                squares[axis * LEAVES + t, :, 128:256] = d * d
            elif t == 0:
                d = outer - ((segment - 1.5) + last)
                squares[axis * LEAVES, :, 128:256] = d * d + soft


def upward_kernel(
    pos, chg, counts, up, column, row, tail, nodes,
    below, above,
    terms, operator, squares, leaves,
):
    padded_operator(up, operator)
    flipped = operator[...].T
    leaf_squares(column, row, tail, squares)
    for x in range(4):
        for y in range(4):
            r = x * 4 + y
            q = chg[x, y : y + 1, :] * occupied_row(counts, x, y)
            px, py, pz = (pos[c, x, y : y + 1, :] for c in range(3))
            k = surface_terms(px, py, pz, nodes[...]) * q
            hi, lo = split2(k)
            terms[0:SPAD, r * WIDE : (r + 1) * WIDE] = hi
            terms[SPAD : 2 * SPAD, r * WIDE : (r + 1) * WIDE] = lo
            for c, v in enumerate((px, py, pz, q)):
                below[16 + r, c : c + 1, :] = v[:, 0:128]
                above[16 + r, c : c + 1, :] = v[:, 128:256]
    gather = ((iota((16 * WIDE, 128), 0) >> 6) == iota((16 * WIDE, 128), 1)).astype(F32).astype(BF16)
    both = jnp.dot(terms[...], gather, preferred_element_type=F32)
    check = both[0:SPAD] + both[SPAD : 2 * SPAD]
    check = jnp.concatenate([check, jnp.zeros((WIDE - SPAD, 128), F32)], axis=0).T[0:64, :]
    up_eq = jnp.dot(check, flipped, precision=HIGHEST, preferred_element_type=F32)
    low = up_eq.astype(BF16).astype(F32)
    for r in range(16):
        for out, at in ((below, 0), (above, 2)):
            pair = low[r * 4 + at : r * 4 + at + 2]
            out[r, 0:2, :] = pair[:, 0:128]
            out[r, 2:4, :] = pair[:, 128:256]
    leaves[0] = up_eq[:, 128:256]
    lines = leaves.at[0][pl.ds(0, 16, stride=4), :]
    for z in range(1, 4):
        lines = lines + pltpu.roll(leaves.at[0][pl.ds(z, 16, stride=4), :], 32 * z, 1)
    block = jnp.zeros((8, WIDE), F32)
    for part in range(4):
        rows = slice(part * 40, part * 40 + 40)
        first, last = jnp.zeros((40, 128), F32), jnp.zeros((40, 128), F32)
        for x in range(4):
            for y in range(4):
                xy = squares[x, rows, 0:128] + squares[4 + y, rows, 0:128]
                for z in range(4):
                    t = x * 16 + y * 4 + z
                    first = first + lax.rsqrt(xy + squares[8 + z, rows, 0:128]) * up_eq[t : t + 1, 0:128]
                xy = squares[x, rows, 128:256] + squares[4 + y, rows, 128:256]
                r = x * 4 + y
                last = last + lax.rsqrt(xy + squares[8, rows, 128:256]) * lines[r : r + 1, :]
        weight = BREADTH * jnp.sum(first + last, axis=1, keepdims=True)
        for n in range(part * 40, part * 40 + 40, 8):
            block = block + flipped[n : n + 8] * weight[n - part * 40 : n - part * 40 + 8]
    block = jnp.sum(block, axis=0, keepdims=True)
    for out in (below, above):
        out[32, 0:1, :] = block[0:1, 0:128]
        out[32, 1:2, :] = block[0:1, 128:256]
        out[32, 2:4, :] = jnp.zeros((2, 128), F32)


def eq_record(refs, x, y, s):
    own, ylo, yhi, xlo, xhi = refs
    if x < 2:
        return xlo[(s * 2 + x) * 8 + y]
    if x > 5:
        return xhi[(s * 2 + x - 6) * 8 + y]
    if y < 2:
        return ylo[s * 8 + (x - 2) * 2 + y]
    if y > 5:
        return yhi[s * 8 + (x - 2) * 2 + y - 6]
    return own[s][(x - 2) * 4 + y - 2]


def particle_record(refs, x, y, s):
    own, ylo, yhi, xlo, xhi = refs
    if x < 0:
        return xlo[64 + s * 6 + y + 1]
    if x > 3:
        return xhi[64 + s * 6 + y + 1]
    if y < 0:
        return ylo[32 + s * 4 + x]
    if y > 3:
        return yhi[32 + s * 4 + x]
    return own[s][16 + x * 4 + y]


def far_groups():
    groups = {}
    for a in range(4):
        for b in range(4):
            for c in range(4):
                if max(a, b, c) >= 2:
                    key = tuple(v in (1, 2) for v in (a, b, c))
                    groups.setdefault(key, []).append((a, b, c))
    return groups


def far_kernel(
    z0, z1, z2, z3, ylo, yhi, xlo, xhi, flags, pick, mirror, column, row,
    out, halo, low, turned, framed, chosen, squares, stacked, matrices, total,
):
    refs = ((z0, z1, z2, z3), ylo, yhi, xlo, xhi)
    for x in range(8):
        for y in range(8):
            for pair in range(4):
                record = eq_record(refs, x, y, pair)
                at = (x * 8 + y) * 8 + pair * 2
                halo[0, at : at + 2, :] = record[0:2]
                halo[1, at : at + 2, :] = record[2:4]
    for half in range(2):
        low[:, half * 128 : half * 128 + 128] = halo[half].astype(BF16)
    turn = ((iota((WIDE, WIDE), 0) ^ 7) == iota((WIDE, WIDE), 1)).astype(F32).astype(BF16)
    for n in range(2):
        part = slice(n * WIDE, n * WIDE + WIDE)
        turned[part, :] = jnp.dot(turn, low[part, :], preferred_element_type=F32).astype(BF16)

    def permutation(h):
        return (iota((WIDE, WIDE), 0) == mirror[h : h + 1, :]).astype(F32).astype(BF16)

    for h in range(8):
        source = turned if h & 1 else low
        frame = jnp.dot(source[...], permutation(h), preferred_element_type=F32)
        for x in range(8):
            for y in range(8):
                xf, yf = (7 - x if h & 4 else x), (7 - y if h & 2 else y)
                at = (x * 8 + y) * 8
                for n in range(2):
                    framed.at[n][pl.ds((xf * 8 + yf) * 64 + h, 8, stride=8), :] = frame[
                        at : at + 8, n * 128 : n * 128 + 128
                    ]
    picked = jnp.dot(pick[...], flags[...], preferred_element_type=F32)
    which = iota((512, 128), 0) & 7
    for h in range(8):
        mask = (48 if h & 4 else 0) + (12 if h & 2 else 0) + (3 if h & 1 else 0)
        turn = ((iota((128, 128), 0) ^ mask) == iota((128, 128), 1)).astype(F32).astype(BF16)
        part = jnp.dot(jnp.where(which == h, picked, 0.0).astype(BF16), turn, preferred_element_type=F32)
        chosen[...] = part if h == 0 else chosen[...] + part
    for axis in range(3):
        for d in range(4):
            for half in range(2):
                lanes = slice(half * 128, half * 128 + 128)
                v = (INNER * 0.5) * row[axis : axis + 1, lanes] - d - (INNER * 0.5) * column[axis]
                squares[axis * 4 + d, :, lanes] = v * v + (SOFTEN if axis == 2 else 0.0)
    matrices[...] = jnp.zeros_like(matrices)
    total[...] = jnp.zeros_like(total)
    for key, members in far_groups().items():
        ranges = [range(4) if every else (0, 2) for every in key]
        leaves = [(x, y, z) for x in ranges[0] for y in ranges[1] for z in ranges[2]]
        for n, (a, b, c) in enumerate(members):
            m = lax.rsqrt(squares[a] + squares[4 + b] + squares[8 + c])
            matrices[n * WIDE : n * WIDE + SPAD, :] = m.astype(BF16)
            flag = chosen[(a * 16 + b * 4 + c) * 8 : (a * 16 + b * 4 + c) * 8 + 8, :]
            for i in range(0, len(leaves), 2):
                tiles = []
                for x, y, z in leaves[i : i + 2]:
                    at = (((x + 2 + a) * 8 + y + 2 + b) * 8 + z + 2 + c) * 8
                    leaf = x * 16 + y * 4 + z
                    keep = jnp.broadcast_to(flag[:, leaf : leaf + 1], (8, 128))
                    tiles.append([framed[half, at : at + 8, :] * keep for half in range(2)])
                for half in range(2):
                    lanes = slice(n * WIDE + half * 128, n * WIDE + half * 128 + 128)
                    stacked[i * 8 : i * 8 + 16, lanes] = jnp.concatenate([t[half] for t in tiles], axis=0).astype(BF16)
        rows, depth = len(leaves) * 8, len(members) * WIDE
        product = jnp.dot(stacked[0:rows, 0:depth], matrices[0:depth, :], preferred_element_type=F32)
        for i, (x, y, z) in enumerate(leaves):
            leaf = x * 16 + y * 4 + z
            for half in range(2):
                total[half, leaf * 8 : leaf * 8 + 8, :] += product[i * 8 : i * 8 + 8, half * 128 : half * 128 + 128]
    result = jnp.zeros((64, WIDE), F32)
    for h in range(8):
        parts = [total.at[half][pl.ds(h, 64, stride=8), :] for half in range(2)]
        hi, lo = split2(jnp.concatenate(parts, axis=1))
        both = jnp.dot(jnp.concatenate([hi, lo], axis=0), permutation(h), preferred_element_type=F32).astype(BF16)
        mask = (48 if h & 4 else 0) + (12 if h & 2 else 0) + (3 if h & 1 else 0)
        turn = ((iota((64, 128), 0) ^ mask) == (iota((64, 128), 1) & 63)).astype(F32).astype(BF16)
        result = result + jnp.dot(turn, both, preferred_element_type=F32)
    out[...] = result


def near_kernel(planes, first_x, count_x, *refs):
    *halo, flags, out, lines, sources, points, shifted, sums = refs
    refs = (halo[0:4], *halo[4:])
    if len(halo) == 6:
        refs = (*refs, None, None)
    z1, z2 = halo[1], halo[2]
    targets = [(x, y) for x in planes for y in range(4)]
    count = count_x * 6
    for x in range(count_x):
        for y in range(6):
            for pair in range(4):
                record = particle_record(refs, x + first_x, y - 1, pair)
                for c in range(4):
                    lines[c, x * 6 + y : x * 6 + y + 1, pair * 128 : pair * 128 + 128] = record[c : c + 1]
    for c in range(4):
        whole = lines[c]
        half_turn = pltpu.roll(whole, 64, 1)
        for e, (line, at) in enumerate(((half_turn, 128), (whole, 128), (half_turn, 256))):
            if c == 2:
                line = line + float(e - 1)
            for half in range(2):
                lanes = slice(at + half * 128, at + half * 128 + 128)
                sources.at[c, half][pl.ds(e, count, stride=3), :] = line[0:count, lanes]
    same = (iota((64, WIDE), 1) & 63) == iota((64, WIDE), 0)
    block = ((iota((WIDE, WIDE), 0) >> 6) == (iota((WIDE, WIDE), 1) >> 6)).astype(F32).astype(BF16)
    zone = iota((32, WIDE), 1) >> 6
    step_y = (iota((9, WIDE), 0) // 3 - 1).astype(F32)
    for i, (x, y) in enumerate(targets):
        r = x * 4 + y
        pieces = []
        for c in range(3):
            v = jnp.concatenate([z1[16 + r, c : c + 1, :], z2[16 + r, c : c + 1, :]], axis=1)
            for _ in range(3):
                b = v.astype(BF16).astype(F32)
                pieces.append(jnp.where(same, b, 0.0).astype(BF16))
                v = v - b
        spread = jnp.dot(jnp.concatenate(pieces, axis=0), block, preferred_element_type=F32)
        square = jnp.full((64, WIDE), SOFTEN, F32)
        for c in range(3):
            at = c * 192
            v = spread[at : at + 64] + spread[at + 64 : at + 128] + spread[at + 128 : at + 192]
            square = square + v * v
            points[i, c] = -2.0 * v
        points[i, 3] = square
        f = flags[x, y]
        lists = jnp.zeros((32, WIDE), F32)
        for z in range(4):
            lists = jnp.where(zone == z, f[:, z : z + 1], lists)
        for ex in range(3):
            at = ((x - 1 + ex - first_x) * 6 + y) * 3
            here = slice(ex * 9, ex * 9 + 9)
            sx, sy, sz, q = (
                jnp.concatenate([sources[c, half, at : at + 9, :] for half in range(2)], axis=1) for c in range(4)
            )
            sx = sx + float(ex - 1)
            sy = sy + step_y
            shifted[i, 0, here, :] = sx
            shifted[i, 1, here, :] = sy
            shifted[i, 2, here, :] = sz
            shifted[i, 3, here, :] = sx * sx + sy * sy + sz * sz
            shifted[i, 4, here, :] = q * lists[here]

    def one_row(i, carry):
        for half in range(2):
            lanes = slice(half * 128, half * 128 + 128)
            tx, ty, tz, tt = (points[i, c, :, lanes] for c in range(4))
            acc = jnp.zeros((64, 128), F32)
            for n in range(27):
                sx, sy, sz, ss, q = (shifted[i, c, n : n + 1, lanes] for c in range(5))
                k = lax.rsqrt((tt + ss) + tx * sx + ty * sy + tz * sz)
                if n == 13:
                    k = jnp.where(same[:, lanes], 0.0, k)
                acc = acc + k * q
            sums[i, :, lanes] = acc
        return carry

    lax.fori_loop(0, len(targets), one_row, 0)
    for i in range(len(targets)):
        hi, lo = split2(sums[i])
        both = jnp.dot(jnp.concatenate([hi, lo], axis=0), block, preferred_element_type=F32)
        picked = jnp.where(same, both[0:64] + both[64:128], 0.0)
        out[i : i + 1, :] = jnp.sum(picked, axis=0, keepdims=True)


def last_kernel(
    counts, gathered, far, near_in, near_out, pos, down, column, row, tail, nodes,
    out, operator, squares, offsets, tails, acc, checks, ends,
):
    padded_operator(down, operator)
    flipped = operator[...].T
    segment = iota((1, 128), 1) >> 5
    at = 0
    for axis, ring in enumerate((RING8, RING4, RING8)):
        outer = (INNER * HALF) * column[axis]
        base = outer - (INNER * HALF) * row[axis : axis + 1, 0:128]
        end = outer - (INNER * HALF) * tail[axis : axis + 1, :]
        soft = SOFTEN if axis == 2 else 0.0
        for i, delta in enumerate(ring):
            v = base - float(delta * 4)
            offsets[at + i] = v * v + soft
            if axis < 2:
                v = end - float(delta * 4)
                tails[at + i] = v * v
            elif i % 4 == 0:
                d = ring[i : i + 4]
                shift = jnp.where(
                    segment < 2, jnp.where(segment == 0, d[0], d[1]), jnp.where(segment == 2, d[2], d[3])
                ).astype(F32)
                v = end - 4.0 * shift
                tails[at + i // 4] = v * v + soft
        at += len(ring)
    acc[...] = jnp.zeros_like(acc)

    def pair(i, carry):
        x, y = i >> 2, i & 3
        lines, ends = [], [jnp.zeros((1, 128), F32)] * 2
        for z in range(8):
            m = i * 8 + z
            both = gathered[m] * jnp.where(m == SELF, 0.0, 1.0)
            lines.append(both[0:1])
            end = both[1:2]
            ends[z // 4] = ends[z // 4] + (pltpu.roll(end, 32 * (z % 4), 1) if z % 4 else end)
        for part in range(4):
            rows = slice(part * 40, part * 40 + 40)
            xy = offsets[x, rows, :] + offsets[8 + y, rows, :]
            total = acc[rows, 0:128]
            for z in range(8):
                total = total + lax.rsqrt(xy + offsets[12 + z, rows, :]) * lines[z]
            acc[rows, 0:128] = total
            xy = tails[x, rows, :] + tails[8 + y, rows, :]
            total = acc[rows, 128:256]
            for z in range(2):
                total = total + lax.rsqrt(xy + tails[12 + z, rows, :]) * ends[z]
            acc[rows, 128:256] = total
        return carry

    lax.fori_loop(0, 32, pair, 0)
    weight = BREADTH * jnp.sum(acc[0:SPAD, 0:128] + acc[0:SPAD, 128:256], axis=1, keepdims=True)
    line = jnp.sum(flipped[0:SPAD] * weight, axis=0, keepdims=True)
    local = jnp.broadcast_to(line, (128, WIDE)).T
    leaf_squares(column, row, tail, squares)
    checks[...] = jnp.zeros_like(checks)
    for x in range(4):
        for y in range(4):
            lines = [jnp.zeros((8, 128), F32)] * 5
            for part in range(4):
                rows = slice(part * 40, part * 40 + 40)
                weight = local[rows, 0:128]
                for z in range(5):
                    lanes = slice(0, 128) if z < 4 else slice(128, 256)
                    if z % 4 == 0:
                        xy = squares[x, rows, lanes] + squares[4 + y, rows, lanes]
                    v = lax.rsqrt(xy + squares[8 + z % 4, rows, lanes]) * weight
                    for s in range(5):
                        lines[z] = lines[z] + v[s * 8 : s * 8 + 8]
            for z in range(4):
                t = x * 16 + y * 4 + z
                checks[0, t : t + 1, :] = jnp.sum(lines[z], axis=0, keepdims=True)
            r = x * 4 + y
            ends[r : r + 1, :] = jnp.sum(lines[4], axis=0, keepdims=True)
    used = iota((16, 128), 1) < SURF - 128
    for z in range(4):
        part = pltpu.roll(ends[...], 128 - 32 * z, 1) if z else ends[...]
        checks.at[1][pl.ds(z, 16, stride=4), :] = jnp.where(used, part, 0.0)
    both = jnp.concatenate([checks[0], checks[1]], axis=1)
    local = jnp.dot(both[0:64] + far[...], flipped, precision=HIGHEST, preferred_element_type=F32)
    local = jnp.concatenate([local, jnp.zeros((64, WIDE), F32)], axis=0).T
    hi, lo = split2(local[0:SPAD])
    both = jnp.concatenate([hi, lo], axis=0)
    for x in range(4):
        for y in range(4):
            r = x * 4 + y
            spread = (iota((128, WIDE), 0) == r * 4 + (iota((128, WIDE), 1) >> 6)).astype(F32).astype(BF16)
            wide = jnp.dot(both, spread, preferred_element_type=F32)
            px, py, pz = (pos[c, x, y : y + 1, :] for c in range(3))
            k = surface_terms(px, py, pz, nodes[...])
            line = jnp.sum(k * (wide[0:SPAD] + wide[SPAD : 2 * SPAD]), axis=0, keepdims=True)
            near, i = (near_in, r - 4) if x in (1, 2) else (near_out, r % 8)
            out[x, y : y + 1, :] = occupied_row(counts, x, y) * (line + near[i : i + 1, :])


def call(body, outs, scratch, memory, name, work, *args, vmem=40):
    spaces = {"v": pltpu.VMEM, "s": pltpu.SMEM}
    return pl.pallas_call(
        body,
        out_shape=[jax.ShapeDtypeStruct(s, F32) for s in outs],
        in_specs=[pl.BlockSpec(memory_space=spaces[m]) for m in memory],
        out_specs=[pl.BlockSpec(memory_space=pltpu.VMEM) for _ in outs],
        scratch_shapes=[pltpu.VMEM(s, d) for s, d in scratch],
        compiler_params=pltpu.CompilerParams(vmem_limit_bytes=vmem << 20),
        cost_estimate=pl.CostEstimate(flops=work * 1000000, transcendentals=0, bytes_accessed=1 << 20),
        name=name,
    )(*args)


def shifted(array, axis, distance):
    n = lax.axis_size(axis)
    return lax.ppermute(array, axis, [((i + distance) % n, i) for i in range(n)])


def body(positions, charges, counts, near_flags, far_flags, up_operator, down_operator):
    column, row, tail, nodes, mirror, pick = (jnp.asarray(t) for t in tables())
    below, above = call(
        upward_kernel,
        [(33, 4, 128), (33, 4, 128)],
        [
            ((2 * SPAD, 16 * WIDE), BF16), ((WIDE, WIDE), F32), ((12, SPAD, WIDE), F32),
            ((1, 64, 128), F32),
        ],
        "vvsvvvvv", "upward", 6000, positions, charges, counts, up_operator, column, row, tail, nodes, vmem=59,
    )
    own = (shifted(above, "gz", -1), below, above, shifted(below, "gz", 1))

    grid = [[v[k * 16 : k * 16 + 16].reshape(4, 4, 4, 128) for v in own] for k in range(2)]
    blocks = [own[n][32:33] for n in (0, 1, 3)]

    def to_y(low, one):
        parts = [v[:, low : low + 2].reshape(8, 4, 128) for v in grid[0]]
        parts += [v[:, one].reshape(4, 4, 128) for v in grid[1]]
        return jnp.concatenate(parts + blocks, axis=0)

    middle = jnp.concatenate(blocks, axis=0)
    up, down, middle, far_flags, near_flags = lax.optimization_barrier(
        (to_y(2, 3), to_y(0, 0), middle, far_flags, near_flags)
    )
    ylo = shifted(up, "gy", -1)
    yhi = shifted(down, "gy", 1)
    far_blocks = shifted(middle, "gy", 2)
    blocks = jnp.concatenate([ylo[48:51], middle, yhi[48:51], far_blocks], axis=0)

    def to_x(low, one):
        parts = []
        for s in range(4):
            sides = [v[s * 8 : s * 8 + 8].reshape(4, 2, 4, 128)[low : low + 2] for v in (ylo, yhi)]
            parts.append(jnp.concatenate([sides[0], grid[0][s][low : low + 2], sides[1]], axis=1).reshape(16, 4, 128))
        for s in range(4):
            at = 32 + s * 4 + one
            parts += [ylo[at : at + 1], grid[1][s][one], yhi[at : at + 1]]
        return jnp.concatenate(parts + [blocks], axis=0)

    up, down = lax.optimization_barrier((to_x(2, 3), to_x(0, 0)))
    xlo = shifted(up, "gx", -1)
    xhi = shifted(down, "gx", 1)
    halo = (*own, ylo, yhi, xlo, xhi)

    held = jnp.concatenate([xlo[88:100], blocks, xhi[88:100]], axis=0)[:, 0:2]
    held = jnp.concatenate([held, shifted(held, "gx", 3), shifted(held[12:36], "gx", -3)], axis=0)
    held = held.reshape(8, 4, 3, 2, 128)
    forward, back = shifted(held, "gz", 3), shifted(held[:, :, 1:3], "gz", -3)
    gathered = jnp.concatenate([held, forward, back], axis=2).reshape(256, 2, 128)

    flags = jnp.pad(far_flags.reshape(CLASSES, 64).astype(BF16), ((0, 384 - CLASSES), (0, 64)))
    (far,) = call(
        far_kernel,
        [(64, WIDE)],
        [
            ((2, 512, 128), F32),
            ((512, WIDE), BF16), ((512, WIDE), BF16), ((2, 4096, 128), F32), ((512, 128), F32),
            ((12, SPAD, WIDE), F32), ((512, 8 * WIDE), BF16), ((8 * WIDE, WIDE), BF16), ((2, 512, 128), F32),
        ],
        "v" * 13, "far", 7000, *halo, flags, pick, mirror, column, row,
    )
    near_flags = near_flags.astype(F32)
    centre = jnp.ones((1, *near_flags.shape[1:]), F32)
    listed = jnp.concatenate([near_flags[0:13], centre, near_flags[13:26], jnp.zeros((5, *near_flags.shape[1:]), F32)], axis=0)
    listed = listed.transpose(1, 2, 0, 3)

    def near(planes, first_x, count_x, halo):
        count, here = count_x * 6, len(planes) * 4
        (result,) = call(
            functools.partial(near_kernel, planes, first_x, count_x),
            [(here, WIDE)],
            [
                ((4, count + -count % 8, 512), F32), ((4, 2, count * 3, 128), F32), ((here, 4, 64, WIDE), F32),
                ((here, 5, 32, WIDE), F32), ((here, 64, WIDE), F32),
            ],
            "v" * (len(halo) + 1), "near", 6000, *halo, listed,
        )
        return result

    inner, outer = near((1, 2), 0, 4, halo[0:6]), near((0, 3), -1, 6, halo)
    (potential,) = call(
        last_kernel,
        [(4, 4, WIDE)],
        [
            ((WIDE, WIDE), F32), ((12, SPAD, WIDE), F32), ((20, SPAD, 128), F32), ((14, SPAD, 128), F32),
            ((WIDE, WIDE), F32), ((2, 128, 128), F32), ((16, 128), F32),
        ],
        "svvvvvvvvvv", "last", 9000, counts, gathered, far, inner, outer, positions, down_operator, column, row, tail, nodes,
    )
    return potential


def solution(mesh):
    return jax.shard_map(
        body,
        mesh=mesh,
        in_specs=(
            P(None, "gx", "gy", "gz"),
            P("gx", "gy", "gz"),
            P("gx", "gy", "gz"),
            P(None, "gx", "gy", "gz"),
            P(None, "gx", "gy", "gz"),
            P(),
            P(),
        ),
        out_specs=P("gx", "gy", "gz"),
        check_vma=False,
    )
```

```python
import functools

import jax
import jax.numpy as jnp
import ml_dtypes
import numpy as np
from jax import lax
from jax.experimental import pallas as pl
from jax.experimental.pallas import tpu as pltpu
from jax.sharding import PartitionSpec as P

ORDER = 6
SURF = 152
SPAD = 160
WIDE = 256
LEAVES = 4
SLOTS = 64
CLASSES = 343
INNER = 1.05
OUTER = 2.95
SOFTEN = 0.01
HALF = 2.0
BREADTH = 4.0
HIGHEST = lax.Precision.HIGHEST
F32 = jnp.float32
BF16 = jnp.bfloat16
RING8 = (-1, 0, 1, 2, 3, -4, -3, -2)
RING4 = (-1, 0, 1, -2)
SELF = (1 * 4 + 1) * 8 + 1


def surface_points():
    points = []
    for i in range(ORDER):
        for j in range(ORDER):
            for k in range(ORDER):
                if min(i, j, k) == 0 or max(i, j, k) == ORDER - 1:
                    points.append((i, j, k))
    return points


def tables():
    points = surface_points()
    spacing = np.linspace(-1.0, 1.0, ORDER)
    g = np.array([[spacing[i] for i in p] for p in points], dtype=np.float32)
    column = np.zeros((3, SPAD, 128), np.float32)
    column[:, :SURF, :] = g.T[:, :, None]
    row = np.zeros((8, WIDE), np.float32)
    row[:3, :SURF] = g.T
    tail = np.tile(row[:, 128:160], (1, 4))
    nodes = np.zeros((SPAD, 128), np.float32)
    for n, p in enumerate(points + [points[0]] * (SPAD - SURF)):
        for part in range(3):
            for axis in range(3):
                nodes[n, part * 24 + axis * 8 + p[axis]] = 1.0
    where = {p: n for n, p in enumerate(points)}
    mirror = np.full((8, WIDE), -1, np.int32)
    for h in range(8):
        sign = (h >> 2 & 1, h >> 1 & 1, h & 1)
        for n, p in enumerate(points):
            mirror[h, n] = where[tuple(ORDER - 1 - c if f else c for c, f in zip(p, sign))]
    pick = np.zeros((64 * 8, 384), np.float32)
    for a in range(4):
        for b in range(4):
            for c in range(4):
                if max(a, b, c) < 2:
                    continue
                for h in range(8):
                    d = [-v if f else v for v, f in zip((a, b, c), (h >> 2 & 1, h >> 1 & 1, h & 1))]
                    number = (d[0] + 3) * 49 + (d[1] + 3) * 7 + d[2] + 3
                    pick[(a * 16 + b * 4 + c) * 8 + h, number] = 1.0
    return column, row, tail, nodes.astype(ml_dtypes.bfloat16), mirror, pick.astype(ml_dtypes.bfloat16)


def iota(shape, dim):
    return lax.broadcasted_iota(jnp.int32, shape, dim)


def split2(v):
    hi = v.astype(BF16)
    return hi, (v - hi.astype(F32)).astype(BF16)


def surface_terms(px, py, pz, nodes):
    step = iota((8, WIDE), 0).astype(F32) * (OUTER / (ORDER - 1)) - OUTER * 0.5
    parts = []
    for n, p in enumerate((px, py, pz)):
        d = step - p
        parts.append(d * d + (SOFTEN if n == 2 else 0.0))
    rest = jnp.concatenate(parts, axis=0)
    parts = []
    for _ in range(3):
        b = rest.astype(BF16).astype(F32)
        parts.append(b)
        rest = rest - b
    parts.append(jnp.zeros((128 - 72, WIDE), F32))
    squares = jnp.concatenate(parts, axis=0).astype(BF16)
    return lax.rsqrt(jnp.dot(nodes, squares, preferred_element_type=F32))


def occupied_row(counts, x, y):
    lane = iota((1, WIDE), 1)
    zone = lane >> 6
    n = jnp.where(
        zone < 2,
        jnp.where(zone == 0, counts[x, y, 0], counts[x, y, 1]),
        jnp.where(zone == 2, counts[x, y, 2], counts[x, y, 3]),
    )
    return ((lane & 63) < n).astype(F32)


def padded_operator(ref, out):
    out[...] = jnp.zeros_like(out)
    out[0:SURF, 0:SURF] = ref[...]


def leaf_squares(column, row, tail, squares):
    segment = (iota((1, 128), 1) >> 5).astype(F32)
    for axis in range(3):
        outer = (OUTER * HALF) * column[axis]
        inner = (INNER * 0.5) * row[axis : axis + 1, 0:128]
        last = (INNER * 0.5) * tail[axis : axis + 1, :]
        soft = SOFTEN if axis == 2 else 0.0
        for t in range(LEAVES):
            d = outer - ((t - 1.5) + inner)
            squares[axis * LEAVES + t, :, 0:128] = d * d + soft
            if axis < 2:
                d = outer - ((t - 1.5) + last)
                squares[axis * LEAVES + t, :, 128:256] = d * d
            elif t == 0:
                d = outer - ((segment - 1.5) + last)
                squares[axis * LEAVES, :, 128:256] = d * d + soft


def upward_kernel(
    pos, chg, counts, up, column, row, tail, nodes,
    below, above,
    terms, operator, squares, leaves,
):
    padded_operator(up, operator)
    flipped = operator[...].T
    leaf_squares(column, row, tail, squares)
    for x in range(4):
        for y in range(4):
            r = x * 4 + y
            q = chg[x, y : y + 1, :] * occupied_row(counts, x, y)
            px, py, pz = (pos[c, x, y : y + 1, :] for c in range(3))
            k = surface_terms(px, py, pz, nodes[...]) * q
            hi, lo = split2(k)
            terms[0:SPAD, r * WIDE : (r + 1) * WIDE] = hi
            terms[SPAD : 2 * SPAD, r * WIDE : (r + 1) * WIDE] = lo
            for c, v in enumerate((px, py, pz, q)):
                below[16 + r, c : c + 1, :] = v[:, 0:128]
                above[16 + r, c : c + 1, :] = v[:, 128:256]
    gather = ((iota((16 * WIDE, 128), 0) >> 6) == iota((16 * WIDE, 128), 1)).astype(F32).astype(BF16)
    both = jnp.dot(terms[...], gather, preferred_element_type=F32)
    check = both[0:SPAD] + both[SPAD : 2 * SPAD]
    check = jnp.concatenate([check, jnp.zeros((WIDE - SPAD, 128), F32)], axis=0).T[0:64, :]
    up_eq = jnp.dot(check, flipped, precision=HIGHEST, preferred_element_type=F32)
    low = up_eq.astype(BF16).astype(F32)
    for r in range(16):
        for out, at in ((below, 0), (above, 2)):
            pair = low[r * 4 + at : r * 4 + at + 2]
            out[r, 0:2, :] = pair[:, 0:128]
            out[r, 2:4, :] = pair[:, 128:256]
    leaves[0] = up_eq[:, 128:256]
    lines = leaves.at[0][pl.ds(0, 16, stride=4), :]
    for z in range(1, 4):
        lines = lines + pltpu.roll(leaves.at[0][pl.ds(z, 16, stride=4), :], 32 * z, 1)
    block = jnp.zeros((8, WIDE), F32)
    for part in range(4):
        rows = slice(part * 40, part * 40 + 40)
        first, last = jnp.zeros((40, 128), F32), jnp.zeros((40, 128), F32)
        for x in range(4):
            for y in range(4):
                xy = squares[x, rows, 0:128] + squares[4 + y, rows, 0:128]
                for z in range(4):
                    t = x * 16 + y * 4 + z
                    first = first + lax.rsqrt(xy + squares[8 + z, rows, 0:128]) * up_eq[t : t + 1, 0:128]
                xy = squares[x, rows, 128:256] + squares[4 + y, rows, 128:256]
                r = x * 4 + y
                last = last + lax.rsqrt(xy + squares[8, rows, 128:256]) * lines[r : r + 1, :]
        weight = BREADTH * jnp.sum(first + last, axis=1, keepdims=True)
        for n in range(part * 40, part * 40 + 40, 8):
            block = block + flipped[n : n + 8] * weight[n - part * 40 : n - part * 40 + 8]
    block = jnp.sum(block, axis=0, keepdims=True)
    for out in (below, above):
        out[32, 0:1, :] = block[0:1, 0:128]
        out[32, 1:2, :] = block[0:1, 128:256]
        out[32, 2:4, :] = jnp.zeros((2, 128), F32)


def eq_record(refs, x, y, s):
    own, ylo, yhi, xlo, xhi = refs
    if x < 2:
        return xlo[(s * 2 + x) * 8 + y]
    if x > 5:
        return xhi[(s * 2 + x - 6) * 8 + y]
    if y < 2:
        return ylo[s * 8 + (x - 2) * 2 + y]
    if y > 5:
        return yhi[s * 8 + (x - 2) * 2 + y - 6]
    return own[s][(x - 2) * 4 + y - 2]


def particle_record(refs, x, y, s):
    own, ylo, yhi, xlo, xhi = refs
    if x < 0:
        return xlo[64 + s * 6 + y + 1]
    if x > 3:
        return xhi[64 + s * 6 + y + 1]
    if y < 0:
        return ylo[32 + s * 4 + x]
    if y > 3:
        return yhi[32 + s * 4 + x]
    return own[s][16 + x * 4 + y]


def far_groups():
    groups = {}
    for a in range(4):
        for b in range(4):
            for c in range(4):
                if max(a, b, c) >= 2:
                    key = tuple(v in (1, 2) for v in (a, b, c))
                    groups.setdefault(key, []).append((a, b, c))
    return groups


def far_kernel(
    z0, z1, z2, z3, ylo, yhi, xlo, xhi, flags, pick, mirror, column, row,
    out, halo, low, turned, framed, chosen, squares, stacked, matrices, total,
):
    refs = ((z0, z1, z2, z3), ylo, yhi, xlo, xhi)
    for x in range(8):
        for y in range(8):
            for pair in range(4):
                record = eq_record(refs, x, y, pair)
                at = (x * 8 + y) * 8 + pair * 2
                halo[0, at : at + 2, :] = record[0:2]
                halo[1, at : at + 2, :] = record[2:4]
    for half in range(2):
        low[:, half * 128 : half * 128 + 128] = halo[half].astype(BF16)
    turn = ((iota((WIDE, WIDE), 0) ^ 7) == iota((WIDE, WIDE), 1)).astype(F32).astype(BF16)
    for n in range(2):
        part = slice(n * WIDE, n * WIDE + WIDE)
        turned[part, :] = jnp.dot(turn, low[part, :], preferred_element_type=F32).astype(BF16)

    def permutation(h):
        return (iota((WIDE, WIDE), 0) == mirror[h : h + 1, :]).astype(F32).astype(BF16)

    for h in range(8):
        source = turned if h & 1 else low
        frame = jnp.dot(source[...], permutation(h), preferred_element_type=F32)
        for x in range(8):
            for y in range(8):
                xf, yf = (7 - x if h & 4 else x), (7 - y if h & 2 else y)
                at = (x * 8 + y) * 8
                for n in range(2):
                    framed.at[n][pl.ds((xf * 8 + yf) * 64 + h, 8, stride=8), :] = frame[
                        at : at + 8, n * 128 : n * 128 + 128
                    ]
    picked = jnp.dot(pick[...], flags[...], preferred_element_type=F32)
    which = iota((512, 128), 0) & 7
    for h in range(8):
        mask = (48 if h & 4 else 0) + (12 if h & 2 else 0) + (3 if h & 1 else 0)
        turn = ((iota((128, 128), 0) ^ mask) == iota((128, 128), 1)).astype(F32).astype(BF16)
        part = jnp.dot(jnp.where(which == h, picked, 0.0).astype(BF16), turn, preferred_element_type=F32)
        chosen[...] = part if h == 0 else chosen[...] + part
    for axis in range(3):
        for d in range(4):
            for half in range(2):
                lanes = slice(half * 128, half * 128 + 128)
                v = (INNER * 0.5) * row[axis : axis + 1, lanes] - d - (INNER * 0.5) * column[axis]
                squares[axis * 4 + d, :, lanes] = v * v + (SOFTEN if axis == 2 else 0.0)
    matrices[...] = jnp.zeros_like(matrices)
    total[...] = jnp.zeros_like(total)
    for key, members in far_groups().items():
        ranges = [range(4) if every else (0, 2) for every in key]
        leaves = [(x, y, z) for x in ranges[0] for y in ranges[1] for z in ranges[2]]
        for n, (a, b, c) in enumerate(members):
            m = lax.rsqrt(squares[a] + squares[4 + b] + squares[8 + c])
            matrices[n * WIDE : n * WIDE + SPAD, :] = m.astype(BF16)
            flag = chosen[(a * 16 + b * 4 + c) * 8 : (a * 16 + b * 4 + c) * 8 + 8, :]
            for i in range(0, len(leaves), 2):
                tiles = []
                for x, y, z in leaves[i : i + 2]:
                    at = (((x + 2 + a) * 8 + y + 2 + b) * 8 + z + 2 + c) * 8
                    leaf = x * 16 + y * 4 + z
                    keep = jnp.broadcast_to(flag[:, leaf : leaf + 1], (8, 128))
                    tiles.append([framed[half, at : at + 8, :] * keep for half in range(2)])
                for half in range(2):
                    lanes = slice(n * WIDE + half * 128, n * WIDE + half * 128 + 128)
                    stacked[i * 8 : i * 8 + 16, lanes] = jnp.concatenate([t[half] for t in tiles], axis=0).astype(BF16)
        rows, depth = len(leaves) * 8, len(members) * WIDE
        product = jnp.dot(stacked[0:rows, 0:depth], matrices[0:depth, :], preferred_element_type=F32)
        for i, (x, y, z) in enumerate(leaves):
            leaf = x * 16 + y * 4 + z
            for half in range(2):
                total[half, leaf * 8 : leaf * 8 + 8, :] += product[i * 8 : i * 8 + 8, half * 128 : half * 128 + 128]
    result = jnp.zeros((64, WIDE), F32)
    for h in range(8):
        parts = [total.at[half][pl.ds(h, 64, stride=8), :] for half in range(2)]
        hi, lo = split2(jnp.concatenate(parts, axis=1))
        both = jnp.dot(jnp.concatenate([hi, lo], axis=0), permutation(h), preferred_element_type=F32).astype(BF16)
        mask = (48 if h & 4 else 0) + (12 if h & 2 else 0) + (3 if h & 1 else 0)
        turn = ((iota((64, 128), 0) ^ mask) == (iota((64, 128), 1) & 63)).astype(F32).astype(BF16)
        result = result + jnp.dot(turn, both, preferred_element_type=F32)
    out[...] = result


def near_kernel(planes, first_x, count_x, *refs):
    *halo, flags, out, lines, sources, points, shifted, sums = refs
    refs = (halo[0:4], *halo[4:])
    if len(halo) == 6:
        refs = (*refs, None, None)
    z1, z2 = halo[1], halo[2]
    targets = [(x, y) for x in planes for y in range(4)]
    count = count_x * 6
    for x in range(count_x):
        for y in range(6):
            for pair in range(4):
                record = particle_record(refs, x + first_x, y - 1, pair)
                for c in range(4):
                    lines[c, x * 6 + y : x * 6 + y + 1, pair * 128 : pair * 128 + 128] = record[c : c + 1]
    for c in range(4):
        whole = lines[c]
        half_turn = pltpu.roll(whole, 64, 1)
        for e, (line, at) in enumerate(((half_turn, 128), (whole, 128), (half_turn, 256))):
            if c == 2:
                line = line + float(e - 1)
            for half in range(2):
                lanes = slice(at + half * 128, at + half * 128 + 128)
                sources.at[c, half][pl.ds(e, count, stride=3), :] = line[0:count, lanes]
    same = (iota((64, WIDE), 1) & 63) == iota((64, WIDE), 0)
    block = ((iota((WIDE, WIDE), 0) >> 6) == (iota((WIDE, WIDE), 1) >> 6)).astype(F32).astype(BF16)
    zone = iota((32, WIDE), 1) >> 6
    step_y = (iota((9, WIDE), 0) // 3 - 1).astype(F32)
    for i, (x, y) in enumerate(targets):
        r = x * 4 + y
        pieces = []
        for c in range(3):
            v = jnp.concatenate([z1[16 + r, c : c + 1, :], z2[16 + r, c : c + 1, :]], axis=1)
            for _ in range(3):
                b = v.astype(BF16).astype(F32)
                pieces.append(jnp.where(same, b, 0.0).astype(BF16))
                v = v - b
        spread = jnp.dot(jnp.concatenate(pieces, axis=0), block, preferred_element_type=F32)
        square = jnp.full((64, WIDE), SOFTEN, F32)
        for c in range(3):
            at = c * 192
            v = spread[at : at + 64] + spread[at + 64 : at + 128] + spread[at + 128 : at + 192]
            square = square + v * v
            points[i, c] = -2.0 * v
        points[i, 3] = square
        f = flags[x, y]
        lists = jnp.zeros((32, WIDE), F32)
        for z in range(4):
            lists = jnp.where(zone == z, f[:, z : z + 1], lists)
        for ex in range(3):
            at = ((x - 1 + ex - first_x) * 6 + y) * 3
            here = slice(ex * 9, ex * 9 + 9)
            sx, sy, sz, q = (
                jnp.concatenate([sources[c, half, at : at + 9, :] for half in range(2)], axis=1) for c in range(4)
            )
            sx = sx + float(ex - 1)
            sy = sy + step_y
            shifted[i, 0, here, :] = sx
            shifted[i, 1, here, :] = sy
            shifted[i, 2, here, :] = sz
            shifted[i, 3, here, :] = sx * sx + sy * sy + sz * sz
            shifted[i, 4, here, :] = q * lists[here]

    def one_row(i, carry):
        for half in range(2):
            lanes = slice(half * 128, half * 128 + 128)
            tx, ty, tz, tt = (points[i, c, :, lanes] for c in range(4))
            acc = jnp.zeros((64, 128), F32)
            for n in range(27):
                sx, sy, sz, ss, q = (shifted[i, c, n : n + 1, lanes] for c in range(5))
                k = lax.rsqrt((tt + ss) + tx * sx + ty * sy + tz * sz)
                if n == 13:
                    k = jnp.where(same[:, lanes], 0.0, k)
                acc = acc + k * q
            sums[i, :, lanes] = acc
        return carry

    lax.fori_loop(0, len(targets), one_row, 0)
    for i in range(len(targets)):
        hi, lo = split2(sums[i])
        both = jnp.dot(jnp.concatenate([hi, lo], axis=0), block, preferred_element_type=F32)
        picked = jnp.where(same, both[0:64] + both[64:128], 0.0)
        out[i : i + 1, :] = jnp.sum(picked, axis=0, keepdims=True)


def last_kernel(
    counts, gathered, far, near_in, near_out, pos, down, column, row, tail, nodes,
    out, operator, squares, offsets, tails, acc, checks, ends,
):
    padded_operator(down, operator)
    flipped = operator[...].T
    segment = iota((1, 128), 1) >> 5
    at = 0
    for axis, ring in enumerate((RING8, RING4, RING8)):
        outer = (INNER * HALF) * column[axis]
        base = outer - (INNER * HALF) * row[axis : axis + 1, 0:128]
        end = outer - (INNER * HALF) * tail[axis : axis + 1, :]
        soft = SOFTEN if axis == 2 else 0.0
        for i, delta in enumerate(ring):
            v = base - float(delta * 4)
            offsets[at + i] = v * v + soft
            if axis < 2:
                v = end - float(delta * 4)
                tails[at + i] = v * v
            elif i % 4 == 0:
                d = ring[i : i + 4]
                shift = jnp.where(
                    segment < 2, jnp.where(segment == 0, d[0], d[1]), jnp.where(segment == 2, d[2], d[3])
                ).astype(F32)
                v = end - 4.0 * shift
                tails[at + i // 4] = v * v + soft
        at += len(ring)
    acc[...] = jnp.zeros_like(acc)

    def pair(i, carry):
        x, y = i >> 2, i & 3
        lines, ends = [], [jnp.zeros((1, 128), F32)] * 2
        for z in range(8):
            m = i * 8 + z
            both = gathered[m] * jnp.where(m == SELF, 0.0, 1.0)
            lines.append(both[0:1])
            end = both[1:2]
            ends[z // 4] = ends[z // 4] + (pltpu.roll(end, 32 * (z % 4), 1) if z % 4 else end)
        for part in range(4):
            rows = slice(part * 40, part * 40 + 40)
            xy = offsets[x, rows, :] + offsets[8 + y, rows, :]
            total = acc[rows, 0:128]
            for z in range(8):
                total = total + lax.rsqrt(xy + offsets[12 + z, rows, :]) * lines[z]
            acc[rows, 0:128] = total
            xy = tails[x, rows, :] + tails[8 + y, rows, :]
            total = acc[rows, 128:256]
            for z in range(2):
                total = total + lax.rsqrt(xy + tails[12 + z, rows, :]) * ends[z]
            acc[rows, 128:256] = total
        return carry

    lax.fori_loop(0, 32, pair, 0)
    weight = BREADTH * jnp.sum(acc[0:SPAD, 0:128] + acc[0:SPAD, 128:256], axis=1, keepdims=True)
    line = jnp.sum(flipped[0:SPAD] * weight, axis=0, keepdims=True)
    local = jnp.broadcast_to(line, (128, WIDE)).T
    leaf_squares(column, row, tail, squares)
    checks[...] = jnp.zeros_like(checks)
    for x in range(4):
        for y in range(4):
            lines = [jnp.zeros((8, 128), F32)] * 5
            for part in range(4):
                rows = slice(part * 40, part * 40 + 40)
                weight = local[rows, 0:128]
                for z in range(5):
                    lanes = slice(0, 128) if z < 4 else slice(128, 256)
                    if z % 4 == 0:
                        xy = squares[x, rows, lanes] + squares[4 + y, rows, lanes]
                    v = lax.rsqrt(xy + squares[8 + z % 4, rows, lanes]) * weight
                    for s in range(5):
                        lines[z] = lines[z] + v[s * 8 : s * 8 + 8]
            for z in range(4):
                t = x * 16 + y * 4 + z
                checks[0, t : t + 1, :] = jnp.sum(lines[z], axis=0, keepdims=True)
            r = x * 4 + y
            ends[r : r + 1, :] = jnp.sum(lines[4], axis=0, keepdims=True)
    used = iota((16, 128), 1) < SURF - 128
    for z in range(4):
        part = pltpu.roll(ends[...], 128 - 32 * z, 1) if z else ends[...]
        checks.at[1][pl.ds(z, 16, stride=4), :] = jnp.where(used, part, 0.0)
    both = jnp.concatenate([checks[0], checks[1]], axis=1)
    local = jnp.dot(both[0:64] + far[...], flipped, precision=HIGHEST, preferred_element_type=F32)
    local = jnp.concatenate([local, jnp.zeros((64, WIDE), F32)], axis=0).T
    hi, lo = split2(local[0:SPAD])
    both = jnp.concatenate([hi, lo], axis=0)
    for x in range(4):
        for y in range(4):
            r = x * 4 + y
            spread = (iota((128, WIDE), 0) == r * 4 + (iota((128, WIDE), 1) >> 6)).astype(F32).astype(BF16)
            wide = jnp.dot(both, spread, preferred_element_type=F32)
            px, py, pz = (pos[c, x, y : y + 1, :] for c in range(3))
            k = surface_terms(px, py, pz, nodes[...])
            line = jnp.sum(k * (wide[0:SPAD] + wide[SPAD : 2 * SPAD]), axis=0, keepdims=True)
            near, i = (near_in, r - 4) if x in (1, 2) else (near_out, r % 8)
            out[x, y : y + 1, :] = occupied_row(counts, x, y) * (line + near[i : i + 1, :])


def call(body, outs, scratch, memory, name, work, *args, vmem=40):
    spaces = {"v": pltpu.VMEM, "s": pltpu.SMEM}
    return pl.pallas_call(
        body,
        out_shape=[jax.ShapeDtypeStruct(s, F32) for s in outs],
        in_specs=[pl.BlockSpec(memory_space=spaces[m]) for m in memory],
        out_specs=[pl.BlockSpec(memory_space=pltpu.VMEM) for _ in outs],
        scratch_shapes=[pltpu.VMEM(s, d) for s, d in scratch],
        compiler_params=pltpu.CompilerParams(vmem_limit_bytes=vmem << 20),
        cost_estimate=pl.CostEstimate(flops=work * 1000000, transcendentals=0, bytes_accessed=1 << 20),
        name=name,
    )(*args)


def shifted(array, axis, distance):
    n = lax.axis_size(axis)
    return lax.ppermute(array, axis, [((i + distance) % n, i) for i in range(n)])


def body(positions, charges, counts, near_flags, far_flags, up_operator, down_operator):
    column, row, tail, nodes, mirror, pick = (jnp.asarray(t) for t in tables())
    below, above = call(
        upward_kernel,
        [(33, 4, 128), (33, 4, 128)],
        [
            ((2 * SPAD, 16 * WIDE), BF16), ((WIDE, WIDE), F32), ((12, SPAD, WIDE), F32),
            ((1, 64, 128), F32),
        ],
        "vvsvvvvv", "upward", 6000, positions, charges, counts, up_operator, column, row, tail, nodes, vmem=59,
    )
    own = (shifted(above, "gz", -1), below, above, shifted(below, "gz", 1))
    beyond = shifted(below[32:33], "gz", 2)

    grid = [[v[k * 16 : k * 16 + 16].reshape(4, 4, 4, 128) for v in own] for k in range(2)]
    blocks = [own[n][32:33] for n in (0, 1, 3)] + [beyond]

    def to_y(low, one):
        parts = [v[:, low : low + 2].reshape(8, 4, 128) for v in grid[0]]
        parts += [v[:, one].reshape(4, 4, 128) for v in grid[1]]
        return jnp.concatenate(parts + blocks, axis=0)

    middle = jnp.concatenate(blocks, axis=0)
    up, down, middle, far_flags, near_flags = lax.optimization_barrier(
        (to_y(2, 3), to_y(0, 0), middle, far_flags, near_flags)
    )
    ylo = shifted(up, "gy", -1)
    yhi = shifted(down, "gy", 1)
    far_blocks = shifted(middle, "gy", 2)
    blocks = jnp.concatenate([ylo[48:52], middle, yhi[48:52], far_blocks], axis=0)

    def to_x(low, one):
        parts = []
        for s in range(4):
            sides = [v[s * 8 : s * 8 + 8].reshape(4, 2, 4, 128)[low : low + 2] for v in (ylo, yhi)]
            parts.append(jnp.concatenate([sides[0], grid[0][s][low : low + 2], sides[1]], axis=1).reshape(16, 4, 128))
        for s in range(4):
            at = 32 + s * 4 + one
            parts += [ylo[at : at + 1], grid[1][s][one], yhi[at : at + 1]]
        return jnp.concatenate(parts + [blocks], axis=0)

    up, down = lax.optimization_barrier((to_x(2, 3), to_x(0, 0)))
    xlo = shifted(up, "gx", -1)
    xhi = shifted(down, "gx", 1)
    halo = (*own, ylo, yhi, xlo, xhi)

    held = jnp.concatenate([xlo[88:104], blocks, xhi[88:104]], axis=0)[:, 0:2]
    held = jnp.concatenate([held, shifted(held, "gx", 3), shifted(held[16:48], "gx", -3)], axis=0)
    held = held.reshape(8, 4, 4, 2, 128)
    gathered = jnp.concatenate([held, shifted(held, "gz", 4)], axis=2).reshape(256, 2, 128)

    flags = jnp.pad(far_flags.reshape(CLASSES, 64).astype(BF16), ((0, 384 - CLASSES), (0, 64)))
    (far,) = call(
        far_kernel,
        [(64, WIDE)],
        [
            ((2, 512, 128), F32),
            ((512, WIDE), BF16), ((512, WIDE), BF16), ((2, 4096, 128), F32), ((512, 128), F32),
            ((12, SPAD, WIDE), F32), ((512, 8 * WIDE), BF16), ((8 * WIDE, WIDE), BF16), ((2, 512, 128), F32),
        ],
        "v" * 13, "far", 7000, *halo, flags, pick, mirror, column, row,
    )
    near_flags = near_flags.astype(F32)
    centre = jnp.ones((1, *near_flags.shape[1:]), F32)
    listed = jnp.concatenate([near_flags[0:13], centre, near_flags[13:26], jnp.zeros((5, *near_flags.shape[1:]), F32)], axis=0)
    listed = listed.transpose(1, 2, 0, 3)

    def near(planes, first_x, count_x, halo):
        count, here = count_x * 6, len(planes) * 4
        (result,) = call(
            functools.partial(near_kernel, planes, first_x, count_x),
            [(here, WIDE)],
            [
                ((4, count + -count % 8, 512), F32), ((4, 2, count * 3, 128), F32), ((here, 4, 64, WIDE), F32),
                ((here, 5, 32, WIDE), F32), ((here, 64, WIDE), F32),
            ],
            "v" * (len(halo) + 1), "near", 6000, *halo, listed,
        )
        return result

    inner, outer = near((1, 2), 0, 4, halo[0:6]), near((0, 3), -1, 6, halo)
    (potential,) = call(
        last_kernel,
        [(4, 4, WIDE)],
        [
            ((WIDE, WIDE), F32), ((12, SPAD, WIDE), F32), ((20, SPAD, 128), F32), ((14, SPAD, 128), F32),
            ((WIDE, WIDE), F32), ((2, 128, 128), F32), ((16, 128), F32),
        ],
        "svvvvvvvvvv", "last", 9000, counts, gathered, far, inner, outer, positions, down_operator, column, row, tail, nodes,
    )
    return potential


def solution(mesh):
    return jax.shard_map(
        body,
        mesh=mesh,
        in_specs=(
            P(None, "gx", "gy", "gz"),
            P("gx", "gy", "gz"),
            P("gx", "gy", "gz"),
            P(None, "gx", "gy", "gz"),
            P(None, "gx", "gy", "gz"),
            P(),
            P(),
        ),
        out_specs=P("gx", "gy", "gz"),
        check_vma=False,
    )
```

```python
import functools

import jax
import jax.numpy as jnp
import ml_dtypes
import numpy as np
from jax import lax
from jax.experimental import pallas as pl
from jax.experimental.pallas import tpu as pltpu
from jax.sharding import PartitionSpec as P

ORDER = 6
SURF = 152
SPAD = 160
WIDE = 256
LEAVES = 4
SLOTS = 64
CLASSES = 343
INNER = 1.05
OUTER = 2.95
SOFTEN = 0.01
HALF = 2.0
BREADTH = 4.0
HIGHEST = lax.Precision.HIGHEST
F32 = jnp.float32
BF16 = jnp.bfloat16
RING8 = (-1, 0, 1, 2, 3, -4, -3, -2)
RING4 = (-1, 0, 1, -2)
SELF = (1 * 4 + 1) * 8 + 1


def surface_points():
    points = []
    for i in range(ORDER):
        for j in range(ORDER):
            for k in range(ORDER):
                if min(i, j, k) == 0 or max(i, j, k) == ORDER - 1:
                    points.append((i, j, k))
    return points


def tables():
    points = surface_points()
    spacing = np.linspace(-1.0, 1.0, ORDER)
    g = np.array([[spacing[i] for i in p] for p in points], dtype=np.float32)
    column = np.zeros((3, SPAD, 128), np.float32)
    column[:, :SURF, :] = g.T[:, :, None]
    row = np.zeros((8, WIDE), np.float32)
    row[:3, :SURF] = g.T
    tail = np.tile(row[:, 128:160], (1, 4))
    nodes = np.zeros((SPAD, 128), np.float32)
    for n, p in enumerate(points + [points[0]] * (SPAD - SURF)):
        for part in range(3):
            for axis in range(3):
                nodes[n, part * 24 + axis * 8 + p[axis]] = 1.0
    where = {p: n for n, p in enumerate(points)}
    mirror = np.full((8, WIDE), -1, np.int32)
    for h in range(8):
        sign = (h >> 2 & 1, h >> 1 & 1, h & 1)
        for n, p in enumerate(points):
            mirror[h, n] = where[tuple(ORDER - 1 - c if f else c for c, f in zip(p, sign))]
    pick = np.zeros((64 * 8, 384), np.float32)
    for a in range(4):
        for b in range(4):
            for c in range(4):
                if max(a, b, c) < 2:
                    continue
                for h in range(8):
                    d = [-v if f else v for v, f in zip((a, b, c), (h >> 2 & 1, h >> 1 & 1, h & 1))]
                    number = (d[0] + 3) * 49 + (d[1] + 3) * 7 + d[2] + 3
                    pick[(a * 16 + b * 4 + c) * 8 + h, number] = 1.0
    return column, row, tail, nodes.astype(ml_dtypes.bfloat16), mirror, pick.astype(ml_dtypes.bfloat16)


def iota(shape, dim):
    return lax.broadcasted_iota(jnp.int32, shape, dim)


def split2(v):
    hi = v.astype(BF16)
    return hi, (v - hi.astype(F32)).astype(BF16)


def surface_terms(px, py, pz, nodes):
    step = iota((8, WIDE), 0).astype(F32) * (OUTER / (ORDER - 1)) - OUTER * 0.5
    parts = []
    for n, p in enumerate((px, py, pz)):
        d = step - p
        parts.append(d * d + (SOFTEN if n == 2 else 0.0))
    rest = jnp.concatenate(parts, axis=0)
    parts = []
    for _ in range(3):
        b = rest.astype(BF16).astype(F32)
        parts.append(b)
        rest = rest - b
    parts.append(jnp.zeros((128 - 72, WIDE), F32))
    squares = jnp.concatenate(parts, axis=0).astype(BF16)
    return lax.rsqrt(jnp.dot(nodes, squares, preferred_element_type=F32))


def occupied_row(counts, x, y):
    lane = iota((1, WIDE), 1)
    zone = lane >> 6
    n = jnp.where(
        zone < 2,
        jnp.where(zone == 0, counts[x, y, 0], counts[x, y, 1]),
        jnp.where(zone == 2, counts[x, y, 2], counts[x, y, 3]),
    )
    return ((lane & 63) < n).astype(F32)


def padded_operator(ref, out):
    out[...] = jnp.zeros_like(out)
    out[0:SURF, 0:SURF] = ref[...]


def leaf_squares(column, row, tail, squares):
    segment = (iota((1, 128), 1) >> 5).astype(F32)
    for axis in range(3):
        outer = (OUTER * HALF) * column[axis]
        inner = (INNER * 0.5) * row[axis : axis + 1, 0:128]
        last = (INNER * 0.5) * tail[axis : axis + 1, :]
        soft = SOFTEN if axis == 2 else 0.0
        for t in range(LEAVES):
            d = outer - ((t - 1.5) + inner)
            squares[axis * LEAVES + t, :, 0:128] = d * d + soft
            if axis < 2:
                d = outer - ((t - 1.5) + last)
                squares[axis * LEAVES + t, :, 128:256] = d * d
            elif t == 0:
                d = outer - ((segment - 1.5) + last)
                squares[axis * LEAVES, :, 128:256] = d * d + soft


def upward_kernel(
    pos, chg, counts, up, column, row, tail, nodes,
    below, above,
    terms, operator, squares, leaves,
):
    padded_operator(up, operator)
    flipped = operator[...].T
    leaf_squares(column, row, tail, squares)
    for x in range(4):
        for y in range(4):
            r = x * 4 + y
            q = chg[x, y : y + 1, :] * occupied_row(counts, x, y)
            px, py, pz = (pos[c, x, y : y + 1, :] for c in range(3))
            k = surface_terms(px, py, pz, nodes[...]) * q
            hi, lo = split2(k)
            terms[0:SPAD, r * WIDE : (r + 1) * WIDE] = hi
            terms[SPAD : 2 * SPAD, r * WIDE : (r + 1) * WIDE] = lo
            for c, v in enumerate((px, py, pz, q)):
                below[16 + r, c : c + 1, :] = v[:, 0:128]
                above[16 + r, c : c + 1, :] = v[:, 128:256]
    gather = ((iota((16 * WIDE, 128), 0) >> 6) == iota((16 * WIDE, 128), 1)).astype(F32).astype(BF16)
    both = jnp.dot(terms[...], gather, preferred_element_type=F32)
    check = both[0:SPAD] + both[SPAD : 2 * SPAD]
    check = jnp.concatenate([check, jnp.zeros((WIDE - SPAD, 128), F32)], axis=0).T[0:64, :]
    up_eq = jnp.dot(check, flipped, precision=HIGHEST, preferred_element_type=F32)
    low = up_eq.astype(BF16).astype(F32)
    for r in range(16):
        for out, at in ((below, 0), (above, 2)):
            pair = low[r * 4 + at : r * 4 + at + 2]
            out[r, 0:2, :] = pair[:, 0:128]
            out[r, 2:4, :] = pair[:, 128:256]
    leaves[0] = up_eq[:, 128:256]
    lines = leaves.at[0][pl.ds(0, 16, stride=4), :]
    for z in range(1, 4):
        lines = lines + pltpu.roll(leaves.at[0][pl.ds(z, 16, stride=4), :], 32 * z, 1)
    block = jnp.zeros((8, WIDE), F32)
    for part in range(4):
        rows = slice(part * 40, part * 40 + 40)
        first, last = jnp.zeros((40, 128), F32), jnp.zeros((40, 128), F32)
        for x in range(4):
            for y in range(4):
                xy = squares[x, rows, 0:128] + squares[4 + y, rows, 0:128]
                for z in range(4):
                    t = x * 16 + y * 4 + z
                    first = first + lax.rsqrt(xy + squares[8 + z, rows, 0:128]) * up_eq[t : t + 1, 0:128]
                xy = squares[x, rows, 128:256] + squares[4 + y, rows, 128:256]
                r = x * 4 + y
                last = last + lax.rsqrt(xy + squares[8, rows, 128:256]) * lines[r : r + 1, :]
        weight = BREADTH * jnp.sum(first + last, axis=1, keepdims=True)
        for n in range(part * 40, part * 40 + 40, 8):
            block = block + flipped[n : n + 8] * weight[n - part * 40 : n - part * 40 + 8]
    block = jnp.sum(block, axis=0, keepdims=True)
    for out in (below, above):
        out[32, 0:1, :] = block[0:1, 0:128]
        out[32, 1:2, :] = block[0:1, 128:256]
        out[32, 2:4, :] = jnp.zeros((2, 128), F32)


def eq_record(refs, x, y, s):
    own, ylo, yhi, xlo, xhi = refs
    if x < 2:
        return xlo[(s * 2 + x) * 8 + y]
    if x > 5:
        return xhi[(s * 2 + x - 6) * 8 + y]
    if y < 2:
        return ylo[s * 8 + (x - 2) * 2 + y]
    if y > 5:
        return yhi[s * 8 + (x - 2) * 2 + y - 6]
    return own[s][(x - 2) * 4 + y - 2]


def particle_record(refs, x, y, s):
    own, ylo, yhi, xlo, xhi = refs
    if x < 0:
        return xlo[64 + s * 6 + y + 1]
    if x > 3:
        return xhi[64 + s * 6 + y + 1]
    if y < 0:
        return ylo[32 + s * 4 + x]
    if y > 3:
        return yhi[32 + s * 4 + x]
    return own[s][16 + x * 4 + y]


def far_groups():
    groups = {}
    for a in range(4):
        for b in range(4):
            for c in range(4):
                if max(a, b, c) >= 2:
                    key = tuple(v in (1, 2) for v in (a, b, c))
                    groups.setdefault(key, []).append((a, b, c))
    return groups


def far_kernel(
    z0, z1, z2, z3, ylo, yhi, xlo, xhi, flags, pick, mirror, column, row,
    out, halo, low, turned, framed, chosen, squares, stacked, matrices, total,
):
    refs = ((z0, z1, z2, z3), ylo, yhi, xlo, xhi)
    for x in range(8):
        for y in range(8):
            for pair in range(4):
                record = eq_record(refs, x, y, pair)
                at = (x * 8 + y) * 8 + pair * 2
                halo[0, at : at + 2, :] = record[0:2]
                halo[1, at : at + 2, :] = record[2:4]
    for half in range(2):
        low[:, half * 128 : half * 128 + 128] = halo[half].astype(BF16)
    turn = ((iota((WIDE, WIDE), 0) ^ 7) == iota((WIDE, WIDE), 1)).astype(F32).astype(BF16)
    for n in range(2):
        part = slice(n * WIDE, n * WIDE + WIDE)
        turned[part, :] = jnp.dot(turn, low[part, :], preferred_element_type=F32).astype(BF16)

    def permutation(h):
        return (iota((WIDE, WIDE), 0) == mirror[h : h + 1, :]).astype(F32).astype(BF16)

    for h in range(8):
        source = turned if h & 1 else low
        frame = jnp.dot(source[...], permutation(h), preferred_element_type=F32)
        for x in range(8):
            for y in range(8):
                xf, yf = (7 - x if h & 4 else x), (7 - y if h & 2 else y)
                at = (x * 8 + y) * 8
                for n in range(2):
                    framed.at[n][pl.ds((xf * 8 + yf) * 64 + h, 8, stride=8), :] = frame[
                        at : at + 8, n * 128 : n * 128 + 128
                    ]
    picked = jnp.dot(pick[...], flags[...], preferred_element_type=F32)
    which = iota((512, 128), 0) & 7
    for h in range(8):
        mask = (48 if h & 4 else 0) + (12 if h & 2 else 0) + (3 if h & 1 else 0)
        turn = ((iota((128, 128), 0) ^ mask) == iota((128, 128), 1)).astype(F32).astype(BF16)
        part = jnp.dot(jnp.where(which == h, picked, 0.0).astype(BF16), turn, preferred_element_type=F32)
        chosen[...] = part if h == 0 else chosen[...] + part
    for axis in range(3):
        for d in range(4):
            for half in range(2):
                lanes = slice(half * 128, half * 128 + 128)
                v = (INNER * 0.5) * row[axis : axis + 1, lanes] - d - (INNER * 0.5) * column[axis]
                squares[axis * 4 + d, :, lanes] = v * v + (SOFTEN if axis == 2 else 0.0)
    matrices[...] = jnp.zeros_like(matrices)
    total[...] = jnp.zeros_like(total)
    for key, members in far_groups().items():
        ranges = [range(4) if every else (0, 2) for every in key]
        leaves = [(x, y, z) for x in ranges[0] for y in ranges[1] for z in ranges[2]]
        for n, (a, b, c) in enumerate(members):
            m = lax.rsqrt(squares[a] + squares[4 + b] + squares[8 + c])
            matrices[n * WIDE : n * WIDE + SPAD, :] = m.astype(BF16)
            flag = chosen[(a * 16 + b * 4 + c) * 8 : (a * 16 + b * 4 + c) * 8 + 8, :]
            for i in range(0, len(leaves), 2):
                tiles = []
                for x, y, z in leaves[i : i + 2]:
                    at = (((x + 2 + a) * 8 + y + 2 + b) * 8 + z + 2 + c) * 8
                    leaf = x * 16 + y * 4 + z
                    keep = jnp.broadcast_to(flag[:, leaf : leaf + 1], (8, 128))
                    tiles.append([framed[half, at : at + 8, :] * keep for half in range(2)])
                for half in range(2):
                    lanes = slice(n * WIDE + half * 128, n * WIDE + half * 128 + 128)
                    stacked[i * 8 : i * 8 + 16, lanes] = jnp.concatenate([t[half] for t in tiles], axis=0).astype(BF16)
        rows, depth = len(leaves) * 8, len(members) * WIDE
        product = jnp.dot(stacked[0:rows, 0:depth], matrices[0:depth, :], preferred_element_type=F32)
        for i, (x, y, z) in enumerate(leaves):
            leaf = x * 16 + y * 4 + z
            for half in range(2):
                total[half, leaf * 8 : leaf * 8 + 8, :] += product[i * 8 : i * 8 + 8, half * 128 : half * 128 + 128]
    result = jnp.zeros((64, WIDE), F32)
    for h in range(8):
        parts = [total.at[half][pl.ds(h, 64, stride=8), :] for half in range(2)]
        hi, lo = split2(jnp.concatenate(parts, axis=1))
        both = jnp.dot(jnp.concatenate([hi, lo], axis=0), permutation(h), preferred_element_type=F32).astype(BF16)
        mask = (48 if h & 4 else 0) + (12 if h & 2 else 0) + (3 if h & 1 else 0)
        turn = ((iota((64, 128), 0) ^ mask) == (iota((64, 128), 1) & 63)).astype(F32).astype(BF16)
        result = result + jnp.dot(turn, both, preferred_element_type=F32)
    out[...] = result


def near_kernel(planes, first_x, count_x, *refs):
    *halo, flags, out, lines, sources, points, shifted, sums = refs
    refs = (halo[0:4], *halo[4:])
    if len(halo) == 6:
        refs = (*refs, None, None)
    z1, z2 = halo[1], halo[2]
    targets = [(x, y) for x in planes for y in range(4)]
    count = count_x * 6
    for x in range(count_x):
        for y in range(6):
            for pair in range(4):
                record = particle_record(refs, x + first_x, y - 1, pair)
                for c in range(4):
                    lines[c, x * 6 + y : x * 6 + y + 1, pair * 128 : pair * 128 + 128] = record[c : c + 1]
    for c in range(4):
        whole = lines[c]
        half_turn = pltpu.roll(whole, 64, 1)
        for e, (line, at) in enumerate(((half_turn, 128), (whole, 128), (half_turn, 256))):
            if c == 2:
                line = line + float(e - 1)
            for half in range(2):
                lanes = slice(at + half * 128, at + half * 128 + 128)
                sources.at[c, half][pl.ds(e, count, stride=3), :] = line[0:count, lanes]
    same = (iota((64, WIDE), 1) & 63) == iota((64, WIDE), 0)
    block = ((iota((WIDE, WIDE), 0) >> 6) == (iota((WIDE, WIDE), 1) >> 6)).astype(F32).astype(BF16)
    zone = iota((32, WIDE), 1) >> 6
    step_y = (iota((9, WIDE), 0) // 3 - 1).astype(F32)
    for i, (x, y) in enumerate(targets):
        r = x * 4 + y
        pieces = []
        for c in range(3):
            v = jnp.concatenate([z1[16 + r, c : c + 1, :], z2[16 + r, c : c + 1, :]], axis=1)
            for _ in range(3):
                b = v.astype(BF16).astype(F32)
                pieces.append(jnp.where(same, b, 0.0).astype(BF16))
                v = v - b
        spread = jnp.dot(jnp.concatenate(pieces, axis=0), block, preferred_element_type=F32)
        square = jnp.full((64, WIDE), SOFTEN, F32)
        for c in range(3):
            at = c * 192
            v = spread[at : at + 64] + spread[at + 64 : at + 128] + spread[at + 128 : at + 192]
            square = square + v * v
            points[i, c] = -2.0 * v
        points[i, 3] = square
        f = flags[x, y]
        lists = jnp.zeros((32, WIDE), F32)
        for z in range(4):
            lists = jnp.where(zone == z, f[:, z : z + 1], lists)
        for ex in range(3):
            at = ((x - 1 + ex - first_x) * 6 + y) * 3
            here = slice(ex * 9, ex * 9 + 9)
            sx, sy, sz, q = (
                jnp.concatenate([sources[c, half, at : at + 9, :] for half in range(2)], axis=1) for c in range(4)
            )
            sx = sx + float(ex - 1)
            sy = sy + step_y
            shifted[i, 0, here, :] = sx
            shifted[i, 1, here, :] = sy
            shifted[i, 2, here, :] = sz
            shifted[i, 3, here, :] = sx * sx + sy * sy + sz * sz
            shifted[i, 4, here, :] = q * lists[here]

    def one_row(i, carry):
        for half in range(2):
            lanes = slice(half * 128, half * 128 + 128)
            tx, ty, tz, tt = (points[i, c, :, lanes] for c in range(4))
            acc = jnp.zeros((64, 128), F32)
            for n in range(27):
                sx, sy, sz, ss, q = (shifted[i, c, n : n + 1, lanes] for c in range(5))
                k = lax.rsqrt((tt + ss) + tx * sx + ty * sy + tz * sz)
                if n == 13:
                    k = jnp.where(same[:, lanes], 0.0, k)
                acc = acc + k * q
            sums[i, :, lanes] = acc
        return carry

    lax.fori_loop(0, len(targets), one_row, 0)
    for i in range(len(targets)):
        hi, lo = split2(sums[i])
        both = jnp.dot(jnp.concatenate([hi, lo], axis=0), block, preferred_element_type=F32)
        picked = jnp.where(same, both[0:64] + both[64:128], 0.0)
        out[i : i + 1, :] = jnp.sum(picked, axis=0, keepdims=True)


def last_kernel(
    counts, gathered, far, near_in, near_out, pos, down, column, row, tail, nodes,
    out, operator, squares, offsets, tails, acc, checks, ends,
):
    padded_operator(down, operator)
    flipped = operator[...].T
    segment = iota((1, 128), 1) >> 5
    at = 0
    for axis, ring in enumerate((RING8, RING4, RING8)):
        outer = (INNER * HALF) * column[axis]
        base = outer - (INNER * HALF) * row[axis : axis + 1, 0:128]
        end = outer - (INNER * HALF) * tail[axis : axis + 1, :]
        soft = SOFTEN if axis == 2 else 0.0
        for i, delta in enumerate(ring):
            v = base - float(delta * 4)
            offsets[at + i] = v * v + soft
            if axis < 2:
                v = end - float(delta * 4)
                tails[at + i] = v * v
            elif i % 4 == 0:
                d = ring[i : i + 4]
                shift = jnp.where(
                    segment < 2, jnp.where(segment == 0, d[0], d[1]), jnp.where(segment == 2, d[2], d[3])
                ).astype(F32)
                v = end - 4.0 * shift
                tails[at + i // 4] = v * v + soft
        at += len(ring)
    acc[...] = jnp.zeros_like(acc)

    def pair(i, carry):
        x, y = i >> 2, i & 3
        lines, ends = [], [jnp.zeros((1, 128), F32)] * 2
        for z in range(8):
            m = i * 8 + z
            both = gathered[m] * jnp.where(m == SELF, 0.0, 1.0)
            lines.append(both[0:1])
            end = both[1:2]
            ends[z // 4] = ends[z // 4] + (pltpu.roll(end, 32 * (z % 4), 1) if z % 4 else end)
        for part in range(4):
            rows = slice(part * 40, part * 40 + 40)
            xy = offsets[x, rows, :] + offsets[8 + y, rows, :]
            total = acc[rows, 0:128]
            for z in range(8):
                total = total + lax.rsqrt(xy + offsets[12 + z, rows, :]) * lines[z]
            acc[rows, 0:128] = total
            xy = tails[x, rows, :] + tails[8 + y, rows, :]
            total = acc[rows, 128:256]
            for z in range(2):
                total = total + lax.rsqrt(xy + tails[12 + z, rows, :]) * ends[z]
            acc[rows, 128:256] = total
        return carry

    lax.fori_loop(0, 32, pair, 0)
    weight = BREADTH * jnp.sum(acc[0:SPAD, 0:128] + acc[0:SPAD, 128:256], axis=1, keepdims=True)
    line = jnp.sum(flipped[0:SPAD] * weight, axis=0, keepdims=True)
    local = jnp.broadcast_to(line, (128, WIDE)).T
    leaf_squares(column, row, tail, squares)
    checks[...] = jnp.zeros_like(checks)
    for x in range(4):
        for y in range(4):
            lines = [jnp.zeros((8, 128), F32)] * 5
            for part in range(4):
                rows = slice(part * 40, part * 40 + 40)
                weight = local[rows, 0:128]
                for z in range(5):
                    lanes = slice(0, 128) if z < 4 else slice(128, 256)
                    if z % 4 == 0:
                        xy = squares[x, rows, lanes] + squares[4 + y, rows, lanes]
                    v = lax.rsqrt(xy + squares[8 + z % 4, rows, lanes]) * weight
                    for s in range(5):
                        lines[z] = lines[z] + v[s * 8 : s * 8 + 8]
            for z in range(4):
                t = x * 16 + y * 4 + z
                checks[0, t : t + 1, :] = jnp.sum(lines[z], axis=0, keepdims=True)
            r = x * 4 + y
            ends[r : r + 1, :] = jnp.sum(lines[4], axis=0, keepdims=True)
    used = iota((16, 128), 1) < SURF - 128
    for z in range(4):
        part = pltpu.roll(ends[...], 128 - 32 * z, 1) if z else ends[...]
        checks.at[1][pl.ds(z, 16, stride=4), :] = jnp.where(used, part, 0.0)
    both = jnp.concatenate([checks[0], checks[1]], axis=1)
    local = jnp.dot(both[0:64] + far[...], flipped, precision=HIGHEST, preferred_element_type=F32)
    local = jnp.concatenate([local, jnp.zeros((64, WIDE), F32)], axis=0).T
    hi, lo = split2(local[0:SPAD])
    both = jnp.concatenate([hi, lo], axis=0)
    for x in range(4):
        for y in range(4):
            r = x * 4 + y
            spread = (iota((128, WIDE), 0) == r * 4 + (iota((128, WIDE), 1) >> 6)).astype(F32).astype(BF16)
            wide = jnp.dot(both, spread, preferred_element_type=F32)
            px, py, pz = (pos[c, x, y : y + 1, :] for c in range(3))
            k = surface_terms(px, py, pz, nodes[...])
            line = jnp.sum(k * (wide[0:SPAD] + wide[SPAD : 2 * SPAD]), axis=0, keepdims=True)
            near, i = (near_in, r - 4) if x in (1, 2) else (near_out, r % 8)
            out[x, y : y + 1, :] = occupied_row(counts, x, y) * (line + near[i : i + 1, :])


def call(body, outs, scratch, memory, name, work, *args, vmem=40):
    spaces = {"v": pltpu.VMEM, "s": pltpu.SMEM}
    return pl.pallas_call(
        body,
        out_shape=[jax.ShapeDtypeStruct(s, F32) for s in outs],
        in_specs=[pl.BlockSpec(memory_space=spaces[m]) for m in memory],
        out_specs=[pl.BlockSpec(memory_space=pltpu.VMEM) for _ in outs],
        scratch_shapes=[pltpu.VMEM(s, d) for s, d in scratch],
        compiler_params=pltpu.CompilerParams(vmem_limit_bytes=vmem << 20),
        cost_estimate=pl.CostEstimate(flops=work * 1000000, transcendentals=0, bytes_accessed=1 << 20),
        name=name,
    )(*args)


def shifted(array, axis, distance):
    n = lax.axis_size(axis)
    return lax.ppermute(array, axis, [((i + distance) % n, i) for i in range(n)])


def body(positions, charges, counts, near_flags, far_flags, up_operator, down_operator):
    column, row, tail, nodes, mirror, pick = (jnp.asarray(t) for t in tables())
    below, above = call(
        upward_kernel,
        [(33, 4, 128), (33, 4, 128)],
        [
            ((2 * SPAD, 16 * WIDE), BF16), ((WIDE, WIDE), F32), ((12, SPAD, WIDE), F32),
            ((1, 64, 128), F32),
        ],
        "vvsvvvvv", "upward", 6000, positions, charges, counts, up_operator, column, row, tail, nodes, vmem=59,
    )
    own = (shifted(above, "gz", -1), below, above, shifted(below, "gz", 1))
    beyond = shifted(below, "gz", 2)[32:33]

    grid = [[v[k * 16 : k * 16 + 16].reshape(4, 4, 4, 128) for v in own] for k in range(2)]
    blocks = [own[n][32:33] for n in (0, 1, 3)] + [beyond]

    def to_y(low, one):
        parts = [v[:, low : low + 2].reshape(8, 4, 128) for v in grid[0]]
        parts += [v[:, one].reshape(4, 4, 128) for v in grid[1]]
        return jnp.concatenate(parts + blocks, axis=0)

    middle = jnp.concatenate(blocks, axis=0)
    up, down, middle, far_flags, near_flags = lax.optimization_barrier(
        (to_y(2, 3), to_y(0, 0), middle, far_flags, near_flags)
    )
    ylo = shifted(up, "gy", -1)
    yhi = shifted(down, "gy", 1)
    far_blocks = shifted(middle, "gy", 2)
    blocks = jnp.concatenate([ylo[48:52], middle, yhi[48:52], far_blocks], axis=0)

    def to_x(low, one):
        parts = []
        for s in range(4):
            sides = [v[s * 8 : s * 8 + 8].reshape(4, 2, 4, 128)[low : low + 2] for v in (ylo, yhi)]
            parts.append(jnp.concatenate([sides[0], grid[0][s][low : low + 2], sides[1]], axis=1).reshape(16, 4, 128))
        for s in range(4):
            at = 32 + s * 4 + one
            parts += [ylo[at : at + 1], grid[1][s][one], yhi[at : at + 1]]
        return jnp.concatenate(parts + [blocks], axis=0)

    up, down = lax.optimization_barrier((to_x(2, 3), to_x(0, 0)))
    xlo = shifted(up, "gx", -1)
    xhi = shifted(down, "gx", 1)
    halo = (*own, ylo, yhi, xlo, xhi)

    held = jnp.concatenate([xlo[88:104], blocks, xhi[88:104]], axis=0)[:, 0:2]
    held = jnp.concatenate([held, shifted(held, "gx", 3), shifted(held[16:48], "gx", -3)], axis=0)
    held = held.reshape(8, 4, 4, 2, 128)
    gathered = jnp.concatenate([held, shifted(held, "gz", 4)], axis=2).reshape(256, 2, 128)

    flags = jnp.pad(far_flags.reshape(CLASSES, 64).astype(BF16), ((0, 384 - CLASSES), (0, 64)))
    (far,) = call(
        far_kernel,
        [(64, WIDE)],
        [
            ((2, 512, 128), F32),
            ((512, WIDE), BF16), ((512, WIDE), BF16), ((2, 4096, 128), F32), ((512, 128), F32),
            ((12, SPAD, WIDE), F32), ((512, 8 * WIDE), BF16), ((8 * WIDE, WIDE), BF16), ((2, 512, 128), F32),
        ],
        "v" * 13, "far", 7000, *halo, flags, pick, mirror, column, row,
    )
    near_flags = near_flags.astype(F32)
    centre = jnp.ones((1, *near_flags.shape[1:]), F32)
    listed = jnp.concatenate([near_flags[0:13], centre, near_flags[13:26], jnp.zeros((5, *near_flags.shape[1:]), F32)], axis=0)
    listed = listed.transpose(1, 2, 0, 3)

    def near(planes, first_x, count_x, halo):
        count, here = count_x * 6, len(planes) * 4
        (result,) = call(
            functools.partial(near_kernel, planes, first_x, count_x),
            [(here, WIDE)],
            [
                ((4, count + -count % 8, 512), F32), ((4, 2, count * 3, 128), F32), ((here, 4, 64, WIDE), F32),
                ((here, 5, 32, WIDE), F32), ((here, 64, WIDE), F32),
            ],
            "v" * (len(halo) + 1), "near", 6000, *halo, listed,
        )
        return result

    inner, outer = near((1, 2), 0, 4, halo[0:6]), near((0, 3), -1, 6, halo)
    (potential,) = call(
        last_kernel,
        [(4, 4, WIDE)],
        [
            ((WIDE, WIDE), F32), ((12, SPAD, WIDE), F32), ((20, SPAD, 128), F32), ((14, SPAD, 128), F32),
            ((WIDE, WIDE), F32), ((2, 128, 128), F32), ((16, 128), F32),
        ],
        "svvvvvvvvvv", "last", 9000, counts, gathered, far, inner, outer, positions, down_operator, column, row, tail, nodes,
    )
    return potential


def solution(mesh):
    return jax.shard_map(
        body,
        mesh=mesh,
        in_specs=(
            P(None, "gx", "gy", "gz"),
            P("gx", "gy", "gz"),
            P("gx", "gy", "gz"),
            P(None, "gx", "gy", "gz"),
            P(None, "gx", "gy", "gz"),
            P(),
            P(),
        ),
        out_specs=P("gx", "gy", "gz"),
        check_vma=False,
    )
```
